32 devices in a mesh: groups: 2 (over y), seq: 4 (over z), dp: 4 (over x, core).
Axes of the slice: x: 2, y: 2, z: 4, core: 2. Of those that a mesh axis runs over, the one named last changes fastest.
Arguments:
- dna_features: bfloat16 [8, 1024, 384], P(('groups', 'dp'), 'seq'), parts along dimension 0, may hold values from -6 to 6
- filter_weight: bfloat16 [5, 384, 768], P(None, None, 'dp'), may hold values from -0.03125 to 0.03125
- filter_bias: float32 [768], replicated, may hold values from -0.75 to 0.75
- norm_gain: float32 [768], replicated, may hold values from 0.1 to 1.9
- attend_weight: bfloat16 [768, 1280], replicated, may hold values from -5.8456715 to 5.8456715
- output_weight: bfloat16 [768, 768], replicated, may hold values from -0.21875 to 0.21875
- cotangent: bfloat16 [8, 512, 768], P(('groups', 'dp'), 'seq'), parts along dimension 0, may hold values from -0.1875 to 0.1875
Outputs:
- outputs: float32 [8, 512, 768], P(('groups', 'dp'), 'seq'), parts along dimension 0
- grad_attend: float32 [1536, 1280], P(('groups', 'seq')), parts along dimension 0
- grad_output: float32 [1536, 768], P(('groups', 'seq')), parts along dimension 0
- grad_gain: float32 [1536], P(('groups', 'seq')), parts along dimension 0
The draws below stay inside these ranges and needn't reach their ends.
There are 2 independent parts, one for each index of `groups`. The reference program is written for one: setup_inputs(seed, part) draws one part's arguments, and reference() takes and returns one part's arrays. A program takes and returns all parts, laid end to end along the dimension named above; an argument that names none is the same for every part. Nothing has to cross between parts.
All inputs are finite; a program needn't handle non-finite values.
Results may differ from the reference program's by a relative error of at most 0.033.
Values may be sent and summed in bfloat16 or wider, within the bound.
No kernel may reach another device: no remote copies, remote signals or barrier semaphores. Data moves between devices by JAX's collectives and lax.ppermute only.
A program may use at most 64 MiB of HBM per device.

```python
import jax
import jax.numpy as jnp
from jax import lax

D = 768
CIN = 384
HEADS = 4
KEY_DIM = 64
VAL_DIM = 192
TOK_DEV = 128
LENGTH = 512
SEQS = 4
N_SEQ = 4
N_DP = 4


def draw_attend_weight(key, part):
    first = jax.random.fold_in(key, 0)
    query_width = HEADS * KEY_DIM
    base = jnp.clip(jax.random.normal(first, (D, 2 * query_width + HEADS * VAL_DIM), jnp.float32), -4.0, 4.0) * D ** (-0.5)
    return base.astype(jnp.bfloat16)


def with_spikes(array, stream_key, source, target, shards_of, factor):
    owner, partner = [(jnp.arange(array.shape[axis_at]) // (array.shape[axis_at] // shards_of)).reshape([-1 if axis == axis_at else 1 for axis in range(array.ndim)]) for axis_at in (source, target)]
    chosen = jax.random.permutation(stream_key, shards_of)[partner]
    strong = (owner == chosen) | (owner == (partner + shards_of // 2) % shards_of)
    return jnp.where(strong, factor * array, array)


def level_of(rng, extent, pieces, smallest, top_value):
    def one(position, parts):
        draws = jax.random.uniform(jax.random.fold_in(jax.random.fold_in(rng, 6), position), (parts,), jnp.float32, smallest / len(pieces), top_value / len(pieces))
        return jnp.repeat(jnp.exp(draws), extent[position] // parts).reshape((-1,) + (1,) * (len(extent) - position - 1))

    loudness = one(*pieces[0])
    for cut in pieces[1:]:
        loudness = loudness * one(*cut)
    return loudness


def gaussian(own_key, extent, scale, most, shards=(), held_as=jnp.bfloat16):
    entries = jax.random.normal(own_key, extent, jnp.float32) * scale
    if len(shards) > 0:
        entries = level_of(own_key, extent, shards, -0.22, 0.18) * entries
    return jnp.clip(entries, min=-most, max=most).astype(held_as)


def heavy_noise(key, extent, deviation, most, cuts, heavy, held_as=jnp.bfloat16):
    array = deviation * jax.random.normal(key, extent, jnp.float32)
    if cuts:
        array = array * level_of(key, extent, cuts, -0.22, 0.18)
    return jnp.clip(with_spikes(array, jax.random.fold_in(key, 3), *heavy), -most, most).astype(held_as)


def setup_inputs(seed: int = 0, part: int = 0) -> dict:
    arg_keys = jax.random.split(jax.random.key(seed), 8)
    part_splits = jax.random.split(jax.random.fold_in(arg_keys[7], part), 8)
    return {
        "dna_features": gaussian(part_splits[0], (SEQS, 2 * LENGTH, CIN), 1.0, 6.0, ((0, 4), (1, 4))),
        "filter_weight": gaussian(arg_keys[1], (5, CIN, D), (80 * CIN) ** -0.5, 0.03125, ((2, 4),)),
        "filter_bias": gaussian(arg_keys[2], (D,), 0.125, 0.75, (), jnp.float32),
        "norm_gain": jnp.clip(1.0 + 0.18 * jax.random.normal(arg_keys[3], (D,), jnp.float32), 0.1, 1.9),
        "attend_weight": draw_attend_weight(jax.random.fold_in(arg_keys[7], 71), part),
        "output_weight": gaussian(arg_keys[5], (D, HEADS * VAL_DIM), (HEADS * VAL_DIM) ** -0.5, 0.21875),
        "cotangent": heavy_noise(part_splits[6], (SEQS, LENGTH, D), ((TOK_DEV * N_SEQ * N_DP) ** -0.5), 0.1875, ((0, 4), (1, 4)), (1, 2, 4, 2.0)),
    }


def rounded(values):
    return lax.optimization_barrier(values.astype(jnp.bfloat16)).astype(jnp.float32)

def block_terms(left, right):
    left_blocks = left.astype(jnp.float32).reshape(N_SEQ, TOK_DEV, left.shape[1])
    right_blocks = right.astype(jnp.float32).reshape(N_SEQ, TOK_DEV, right.shape[1])
    terms = jnp.einsum('std,stc->sdc', left_blocks, right_blocks)
    return lax.optimization_barrier(jnp.sum(rounded(terms), axis=0))

def reference(dna_features, filter_weight, filter_bias, norm_gain, attend_weight, output_weight, cotangent):
    query_width = HEADS * KEY_DIM
    value_width = HEADS * VAL_DIM
    total_len = TOK_DEV * N_SEQ
    scale = KEY_DIM ** (-0.5)

    def one_sequence(pair):
        features, upstream = pair
        padded = jnp.pad(features, ((2, 2), (0, 0)))
        filtered = filter_bias
        for offset in range(5):
            filtered = filtered + jnp.dot(padded[offset:offset + 2 * total_len], filter_weight[offset], preferred_element_type=jnp.float32)
        activ = jax.nn.gelu(filtered, approximate=True)
        hidden = (0.5 * (activ[0::2] + activ[1::2])).astype(jnp.bfloat16)
        widen = hidden.astype(jnp.float32)
        nhat = widen * lax.rsqrt(lax.optimization_barrier(jnp.mean(widen * widen, axis=-1, keepdims=True)) + 1e-06)
        normed = (nhat * norm_gain).astype(jnp.bfloat16)
        projected = jnp.dot(normed, attend_weight, preferred_element_type=jnp.float32).astype(jnp.bfloat16)
        queries = projected[:, :query_width].astype(jnp.float32).reshape(total_len, HEADS, KEY_DIM)
        keys = projected[:, query_width:2 * query_width].astype(jnp.float32).reshape(total_len, HEADS, KEY_DIM)
        values = projected[:, 2 * query_width:].astype(jnp.float32).reshape(total_len, HEADS, VAL_DIM)
        scores = jnp.einsum('qhd,khd->hqk', queries, keys) * scale
        peak = lax.optimization_barrier(jnp.max(scores, axis=-1, keepdims=True))
        logsum = peak + jnp.log(lax.optimization_barrier(jnp.sum(jnp.exp(scores - peak), axis=-1, keepdims=True)))
        probs = jnp.exp(scores - logsum)
        probs_b = rounded(probs)
        attended = jnp.einsum('hqk,khd->qhd', probs_b, values).reshape(total_len, value_width).astype(jnp.bfloat16)
        branch = jnp.dot(attended, output_weight.T, preferred_element_type=jnp.float32)
        outputs = widen + branch
        d_attn = jnp.dot(upstream, output_weight, preferred_element_type=jnp.float32).astype(jnp.bfloat16)
        d_heads = d_attn.astype(jnp.float32).reshape(total_len, HEADS, VAL_DIM)
        attn_heads = attended.astype(jnp.float32).reshape(total_len, HEADS, VAL_DIM)
        delta = lax.optimization_barrier(jnp.sum(d_heads * attn_heads, axis=-1))
        dprob = jnp.einsum('qhd,khd->hqk', d_heads, values)
        dscore = rounded(probs * (dprob - delta.T[:, :, None]))
        d_query = jnp.einsum('hqk,khd->qhd', dscore, keys) * scale
        d_key = jnp.einsum('hqk,qhd->khd', dscore, queries) * scale
        d_value = jnp.einsum('hqk,qhd->khd', probs_b, d_heads)
        d_proj = jnp.concatenate([d_query.reshape(total_len, query_width), d_key.reshape(total_len, query_width), d_value.reshape(total_len, value_width)], axis=1).astype(jnp.bfloat16)
        d_normed = jnp.dot(d_proj, attend_weight.T, preferred_element_type=jnp.float32)
        attend_sum = block_terms(normed, d_proj)
        output_sum = block_terms(upstream, attended)
        gain_terms = lax.optimization_barrier(jnp.sum((d_normed * nhat).reshape(N_SEQ, TOK_DEV, D), axis=1))
        gain_sum = lax.optimization_barrier(jnp.sum(rounded(gain_terms), axis=0))
        return (outputs, attend_sum, output_sum, gain_sum)
    outputs, attend_sums, output_sums, gain_sums = lax.map(one_sequence, (dna_features, cotangent))
    return (outputs, lax.optimization_barrier(jnp.sum(attend_sums, axis=0)), lax.optimization_barrier(jnp.sum(output_sums, axis=0)), lax.optimization_barrier(jnp.sum(gain_sums, axis=0)))
```

```python
import functools

import jax
import jax.numpy as jnp
from jax import lax
from jax.experimental import pallas as pl
from jax.experimental.pallas import tpu as pltpu
from jax.sharding import PartitionSpec as P

HEADS = 4
KEY_DIM = 64
VAL_DIM = 192


def extended(value, sides, width):
    for axis, dim in sides:
        devices, length = (lax.axis_size(axis), value.shape[dim])
        up = [(i, (i + 1) % devices) for i in range(devices - 1)]
        down = [(j, i) for i, j in up]
        last = lax.slice_in_dim(value, length - width, length, axis=dim)
        first = lax.slice_in_dim(value, 0, width, axis=dim)
        before = lax.ppermute(last, axis, up)
        after = lax.ppermute(first, axis, down)
        value = jnp.concatenate([before, value, after], axis=dim)
    return value


def filter_block(padded, weights, bias_part):
    count = padded.shape[1] - 4
    total = bias_part
    for offset in range(5):
        total = total + jnp.einsum(
            "spc,co->spo",
            padded[:, offset : offset + count],
            weights[offset],
            preferred_element_type=jnp.float32,
        )
    activ = jax.nn.gelu(total, approximate=True)
    activ = activ.reshape(activ.shape[0], count // 2, 2, activ.shape[2])
    return (0.5 * (activ[:, :, 0] + activ[:, :, 1])).astype(jnp.bfloat16)


def per_device(
    dna_features, filter_weight, filter_bias, norm_gain, attend_weight, output_weight, cotangent
):
    padded = extended(dna_features, (("seq", 1),), 2)
    hidden = filter_block(
        padded, lax.all_gather(filter_weight, "dp", axis=2, tiled=True), filter_bias
    )
    hidden = hidden[0]
    widen = hidden.astype(jnp.float32)
    nhat = widen * lax.rsqrt(jnp.mean(widen * widen, axis=-1, keepdims=True) + 1e-06)
    normed = (nhat * norm_gain).astype(jnp.bfloat16)
    tokens = normed.shape[0]
    query_width = HEADS * KEY_DIM
    value_width = HEADS * VAL_DIM
    scale = KEY_DIM ** (-0.5)
    projected = jnp.dot(normed, attend_weight, preferred_element_type=jnp.float32).astype(
        jnp.bfloat16
    )
    queries = projected[:, :query_width]
    keys_local = projected[:, query_width : 2 * query_width]
    values_local = projected[:, 2 * query_width :]
    keys_all, values_all = (
        lax.all_gather(keys_local, "seq", axis=0, tiled=True),
        lax.all_gather(values_local, "seq", axis=0, tiled=True),
    )
    total_len = keys_all.shape[0]
    query_heads = queries.reshape(tokens, HEADS, KEY_DIM)
    key_heads = keys_all.reshape(total_len, HEADS, KEY_DIM)
    value_heads = values_all.reshape(total_len, HEADS, VAL_DIM)
    scores = (
        jnp.einsum("qhd,khd->hqk", query_heads, key_heads, preferred_element_type=jnp.float32)
        * scale
    )
    peak = jnp.max(scores, axis=-1, keepdims=True)
    logsum = peak + jnp.log(jnp.sum(jnp.exp(scores - peak), axis=-1, keepdims=True))
    probs = jnp.exp(scores - logsum)
    probs_b = probs.astype(jnp.bfloat16)
    attended = (
        jnp.einsum("hqk,khd->qhd", probs_b, value_heads, preferred_element_type=jnp.float32)
        .astype(jnp.bfloat16)
        .reshape(tokens, value_width)
    )
    branch = lax.dot_general(
        attended, output_weight, (((1,), (1,)), ((), ())), preferred_element_type=jnp.float32
    )
    outputs = widen + branch
    upstream = cotangent[0]
    output_part = lax.dot_general(
        upstream, attended, (((0,), (0,)), ((), ())), preferred_element_type=jnp.float32
    )
    d_attn = jnp.dot(upstream, output_weight, preferred_element_type=jnp.float32).astype(
        jnp.bfloat16
    )
    d_heads = d_attn.reshape(tokens, HEADS, VAL_DIM)
    attn_heads = attended.reshape(tokens, HEADS, VAL_DIM)
    delta = jnp.sum(d_heads.astype(jnp.float32) * attn_heads.astype(jnp.float32), axis=-1)
    dprob = jnp.einsum("qhd,khd->hqk", d_heads, value_heads, preferred_element_type=jnp.float32)
    dscore = (probs * (dprob - delta.T[:, :, None])).astype(jnp.bfloat16)
    d_query = (
        jnp.einsum("hqk,khd->qhd", dscore, key_heads, preferred_element_type=jnp.float32) * scale
    )
    logsum_rows = logsum[:, :, 0].T
    logsum_all, delta_all = (
        lax.all_gather(logsum_rows, "seq", axis=0, tiled=True),
        lax.all_gather(delta, "seq", axis=0, tiled=True),
    )
    key_heads_local = keys_local.reshape(tokens, HEADS, KEY_DIM)
    value_heads_local = values_local.reshape(tokens, HEADS, VAL_DIM)
    piece_query = lax.all_gather(queries, "seq", axis=0, tiled=True)
    piece_grad = lax.all_gather(d_attn, "seq", axis=0, tiled=True)
    count = piece_query.shape[0]
    piece_qheads = piece_query.reshape(count, HEADS, KEY_DIM)
    piece_gheads = piece_grad.reshape(count, HEADS, VAL_DIM)
    piece_scores = (
        jnp.einsum(
            "qhd,khd->hqk", piece_qheads, key_heads_local, preferred_element_type=jnp.float32
        )
        * scale
    )
    piece_probs = jnp.exp(piece_scores - logsum_all.T[:, :, None])
    piece_probs_b = piece_probs.astype(jnp.bfloat16)
    piece_dprob = jnp.einsum(
        "qhd,khd->hqk", piece_gheads, value_heads_local, preferred_element_type=jnp.float32
    )
    piece_dscore = (piece_probs * (piece_dprob - delta_all.T[:, :, None])).astype(jnp.bfloat16)
    grad_keys = jnp.einsum(
        "hqk,qhd->khd", piece_dscore, piece_qheads, preferred_element_type=jnp.float32
    )
    grad_values = jnp.einsum(
        "hqk,qhd->khd", piece_probs_b, piece_gheads, preferred_element_type=jnp.float32
    )
    grad_keys, grad_values = (grad_keys, grad_values)
    d_proj = jnp.concatenate(
        [
            d_query.reshape(tokens, query_width),
            (grad_keys * scale).reshape(tokens, query_width),
            grad_values.reshape(tokens, value_width),
        ],
        axis=1,
    ).astype(jnp.bfloat16)
    d_normed = lax.dot_general(
        d_proj, attend_weight, (((1,), (1,)), ((), ())), preferred_element_type=jnp.float32
    )
    attend_part = lax.dot_general(
        normed, d_proj, (((0,), (0,)), ((), ())), preferred_element_type=jnp.float32
    )
    gain_part = jnp.sum(d_normed * nhat, axis=0)
    attend_share, output_share, gain_share = (
        lax.psum_scatter(
            attend_part.astype(jnp.bfloat16), "seq", scatter_dimension=0, tiled=True
        ).astype(jnp.float32),
        lax.psum_scatter(
            output_part.astype(jnp.bfloat16), "seq", scatter_dimension=0, tiled=True
        ).astype(jnp.float32),
        lax.psum_scatter(
            gain_part.astype(jnp.bfloat16), "seq", scatter_dimension=0, tiled=True
        ).astype(jnp.float32),
    )
    grad_attend, grad_output, grad_gain = lax.psum((attend_share, output_share, gain_share), "dp")
    return (outputs[None], grad_attend, grad_output, grad_gain)


F32, BF16 = jnp.float32, jnp.bfloat16
SEQ, DP = 4, 4
TOK = 128
LEN = SEQ * TOK
CIN, WIDTH = 384, 768
SHARD = WIDTH // DP
ROWS = WIDTH // SEQ
QW, VW = HEADS * KEY_DIM, HEADS * VAL_DIM
PROJ = 2 * QW + VW
SCALE = KEY_DIM**-0.5
NN = (((1,), (0,)), ((), ()))
NT = (((1,), (1,)), ((), ()))
TN = (((0,), (0,)), ((), ()))


def mm(left, right, dims=NN):
    return lax.dot_general(left, right, dims, preferred_element_type=F32)


def half_gelu(value):
    inner = 0.7978845608028654 * (value + 0.044715 * value * value * value)
    return 0.5 * value * (1.0 + jnp.tanh(inner))


def ring(value, step):
    return lax.ppermute(value, "seq", [(i, (i + step) % SEQ) for i in range(SEQ)])


def swap(value, bit):
    return lax.ppermute(value, "dp", [(i, i ^ bit) for i in range(DP)])


def put_shards(taps, mine, other, core):
    for tap in range(5):
        lanes = slice(tap * CIN, (tap + 1) * CIN)
        rows = slice(tap * SHARD, (tap + 1) * SHARD)
        taps[pl.ds(core * SHARD, SHARD), lanes] = mine[rows, :]
        taps[pl.ds((1 - core) * SHARD, SHARD), lanes] = other[rows, :]


def filtered_half(windows, taps, bias):
    even = mm(windows[:, : 5 * CIN], taps[...], NT) + bias
    odd = mm(windows[:, CIN:], taps[...], NT) + bias
    return (0.5 * (half_gelu(even) + half_gelu(odd))).astype(BF16)


def near_kernel(f0, fa, fb, fc, w0, w1, bias, windows, hid, positions, taps):
    z, d = lax.axis_index("seq"), lax.axis_index("dp")
    chunk = 2 * TOK
    for g in range(CIN // 128):
        positions[g, 0:8, :] = jnp.zeros((8, 128), F32)
        positions[g, 8 + 2 * LEN :, :] = jnp.zeros((8, 128), F32)
        for ref, off in ((f0, 0), (fa, 3), (fb, 1), (fc, 2)):
            start = pl.multiple_of(lax.rem(z + off, SEQ) * chunk + 8, 8)
            positions[g, pl.ds(start, chunk), :] = ref[:, g * 128 : (g + 1) * 128].astype(F32)
        for k in range(6):
            at = k * CIN + g * 128
            windows[:, at : at + 128] = positions[g, pl.ds(6 + k, LEN, stride=2), :].astype(BF16)
    core = lax.rem(d, 2)
    put_shards(taps, w0, w1, core)
    hid[...] = filtered_half(windows, taps, bias[pl.ds(d // 2, 1), :])


def forward_kernel(
    windows, hid_near, w2, w3, bias, gain, aw, ow, outputs, normed_t, proj, probs_t, att_t, taps, hid, normed
):
    z, d = lax.axis_index("seq"), lax.axis_index("dp")
    side, core = d // 2, lax.rem(d, 2)
    half = WIDTH // 2
    put_shards(taps, w2, w3, core)
    hid[side] = hid_near[...]
    hid[1 - side] = filtered_half(windows, taps, bias[pl.ds(1 - side, 1), :])
    low, high = hid[0].astype(F32), hid[1].astype(F32)
    square = jnp.sum(low * low, axis=1, keepdims=True) + jnp.sum(high * high, axis=1, keepdims=True)
    inv = lax.rsqrt(square * (1.0 / WIDTH) + 1e-06)
    normed[:, :half] = (low * inv * gain[:, :half]).astype(BF16)
    normed[:, half:] = (high * inv * gain[:, half:]).astype(BF16)
    proj[...] = mm(normed[...], aw[...]).astype(BF16)
    for h in range(HEADS):
        q = proj[:, h * KEY_DIM : (h + 1) * KEY_DIM]
        k = proj[:, QW + h * KEY_DIM : QW + (h + 1) * KEY_DIM]
        v = proj[:, 2 * QW + h * VAL_DIM : 2 * QW + (h + 1) * VAL_DIM]
        scores = mm(k, q, NT) * SCALE
        top = jnp.max(scores, axis=0, keepdims=True)
        weight = jnp.exp(scores - top)
        total = jnp.sum(weight, axis=0, keepdims=True)
        probs = (weight * (1.0 / total)).astype(BF16)
        probs_t[h] = probs
        att_t[h * VAL_DIM : (h + 1) * VAL_DIM, :] = mm(v, probs, TN).astype(BF16)
    for at in range(SEQ):

        @pl.when(z == at)
        def _():
            rows = slice(at * TOK, (at + 1) * TOK)
            branch = mm(att_t[:, rows], ow[...], (((0,), (1,)), ((), ())))
            outputs[:, :half] = branch[:, :half] + hid[0, rows, :].astype(F32)
            outputs[:, half:] = branch[:, half:] + hid[1, rows, :].astype(F32)
            normed_t[...] = normed[:, at * ROWS : (at + 1) * ROWS].T


def backward_kernel(
    c0, ca, cb, cc, normed_t, proj, probs_t, att_t, gain, aw, ow, keep, send, cot, cot_t, grad, d_query, d_rest
):
    z, d = lax.axis_index("seq"), lax.axis_index("dp")
    core = lax.rem(d, 2)
    for ref, off in ((c0, 0), (ca, 3), (cb, 1), (cc, 2)):
        start = pl.multiple_of(lax.rem(z + off, SEQ) * TOK, TOK)
        cot[pl.ds(start, TOK), :] = ref[...]
    for at in range(SEQ):

        @pl.when(z == at)
        def _():
            cot_t[...] = cot[:, at * ROWS : (at + 1) * ROWS].T

    grad[...] = mm(cot[...], ow[...]).astype(BF16)
    out_part = mm(cot_t[...], att_t[...], NT)
    for h in range(HEADS):
        q = proj[:, h * KEY_DIM : (h + 1) * KEY_DIM]
        k = proj[:, QW + h * KEY_DIM : QW + (h + 1) * KEY_DIM]
        v = proj[:, 2 * QW + h * VAL_DIM : 2 * QW + (h + 1) * VAL_DIM]
        g = grad[:, h * VAL_DIM : (h + 1) * VAL_DIM]
        probs = probs_t[h].astype(F32)
        product = mm(v, g, NT) * probs
        delta = jnp.sum(product, axis=0, keepdims=True)
        dscore = (product - probs * delta).astype(BF16)
        d_query[h * KEY_DIM : (h + 1) * KEY_DIM, :] = (mm(k, dscore, TN) * SCALE).astype(BF16)
        d_rest[:, h * KEY_DIM : (h + 1) * KEY_DIM] = (mm(dscore, q) * SCALE).astype(BF16)
        d_rest[:, QW + h * VAL_DIM : QW + (h + 1) * VAL_DIM] = mm(probs_t[h], g).astype(BF16)
    query_part = mm(normed_t[...], d_query[...], NT)
    rest_part = mm(normed_t[...], d_rest[...])
    here = pl.multiple_of(z * ROWS, ROWS)
    mixed = jnp.sum(query_part * aw[pl.ds(here, ROWS), :QW].astype(F32), axis=1, keepdims=True)
    mixed = mixed + jnp.sum(rest_part * aw[pl.ds(here, ROWS), QW:].astype(F32), axis=1, keepdims=True)
    gain_part = jnp.broadcast_to(mixed, (ROWS, 128)).T[0:1, :] / gain[pl.ds(z, 1), :]
    split = PROJ // 2 - QW

    def write(ref, side):
        if side == 0:
            ref[:ROWS, :QW] = query_part.astype(ref.dtype)
            ref[:ROWS, QW : PROJ // 2] = rest_part[:, :split].astype(ref.dtype)
        else:
            ref[:ROWS, : PROJ // 2] = rest_part[:, split:].astype(ref.dtype)
        ref[:ROWS, PROJ // 2 :] = out_part[:, side * VW // 2 : (side + 1) * VW // 2].astype(ref.dtype)
        ref[ROWS:, :] = jnp.zeros((16, PROJ // 2 + VW // 2), ref.dtype)
        ref[ROWS : ROWS + 1, :ROWS] = gain_part.astype(ref.dtype)

    for at in range(2):

        @pl.when(core == at)
        def _():
            write(keep, at)
            write(send, 1 - at)


def kernel_call(body, outs, scratch, flops, bytes_accessed, *args):
    return pl.pallas_call(
        body,
        out_shape=[jax.ShapeDtypeStruct(s, t) for s, t in outs],
        scratch_shapes=[pltpu.VMEM(s, t) for s, t in scratch],
        compiler_params=pltpu.CompilerParams(vmem_limit_bytes=40 << 20),
        cost_estimate=pl.CostEstimate(flops=flops, bytes_accessed=bytes_accessed, transcendentals=0),
    )(*args)


def per_device_fast(
    dna_features, filter_weight, filter_bias, norm_gain, attend_weight, output_weight, cotangent
):
    d = lax.axis_index("dp")
    f0, c0 = dna_features[0], cotangent[0]
    w0 = filter_weight.transpose(0, 2, 1).reshape(5 * SHARD, CIN)
    w2 = swap(w0, 2)
    w1 = swap(w0, 1)
    fa, fb = ring(f0, 1), ring(f0, SEQ - 1)
    fc = ring(fa, 1)
    w2, fa, fb, fc = lax.optimization_barrier((w2, fa, fb, fc))
    w3 = swap(w2, 1)
    bias = filter_bias.reshape(2, WIDTH // 2)
    gain = norm_gain.reshape(1, WIDTH)
    windows, hid_near = kernel_call(
        near_kernel,
        [((LEN, 6 * CIN), BF16), ((LEN, WIDTH // 2), BF16)],
        [((CIN // 128, 16 + 2 * LEN, 128), F32), ((2 * SHARD, 5 * CIN), BF16)],
        2 * 2 * LEN * 5 * CIN * WIDTH // 2, 4 << 20,
        f0, fa, fb, fc, w0, w1, bias,
    )
    c0 = lax.optimization_barrier((c0, fc))[0]
    ca, cb = ring(c0, 1), ring(c0, SEQ - 1)
    cc = ring(ca, 1)
    outputs, normed_t, proj, probs_t, att_t = kernel_call(
        forward_kernel,
        [
            ((TOK, WIDTH), F32),
            ((ROWS, LEN), BF16),
            ((LEN, PROJ), BF16),
            ((HEADS, LEN, LEN), BF16),
            ((VW, LEN), BF16),
        ],
        [((2 * SHARD, 5 * CIN), BF16), ((2, LEN, WIDTH // 2), BF16), ((LEN, WIDTH), BF16)],
        5 << 30, 8 << 20,
        windows, hid_near, w2, w3, bias, gain, attend_weight, output_weight,
    )
    keep, send = kernel_call(
        backward_kernel,
        [((ROWS + 16, (PROJ + VW) // 2), F32), ((ROWS + 16, (PROJ + VW) // 2), BF16)],
        [
            ((LEN, WIDTH), BF16),
            ((ROWS, LEN), BF16),
            ((LEN, VW), BF16),
            ((QW, LEN), BF16),
            ((LEN, QW + VW), BF16),
        ],
        5 << 30, 8 << 20,
        c0, ca, cb, cc, normed_t, proj, probs_t, att_t, norm_gain.reshape(SEQ, ROWS), attend_weight, output_weight,
    )
    part = (keep + swap(send, 1).astype(F32)).astype(BF16)
    whole = (part.astype(F32) + swap(part, 2).astype(F32)).astype(BF16)
    other = swap(whole, 1)
    first = lax.rem(d, 2) == 0
    low = jnp.where(first, whole, other).astype(F32)
    high = jnp.where(first, other, whole).astype(F32)
    cut = PROJ // 2
    grad_attend = jnp.concatenate([low[:ROWS, :cut], high[:ROWS, :cut]], axis=1)
    grad_output = jnp.concatenate([low[:ROWS, cut:], high[:ROWS, cut:]], axis=1)
    return outputs[None], grad_attend, grad_output, low[ROWS, :ROWS]


def solution(mesh):
    small = mesh.shape["seq"] == SEQ and mesh.shape["dp"] == DP
    return jax.shard_map(
        per_device_fast if small else per_device,
        mesh=mesh,
        in_specs=(
            P(("groups", "dp"), "seq", None),
            P(None, None, "dp"),
            P(),
            P(),
            P(),
            P(),
            P(("groups", "dp"), "seq", None),
        ),
        out_specs=(
            P(("groups", "dp"), "seq", None),
            P(("groups", "seq"), None),
            P(("groups", "seq"), None),
            P(("groups", "seq")),
        ),
        check_vma=False,
    )
```

```python
import functools

import jax
import jax.numpy as jnp
from jax import lax
from jax.experimental import pallas as pl
from jax.experimental.pallas import tpu as pltpu
from jax.sharding import PartitionSpec as P

HEADS = 4
KEY_DIM = 64
VAL_DIM = 192


def extended(value, sides, width):
    for axis, dim in sides:
        devices, length = (lax.axis_size(axis), value.shape[dim])
        up = [(i, (i + 1) % devices) for i in range(devices - 1)]
        down = [(j, i) for i, j in up]
        last = lax.slice_in_dim(value, length - width, length, axis=dim)
        first = lax.slice_in_dim(value, 0, width, axis=dim)
        before = lax.ppermute(last, axis, up)
        after = lax.ppermute(first, axis, down)
        value = jnp.concatenate([before, value, after], axis=dim)
    return value


def filter_block(padded, weights, bias_part):
    count = padded.shape[1] - 4
    total = bias_part
    for offset in range(5):
        total = total + jnp.einsum(
            "spc,co->spo",
            padded[:, offset : offset + count],
            weights[offset],
            preferred_element_type=jnp.float32,
        )
    activ = jax.nn.gelu(total, approximate=True)
    activ = activ.reshape(activ.shape[0], count // 2, 2, activ.shape[2])
    return (0.5 * (activ[:, :, 0] + activ[:, :, 1])).astype(jnp.bfloat16)


def per_device(
    dna_features, filter_weight, filter_bias, norm_gain, attend_weight, output_weight, cotangent
):
    padded = extended(dna_features, (("seq", 1),), 2)
    hidden = filter_block(
        padded, lax.all_gather(filter_weight, "dp", axis=2, tiled=True), filter_bias
    )
    hidden = hidden[0]
    widen = hidden.astype(jnp.float32)
    nhat = widen * lax.rsqrt(jnp.mean(widen * widen, axis=-1, keepdims=True) + 1e-06)
    normed = (nhat * norm_gain).astype(jnp.bfloat16)
    tokens = normed.shape[0]
    query_width = HEADS * KEY_DIM
    value_width = HEADS * VAL_DIM
    scale = KEY_DIM ** (-0.5)
    projected = jnp.dot(normed, attend_weight, preferred_element_type=jnp.float32).astype(
        jnp.bfloat16
    )
    queries = projected[:, :query_width]
    keys_local = projected[:, query_width : 2 * query_width]
    values_local = projected[:, 2 * query_width :]
    keys_all, values_all = (
        lax.all_gather(keys_local, "seq", axis=0, tiled=True),
        lax.all_gather(values_local, "seq", axis=0, tiled=True),
    )
    total_len = keys_all.shape[0]
    query_heads = queries.reshape(tokens, HEADS, KEY_DIM)
    key_heads = keys_all.reshape(total_len, HEADS, KEY_DIM)
    value_heads = values_all.reshape(total_len, HEADS, VAL_DIM)
    scores = (
        jnp.einsum("qhd,khd->hqk", query_heads, key_heads, preferred_element_type=jnp.float32)
        * scale
    )
    peak = jnp.max(scores, axis=-1, keepdims=True)
    logsum = peak + jnp.log(jnp.sum(jnp.exp(scores - peak), axis=-1, keepdims=True))
    probs = jnp.exp(scores - logsum)
    probs_b = probs.astype(jnp.bfloat16)
    attended = (
        jnp.einsum("hqk,khd->qhd", probs_b, value_heads, preferred_element_type=jnp.float32)
        .astype(jnp.bfloat16)
        .reshape(tokens, value_width)
    )
    branch = lax.dot_general(
        attended, output_weight, (((1,), (1,)), ((), ())), preferred_element_type=jnp.float32
    )
    outputs = widen + branch
    upstream = cotangent[0]
    output_part = lax.dot_general(
        upstream, attended, (((0,), (0,)), ((), ())), preferred_element_type=jnp.float32
    )
    d_attn = jnp.dot(upstream, output_weight, preferred_element_type=jnp.float32).astype(
        jnp.bfloat16
    )
    d_heads = d_attn.reshape(tokens, HEADS, VAL_DIM)
    attn_heads = attended.reshape(tokens, HEADS, VAL_DIM)
    delta = jnp.sum(d_heads.astype(jnp.float32) * attn_heads.astype(jnp.float32), axis=-1)
    dprob = jnp.einsum("qhd,khd->hqk", d_heads, value_heads, preferred_element_type=jnp.float32)
    dscore = (probs * (dprob - delta.T[:, :, None])).astype(jnp.bfloat16)
    d_query = (
        jnp.einsum("hqk,khd->qhd", dscore, key_heads, preferred_element_type=jnp.float32) * scale
    )
    logsum_rows = logsum[:, :, 0].T
    logsum_all, delta_all = (
        lax.all_gather(logsum_rows, "seq", axis=0, tiled=True),
        lax.all_gather(delta, "seq", axis=0, tiled=True),
    )
    key_heads_local = keys_local.reshape(tokens, HEADS, KEY_DIM)
    value_heads_local = values_local.reshape(tokens, HEADS, VAL_DIM)
    piece_query = lax.all_gather(queries, "seq", axis=0, tiled=True)
    piece_grad = lax.all_gather(d_attn, "seq", axis=0, tiled=True)
    count = piece_query.shape[0]
    piece_qheads = piece_query.reshape(count, HEADS, KEY_DIM)
    piece_gheads = piece_grad.reshape(count, HEADS, VAL_DIM)
    piece_scores = (
        jnp.einsum(
            "qhd,khd->hqk", piece_qheads, key_heads_local, preferred_element_type=jnp.float32
        )
        * scale
    )
    piece_probs = jnp.exp(piece_scores - logsum_all.T[:, :, None])
    piece_probs_b = piece_probs.astype(jnp.bfloat16)
    piece_dprob = jnp.einsum(
        "qhd,khd->hqk", piece_gheads, value_heads_local, preferred_element_type=jnp.float32
    )
    piece_dscore = (piece_probs * (piece_dprob - delta_all.T[:, :, None])).astype(jnp.bfloat16)
    grad_keys = jnp.einsum(
        "hqk,qhd->khd", piece_dscore, piece_qheads, preferred_element_type=jnp.float32
    )
    grad_values = jnp.einsum(
        "hqk,qhd->khd", piece_probs_b, piece_gheads, preferred_element_type=jnp.float32
    )
    grad_keys, grad_values = (grad_keys, grad_values)
    d_proj = jnp.concatenate(
        [
            d_query.reshape(tokens, query_width),
            (grad_keys * scale).reshape(tokens, query_width),
            grad_values.reshape(tokens, value_width),
        ],
        axis=1,
    ).astype(jnp.bfloat16)
    d_normed = lax.dot_general(
        d_proj, attend_weight, (((1,), (1,)), ((), ())), preferred_element_type=jnp.float32
    )
    attend_part = lax.dot_general(
        normed, d_proj, (((0,), (0,)), ((), ())), preferred_element_type=jnp.float32
    )
    gain_part = jnp.sum(d_normed * nhat, axis=0)
    attend_share, output_share, gain_share = (
        lax.psum_scatter(
            attend_part.astype(jnp.bfloat16), "seq", scatter_dimension=0, tiled=True
        ).astype(jnp.float32),
        lax.psum_scatter(
            output_part.astype(jnp.bfloat16), "seq", scatter_dimension=0, tiled=True
        ).astype(jnp.float32),
        lax.psum_scatter(
            gain_part.astype(jnp.bfloat16), "seq", scatter_dimension=0, tiled=True
        ).astype(jnp.float32),
    )
    grad_attend, grad_output, grad_gain = lax.psum((attend_share, output_share, gain_share), "dp")
    return (outputs[None], grad_attend, grad_output, grad_gain)


F32, BF16 = jnp.float32, jnp.bfloat16
SEQ, DP = 4, 4
TOK = 128
LEN = SEQ * TOK
CIN, WIDTH = 384, 768
SHARD = WIDTH // DP
ROWS = WIDTH // SEQ
QW, VW = HEADS * KEY_DIM, HEADS * VAL_DIM
PROJ = 2 * QW + VW
SCALE = KEY_DIM**-0.5
NN = (((1,), (0,)), ((), ()))
NT = (((1,), (1,)), ((), ()))
TN = (((0,), (0,)), ((), ()))


def mm(left, right, dims=NN):
    return lax.dot_general(left, right, dims, preferred_element_type=F32)


def half_gelu(value):
    inner = 0.7978845608028654 * (value + 0.044715 * value * value * value)
    return 0.5 * value * (1.0 + jnp.tanh(inner))


def ring(value, step):
    return lax.ppermute(value, "seq", [(i, (i + step) % SEQ) for i in range(SEQ)])


def swap(value, bit):
    return lax.ppermute(value, "dp", [(i, i ^ bit) for i in range(DP)])


def put_shards(taps, mine, other, core):
    for tap in range(5):
        lanes = slice(tap * CIN, (tap + 1) * CIN)
        rows = slice(tap * SHARD, (tap + 1) * SHARD)
        taps[pl.ds(core * SHARD, SHARD), lanes] = mine[rows, :]
        taps[pl.ds((1 - core) * SHARD, SHARD), lanes] = other[rows, :]


def half_of(bias, side):
    both = bias[...].reshape(1, WIDTH)
    return jnp.where(side == 0, both[:, : WIDTH // 2], both[:, WIDTH // 2 :])


def filtered_half(windows, taps, bias):
    even = mm(windows[:, : 5 * CIN], taps[...], NT) + bias
    odd = mm(windows[:, CIN:], taps[...], NT) + bias
    return (0.5 * (half_gelu(even) + half_gelu(odd))).astype(BF16)


def taps_kernel(w0_far, w1, taps, w0, sems):
    load = pltpu.make_async_copy(w0_far, w0, sems.at[0])
    load.start()
    load.wait()
    put_shards(taps, w0, w1, lax.rem(lax.axis_index("dp"), 2))


def near_kernel(f0, fa, fb, fc, taps, bias, windows, hid, positions):
    z, d = lax.axis_index("seq"), lax.axis_index("dp")
    chunk = 2 * TOK
    for g in range(CIN // 128):
        positions[g, 0:8, :] = jnp.zeros((8, 128), F32)
        positions[g, 8 + 2 * LEN :, :] = jnp.zeros((8, 128), F32)
        for ref, off in ((f0, 0), (fa, 3), (fb, 1), (fc, 2)):
            start = pl.multiple_of(lax.rem(z + off, SEQ) * chunk + 8, 8)
            positions[g, pl.ds(start, chunk), :] = ref[:, g * 128 : (g + 1) * 128].astype(F32)
        for k in range(6):
            at = k * CIN + g * 128
            windows[:, at : at + 128] = positions[g, pl.ds(6 + k, LEN, stride=2), :].astype(BF16)
    hid[...] = filtered_half(windows[: LEN // 2, :], taps, half_of(bias, d // 2))


def rest_kernel(windows, taps, bias, hid):
    hid[...] = filtered_half(windows[LEN // 2 :, :], taps, half_of(bias, lax.axis_index("dp") // 2))


def project_kernel(windows, hid_near, hid_rest, w2, w3, bias, gain, aw, hid, normed, proj, normed_t, taps):
    z, d = lax.axis_index("seq"), lax.axis_index("dp")
    side, half = d // 2, WIDTH // 2
    put_shards(taps, w2, w3, lax.rem(d, 2))
    hid[side, : LEN // 2, :] = hid_near[...]
    hid[side, LEN // 2 :, :] = hid_rest[...]
    hid[1 - side] = filtered_half(windows, taps, half_of(bias, 1 - side))
    low, high = hid[0].astype(F32), hid[1].astype(F32)
    square = jnp.sum(low * low, axis=1, keepdims=True) + jnp.sum(high * high, axis=1, keepdims=True)
    inv = lax.rsqrt(square * (1.0 / WIDTH) + 1e-06)
    scales = gain[...].reshape(1, WIDTH)
    normed[:, :half] = (low * inv * scales[:, :half]).astype(BF16)
    normed[:, half:] = (high * inv * scales[:, half:]).astype(BF16)
    proj[...] = mm(normed[...], aw[...]).astype(BF16)
    for at in range(SEQ):

        @pl.when(z == at)
        def _():
            normed_t[...] = normed[:, at * ROWS : (at + 1) * ROWS].T


def heads_of(proj, h):
    q = proj[:, h * KEY_DIM : (h + 1) * KEY_DIM]
    k = proj[:, QW + h * KEY_DIM : QW + (h + 1) * KEY_DIM]
    v = proj[:, 2 * QW + h * VAL_DIM : 2 * QW + (h + 1) * VAL_DIM]
    return q, k, v


def attend_kernel(proj, probs_t, att_t):
    for h in range(HEADS):
        q, k, v = heads_of(proj, h)
        scores = mm(k, q, NT) * SCALE
        top = jnp.max(scores, axis=0, keepdims=True)
        weight = jnp.exp(scores - top)
        total = jnp.sum(weight, axis=0, keepdims=True)
        probs = (weight * (1.0 / total)).astype(BF16)
        probs_t[h] = probs
        att_t[h * VAL_DIM : (h + 1) * VAL_DIM, :] = mm(v, probs, TN).astype(BF16)


def outputs_kernel(hid, att_t, ow, outputs):
    z = lax.axis_index("seq")
    half = WIDTH // 2
    for at in range(SEQ):

        @pl.when(z == at)
        def _():
            rows = slice(at * TOK, (at + 1) * TOK)
            branch = mm(att_t[:, rows], ow[...], (((0,), (1,)), ((), ())))
            outputs[:, :half] = branch[:, :half] + hid[0, rows, :].astype(F32)
            outputs[:, half:] = branch[:, half:] + hid[1, rows, :].astype(F32)


def both_ways(write, keep, send, core):
    for at in range(2):

        @pl.when(core == at)
        def _():
            write(keep, at)
            write(send, 1 - at)


def value_kernel(c0, ca, cb, cc, normed_t, probs_t, att_t, aw, ow, grad, keep, send, mixed, cot, cot_t, d_value):
    z, d = lax.axis_index("seq"), lax.axis_index("dp")
    for ref, off in ((c0, 0), (ca, 3), (cb, 1), (cc, 2)):
        start = pl.multiple_of(lax.rem(z + off, SEQ) * TOK, TOK)
        cot[pl.ds(start, TOK), :] = ref[...]
    for at in range(SEQ):

        @pl.when(z == at)
        def _():
            cot_t[...] = cot[:, at * ROWS : (at + 1) * ROWS].T

    grad[...] = mm(cot[...], ow[...]).astype(BF16)
    out_part = mm(cot_t[...], att_t[...], NT)
    for h in range(HEADS):
        lanes = slice(h * VAL_DIM, (h + 1) * VAL_DIM)
        d_value[:, lanes] = mm(probs_t[h], grad[:, lanes]).astype(BF16)
    value_part = mm(normed_t[...], d_value[...])
    here = pl.multiple_of(z * ROWS, ROWS)
    total = jnp.sum(value_part * aw[pl.ds(here, ROWS), 2 * QW :].astype(F32), axis=1, keepdims=True)
    mixed[...] = jnp.broadcast_to(total, (ROWS, 128))
    half = VW // 2

    def write(ref, side):
        lanes = slice(side * half, (side + 1) * half)
        ref[:, :half] = value_part[:, lanes].astype(ref.dtype)
        ref[:, half:] = out_part[:, lanes].astype(ref.dtype)

    both_ways(write, keep, send, lax.rem(d, 2))


def score_grads(grad, proj, probs_t, d_query, d_key, first):
    for h in range(first, first + HEADS // 2):
        q, k, v = heads_of(proj, h)
        probs = probs_t[h].astype(F32)
        product = mm(v, grad[:, h * VAL_DIM : (h + 1) * VAL_DIM], NT) * probs
        delta = jnp.sum(product, axis=0, keepdims=True)
        dscore = (product - probs * delta).astype(BF16)
        lanes = slice((h - first) * KEY_DIM, (h - first + 1) * KEY_DIM)
        d_query[lanes, :] = (mm(k, dscore, TN) * SCALE).astype(BF16)
        d_key[:, lanes] = (mm(dscore, q) * SCALE).astype(BF16)


def early_key_kernel(grad, proj, probs_t, d_query, d_key):
    score_grads(grad, proj, probs_t, d_query, d_key, 0)


def late_key_kernel(
    grad, proj, probs_t, query_early, key_early, normed_t, mixed, gain, aw, keep, send, d_query, d_key
):
    z, d = lax.axis_index("seq"), lax.axis_index("dp")
    score_grads(grad, proj, probs_t, d_query, d_key, HEADS // 2)
    left = normed_t[...]
    query_part = jnp.concatenate([mm(left, query_early[...], NT), mm(left, d_query[...], NT)], axis=1)
    key_part = jnp.concatenate([mm(left, key_early[...]), mm(left, d_key[...])], axis=1)
    here = pl.multiple_of(z * ROWS, ROWS)
    total = query_part * aw[pl.ds(here, ROWS), :QW].astype(F32)
    total = total + key_part * aw[pl.ds(here, ROWS), QW : 2 * QW].astype(F32)
    total = mixed[...] + jnp.sum(total, axis=1, keepdims=True)
    scales = gain[...].reshape(1, WIDTH)
    mine = scales[:, :ROWS]
    for at in range(1, SEQ):
        mine = jnp.where(z == at, scales[:, at * ROWS : (at + 1) * ROWS], mine)
    gain_part = total.T[0:1, :] / mine

    def write(ref, side):
        ref[:ROWS, :] = (key_part if side else query_part).astype(ref.dtype)
        ref[ROWS:, :] = jnp.zeros((16, QW), ref.dtype)
        ref[ROWS : ROWS + 1, :ROWS] = gain_part.astype(ref.dtype)

    both_ways(write, keep, send, lax.rem(d, 2))


def finish_kernel(whole_v, whole_k, top_v, rest_v, other_k, grad_attend, grad_output, grad_gain):
    half = VW // 2

    def place(source, rows, side):
        lanes = slice(side * half, (side + 1) * half)
        grad_attend[rows, 2 * QW + side * half : 2 * QW + (side + 1) * half] = source[:, :half].astype(F32)
        grad_output[rows, lanes] = source[:, half:].astype(F32)

    for at in range(2):

        @pl.when(lax.rem(lax.axis_index("dp"), 2) == at)
        def _():
            place(whole_v, slice(0, ROWS), at)
            place(top_v, slice(0, ROWS // 2), 1 - at)
            place(rest_v, slice(ROWS // 2, ROWS), 1 - at)
            low, high = (whole_k, other_k) if at == 0 else (other_k, whole_k)
            grad_attend[:, :QW] = low[:ROWS, :].astype(F32)
            grad_attend[:, QW : 2 * QW] = high[:ROWS, :].astype(F32)
            grad_gain[...] = low[ROWS : ROWS + 8, :ROWS].astype(F32)[0]


def kernel_call(body, outs, scratch, flops, *args, far=()):
    whole = pl.BlockSpec(memory_space=pltpu.VMEM)
    away = pl.BlockSpec(memory_space=pltpu.HBM)
    sems = [pltpu.SemaphoreType.DMA((len(far),))] if far else []
    return pl.pallas_call(
        body,
        in_specs=[away if i in far else whole for i in range(len(args))],
        out_shape=[jax.ShapeDtypeStruct(s, t) for s, t in outs],
        scratch_shapes=[pltpu.VMEM(s, t) for s, t in scratch] + sems,
        compiler_params=pltpu.CompilerParams(vmem_limit_bytes=40 << 20),
        cost_estimate=pl.CostEstimate(flops=flops, bytes_accessed=1 << 16, transcendentals=0),
    )(*args)


def combined(keep, arrived):
    return (keep.astype(F32) + arrived.astype(F32)).astype(BF16)


def per_device_fast(
    dna_features, filter_weight, filter_bias, norm_gain, attend_weight, output_weight, cotangent
):
    f0, c0 = dna_features[0], cotangent[0]
    w0 = filter_weight.transpose(0, 2, 1).reshape(5 * SHARD, CIN)
    half = WIDTH // 2
    w2 = swap(w0, 2)
    w1 = swap(w0, 1)
    fa, fb = ring(f0, 1), ring(f0, SEQ - 1)
    (taps,) = kernel_call(
        taps_kernel,
        [((2 * SHARD, 5 * CIN), BF16)],
        [((5 * SHARD, CIN), BF16)],
        1 << 31,
        pltpu.with_memory_space_constraint(w0, pltpu.HBM), w1,
        far=(0,),
    )
    ca = ring(c0, 1)
    far_a, taps = lax.optimization_barrier((fa, taps))
    to_left, far_a, fb = lax.optimization_barrier((c0, far_a, fb))
    fc = ring(far_a, 1)
    cb, cc = ring(to_left, SEQ - 1), ring(ca, 1)
    fc, ca = lax.optimization_barrier((fc, ca))
    windows, hid_near = kernel_call(
        near_kernel,
        [((LEN, 6 * CIN), BF16), ((LEN // 2, half), BF16)],
        [((CIN // 128, 16 + 2 * LEN, 128), F32)],
        1 << 16,
        f0, fa, fb, fc, taps, filter_bias,
    )
    w2, windows = lax.optimization_barrier((w2, windows))
    w3 = swap(w2, 1)
    (hid_rest,) = kernel_call(
        rest_kernel, [((LEN // 2, half), BF16)], [], 1 << 33, windows, taps, filter_bias
    )
    hid, normed, proj, normed_t = kernel_call(
        project_kernel,
        [((2, LEN, half), BF16), ((LEN, WIDTH), BF16), ((LEN, PROJ), BF16), ((ROWS, LEN), BF16)],
        [((2 * SHARD, 5 * CIN), BF16)],
        1 << 24,
        windows, hid_near, hid_rest, w2, w3, filter_bias, norm_gain, attend_weight,
    )
    probs_t, att_t = kernel_call(
        attend_kernel,
        [((HEADS, LEN, LEN), BF16), ((VW, LEN), BF16)],
        [],
        1 << 31,
        proj,
    )
    (outputs,) = kernel_call(
        outputs_kernel, [((TOK, WIDTH), F32)], [], 1 << 31, hid, att_t, output_weight
    )
    grad, keep_v, send_v, mixed = kernel_call(
        value_kernel,
        [((LEN, VW), BF16), ((ROWS, VW), F32), ((ROWS, VW), BF16), ((ROWS, 128), F32)],
        [((LEN, WIDTH), BF16), ((ROWS, LEN), BF16), ((LEN, VW), BF16)],
        1 << 33,
        c0, ca, cb, cc, normed_t, probs_t, att_t, attend_weight, output_weight,
    )
    query_early, key_early = kernel_call(
        early_key_kernel,
        [((QW // 2, LEN), BF16), ((LEN, QW // 2), BF16)],
        [],
        1 << 24,
        grad, proj, probs_t,
    )
    part_v = combined(keep_v, swap(send_v, 1))
    part_v, query_early = lax.optimization_barrier((part_v, query_early))
    keep_k, send_k = kernel_call(
        late_key_kernel,
        [((ROWS + 16, QW), F32), ((ROWS + 16, QW), BF16)],
        [((QW // 2, LEN), BF16), ((LEN, QW // 2), BF16)],
        1 << 29,
        grad, proj, probs_t, query_early, key_early, normed_t, mixed, norm_gain, attend_weight,
    )
    arrived_v = swap(part_v, 2)
    part_k = combined(keep_k, swap(send_k, 1))
    arrived_k = swap(part_k, 2)
    arrived_v = lax.optimization_barrier((arrived_v, part_k))[0]
    whole_v, whole_k = combined(part_v, arrived_v), combined(part_k, arrived_k)
    other_k = swap(whole_k, 1)
    top = swap(whole_v[: ROWS // 2], 1)
    rest, top = lax.optimization_barrier((whole_v[ROWS // 2 :], top))
    other_v = (top, swap(rest, 1))
    grad_attend, grad_output, grad_gain = kernel_call(
        finish_kernel,
        [((ROWS, PROJ), F32), ((ROWS, WIDTH), F32), ((ROWS,), F32)],
        [],
        1 << 24,
        whole_v, whole_k, *other_v, other_k,
    )
    return outputs[None], grad_attend, grad_output, grad_gain


def solution(mesh):
    small = mesh.shape["seq"] == SEQ and mesh.shape["dp"] == DP
    return jax.shard_map(
        per_device_fast if small else per_device,
        mesh=mesh,
        in_specs=(
            P(("groups", "dp"), "seq", None),
            P(None, None, "dp"),
            P(),
            P(),
            P(),
            P(),
            P(("groups", "dp"), "seq", None),
        ),
        out_specs=(
            P(("groups", "dp"), "seq", None),
            P(("groups", "seq"), None),
            P(("groups", "seq"), None),
            P(("groups", "seq")),
        ),
        check_vma=False,
    )
```

```python
import functools

import jax
import jax.numpy as jnp
from jax import lax
from jax.experimental import pallas as pl
from jax.experimental.pallas import tpu as pltpu
from jax.sharding import PartitionSpec as P

HEADS = 4
KEY_DIM = 64
VAL_DIM = 192


def extended(value, sides, width):
    for axis, dim in sides:
        devices, length = (lax.axis_size(axis), value.shape[dim])
        up = [(i, (i + 1) % devices) for i in range(devices - 1)]
        down = [(j, i) for i, j in up]
        last = lax.slice_in_dim(value, length - width, length, axis=dim)
        first = lax.slice_in_dim(value, 0, width, axis=dim)
        before = lax.ppermute(last, axis, up)
        after = lax.ppermute(first, axis, down)
        value = jnp.concatenate([before, value, after], axis=dim)
    return value


def filter_block(padded, weights, bias_part):
    count = padded.shape[1] - 4
    total = bias_part
    for offset in range(5):
        total = total + jnp.einsum(
            "spc,co->spo",
            padded[:, offset : offset + count],
            weights[offset],
            preferred_element_type=jnp.float32,
        )
    activ = jax.nn.gelu(total, approximate=True)
    activ = activ.reshape(activ.shape[0], count // 2, 2, activ.shape[2])
    return (0.5 * (activ[:, :, 0] + activ[:, :, 1])).astype(jnp.bfloat16)


def per_device(
    dna_features, filter_weight, filter_bias, norm_gain, attend_weight, output_weight, cotangent
):
    padded = extended(dna_features, (("seq", 1),), 2)
    hidden = filter_block(
        padded, lax.all_gather(filter_weight, "dp", axis=2, tiled=True), filter_bias
    )
    hidden = hidden[0]
    widen = hidden.astype(jnp.float32)
    nhat = widen * lax.rsqrt(jnp.mean(widen * widen, axis=-1, keepdims=True) + 1e-06)
    normed = (nhat * norm_gain).astype(jnp.bfloat16)
    tokens = normed.shape[0]
    query_width = HEADS * KEY_DIM
    value_width = HEADS * VAL_DIM
    scale = KEY_DIM ** (-0.5)
    projected = jnp.dot(normed, attend_weight, preferred_element_type=jnp.float32).astype(
        jnp.bfloat16
    )
    queries = projected[:, :query_width]
    keys_local = projected[:, query_width : 2 * query_width]
    values_local = projected[:, 2 * query_width :]
    keys_all, values_all = (
        lax.all_gather(keys_local, "seq", axis=0, tiled=True),
        lax.all_gather(values_local, "seq", axis=0, tiled=True),
    )
    total_len = keys_all.shape[0]
    query_heads = queries.reshape(tokens, HEADS, KEY_DIM)
    key_heads = keys_all.reshape(total_len, HEADS, KEY_DIM)
    value_heads = values_all.reshape(total_len, HEADS, VAL_DIM)
    scores = (
        jnp.einsum("qhd,khd->hqk", query_heads, key_heads, preferred_element_type=jnp.float32)
        * scale
    )
    peak = jnp.max(scores, axis=-1, keepdims=True)
    logsum = peak + jnp.log(jnp.sum(jnp.exp(scores - peak), axis=-1, keepdims=True))
    probs = jnp.exp(scores - logsum)
    probs_b = probs.astype(jnp.bfloat16)
    attended = (
        jnp.einsum("hqk,khd->qhd", probs_b, value_heads, preferred_element_type=jnp.float32)
        .astype(jnp.bfloat16)
        .reshape(tokens, value_width)
    )
    branch = lax.dot_general(
        attended, output_weight, (((1,), (1,)), ((), ())), preferred_element_type=jnp.float32
    )
    outputs = widen + branch
    upstream = cotangent[0]
    output_part = lax.dot_general(
        upstream, attended, (((0,), (0,)), ((), ())), preferred_element_type=jnp.float32
    )
    d_attn = jnp.dot(upstream, output_weight, preferred_element_type=jnp.float32).astype(
        jnp.bfloat16
    )
    d_heads = d_attn.reshape(tokens, HEADS, VAL_DIM)
    attn_heads = attended.reshape(tokens, HEADS, VAL_DIM)
    delta = jnp.sum(d_heads.astype(jnp.float32) * attn_heads.astype(jnp.float32), axis=-1)
    dprob = jnp.einsum("qhd,khd->hqk", d_heads, value_heads, preferred_element_type=jnp.float32)
    dscore = (probs * (dprob - delta.T[:, :, None])).astype(jnp.bfloat16)
    d_query = (
        jnp.einsum("hqk,khd->qhd", dscore, key_heads, preferred_element_type=jnp.float32) * scale
    )
    logsum_rows = logsum[:, :, 0].T
    logsum_all, delta_all = (
        lax.all_gather(logsum_rows, "seq", axis=0, tiled=True),
        lax.all_gather(delta, "seq", axis=0, tiled=True),
    )
    key_heads_local = keys_local.reshape(tokens, HEADS, KEY_DIM)
    value_heads_local = values_local.reshape(tokens, HEADS, VAL_DIM)
    piece_query = lax.all_gather(queries, "seq", axis=0, tiled=True)
    piece_grad = lax.all_gather(d_attn, "seq", axis=0, tiled=True)
    count = piece_query.shape[0]
    piece_qheads = piece_query.reshape(count, HEADS, KEY_DIM)
    piece_gheads = piece_grad.reshape(count, HEADS, VAL_DIM)
    piece_scores = (
        jnp.einsum(
            "qhd,khd->hqk", piece_qheads, key_heads_local, preferred_element_type=jnp.float32
        )
        * scale
    )
    piece_probs = jnp.exp(piece_scores - logsum_all.T[:, :, None])
    piece_probs_b = piece_probs.astype(jnp.bfloat16)
    piece_dprob = jnp.einsum(
        "qhd,khd->hqk", piece_gheads, value_heads_local, preferred_element_type=jnp.float32
    )
    piece_dscore = (piece_probs * (piece_dprob - delta_all.T[:, :, None])).astype(jnp.bfloat16)
    grad_keys = jnp.einsum(
        "hqk,qhd->khd", piece_dscore, piece_qheads, preferred_element_type=jnp.float32
    )
    grad_values = jnp.einsum(
        "hqk,qhd->khd", piece_probs_b, piece_gheads, preferred_element_type=jnp.float32
    )
    grad_keys, grad_values = (grad_keys, grad_values)
    d_proj = jnp.concatenate(
        [
            d_query.reshape(tokens, query_width),
            (grad_keys * scale).reshape(tokens, query_width),
            grad_values.reshape(tokens, value_width),
        ],
        axis=1,
    ).astype(jnp.bfloat16)
    d_normed = lax.dot_general(
        d_proj, attend_weight, (((1,), (1,)), ((), ())), preferred_element_type=jnp.float32
    )
    attend_part = lax.dot_general(
        normed, d_proj, (((0,), (0,)), ((), ())), preferred_element_type=jnp.float32
    )
    gain_part = jnp.sum(d_normed * nhat, axis=0)
    attend_share, output_share, gain_share = (
        lax.psum_scatter(
            attend_part.astype(jnp.bfloat16), "seq", scatter_dimension=0, tiled=True
        ).astype(jnp.float32),
        lax.psum_scatter(
            output_part.astype(jnp.bfloat16), "seq", scatter_dimension=0, tiled=True
        ).astype(jnp.float32),
        lax.psum_scatter(
            gain_part.astype(jnp.bfloat16), "seq", scatter_dimension=0, tiled=True
        ).astype(jnp.float32),
    )
    grad_attend, grad_output, grad_gain = lax.psum((attend_share, output_share, gain_share), "dp")
    return (outputs[None], grad_attend, grad_output, grad_gain)


F32, BF16 = jnp.float32, jnp.bfloat16
SEQ, DP = 4, 4
TOK = 128
EDGE = 16
LEN = SEQ * TOK
CIN, WIDTH = 384, 768
SHARD = WIDTH // DP
ROWS = WIDTH // SEQ
QW, VW = HEADS * KEY_DIM, HEADS * VAL_DIM
PROJ = 2 * QW + VW
SCALE = KEY_DIM**-0.5
NN = (((1,), (0,)), ((), ()))
NT = (((1,), (1,)), ((), ()))
TN = (((0,), (0,)), ((), ()))


def mm(left, right, dims=NN):
    return lax.dot_general(left, right, dims, preferred_element_type=F32)


def half_gelu(value):
    inner = 0.7978845608028654 * (value + 0.044715 * value * value * value)
    return 0.5 * value * (1.0 + jnp.tanh(inner))


def ring(value, step):
    return lax.ppermute(value, "seq", [(i, (i + step) % SEQ) for i in range(SEQ)])


def swap(value, bit):
    return lax.ppermute(value, "dp", [(i, i ^ bit) for i in range(DP)])


def put_shards(taps, mine, other, core):
    for tap in range(5):
        lanes = slice(tap * CIN, (tap + 1) * CIN)
        rows = slice(tap * SHARD, (tap + 1) * SHARD)
        taps[pl.ds(core * SHARD, SHARD), lanes] = mine[rows, :]
        taps[pl.ds((1 - core) * SHARD, SHARD), lanes] = other[rows, :]


def half_of(bias, side):
    both = bias[...].reshape(1, WIDTH)
    return jnp.where(side == 0, both[:, : WIDTH // 2], both[:, WIDTH // 2 :])


def filtered_half(windows, taps, bias):
    even = mm(windows[:, : 5 * CIN], taps[...], NT) + bias
    odd = mm(windows[:, CIN:], taps[...], NT) + bias
    return (0.5 * (half_gelu(even) + half_gelu(odd))).astype(BF16)


def taps_kernel(w0_far, w1, taps, w0, sems):
    load = pltpu.make_async_copy(w0_far, w0, sems.at[0])
    load.start()
    load.wait()
    put_shards(taps, w0, w1, lax.rem(lax.axis_index("dp"), 2))


def fill_positions(positions, z, parts):
    chunk = 2 * TOK
    for g in range(CIN // 128):
        positions[g, 0:8, :] = jnp.zeros((8, 128), F32)
        positions[g, 8 + 2 * LEN :, :] = jnp.zeros((8, 128), F32)
        for ref, off in parts:
            start = pl.multiple_of(lax.rem(z + off, SEQ) * chunk + 8, 8)
            if ref is None:
                positions[g, pl.ds(start, chunk), :] = jnp.zeros((chunk, 128), F32)
            else:
                positions[g, pl.ds(start, chunk), :] = ref[:, g * 128 : (g + 1) * 128].astype(F32)


def near_kernel(f0, fa, fb, taps, bias, windows, hid, positions):
    z, d = lax.axis_index("seq"), lax.axis_index("dp")
    fill_positions(positions, z, ((f0, 0), (fa, 3), (fb, 1), (None, 2)))
    for g in range(CIN // 128):
        for k in range(6):
            at = k * CIN + g * 128
            windows[:, at : at + 128] = positions[g, pl.ds(6 + k, LEN, stride=2), :].astype(BF16)
    hid[...] = filtered_half(windows, taps, half_of(bias, d // 2))


def row_picker(z):
    row = lax.broadcasted_iota(jnp.int32, (ROWS, WIDTH), 0)
    lane = lax.broadcasted_iota(jnp.int32, (ROWS, WIDTH), 1)
    return jnp.where(lane == row + z * ROWS, 1.0, 0.0).astype(BF16)


def mend_kernel(fa, fb, fc, windows_in, hid_in, taps, bias, windows, hid, positions):
    z, d = lax.axis_index("seq"), lax.axis_index("dp")
    fill_positions(positions, z, ((fa, 3), (fb, 1), (fc, 2)))
    windows[...] = windows_in[...]
    hid[...] = hid_in[...]
    first = jnp.clip(lax.rem(z + 2, SEQ) * TOK - EDGE, 0, LEN - TOK - 2 * EDGE)
    first = pl.multiple_of(first, EDGE)
    fresh = pl.ds(first, TOK + 2 * EDGE)
    for g in range(CIN // 128):
        for k in range(6):
            at = k * CIN + g * 128
            spots = pl.ds(2 * first + (6 + k), TOK + 2 * EDGE, stride=2)
            windows[fresh, at : at + 128] = positions[g, spots, :].astype(BF16)
    hid[fresh, :] = filtered_half(windows[fresh, :], taps, half_of(bias, d // 2))


def project_kernel(windows, hid_near, w2, w3, bias, gain, aw, hid, normed, proj, normed_t, taps):
    z, d = lax.axis_index("seq"), lax.axis_index("dp")
    side, half = d // 2, WIDTH // 2
    put_shards(taps, w2, w3, lax.rem(d, 2))
    hid[side] = hid_near[...]
    hid[1 - side] = filtered_half(windows, taps, half_of(bias, 1 - side))
    low, high = hid[0].astype(F32), hid[1].astype(F32)
    square = jnp.sum(low * low, axis=1, keepdims=True) + jnp.sum(high * high, axis=1, keepdims=True)
    inv = lax.rsqrt(square * (1.0 / WIDTH) + 1e-06)
    scales = gain[...].reshape(1, WIDTH)
    normed[:, :half] = (low * inv * scales[:, :half]).astype(BF16)
    normed[:, half:] = (high * inv * scales[:, half:]).astype(BF16)
    proj[...] = mm(normed[...], aw[...]).astype(BF16)
    normed_t[...] = mm(row_picker(z), normed[...], NT).astype(BF16)


def heads_of(proj, h):
    q = proj[:, h * KEY_DIM : (h + 1) * KEY_DIM]
    k = proj[:, QW + h * KEY_DIM : QW + (h + 1) * KEY_DIM]
    v = proj[:, 2 * QW + h * VAL_DIM : 2 * QW + (h + 1) * VAL_DIM]
    return q, k, v


def attend_kernel(proj, probs_t, att_t):
    for h in range(HEADS):
        q, k, v = heads_of(proj, h)
        scores = mm(k, q, NT) * SCALE
        top = jnp.max(scores, axis=0, keepdims=True)
        weight = jnp.exp(scores - top)
        total = jnp.sum(weight, axis=0, keepdims=True)
        probs = (weight * (1.0 / total)).astype(BF16)
        probs_t[h] = probs
        att_t[h * VAL_DIM : (h + 1) * VAL_DIM, :] = mm(v, probs, TN).astype(BF16)


def outputs_kernel(hid, att_t, ow, outputs):
    z = lax.axis_index("seq")
    half = WIDTH // 2
    for at in range(SEQ):

        @pl.when(z == at)
        def _():
            rows = slice(at * TOK, (at + 1) * TOK)
            branch = mm(att_t[:, rows], ow[...], (((0,), (1,)), ((), ())))
            outputs[:, :half] = branch[:, :half] + hid[0, rows, :].astype(F32)
            outputs[:, half:] = branch[:, half:] + hid[1, rows, :].astype(F32)


def both_ways(write, keep, send, core):
    for at in range(2):

        @pl.when(core == at)
        def _():
            write(keep, at)
            write(send, 1 - at)


def value_kernel(c0, ca, cb, cc, normed_t, probs_t, att_t, aw, ow, grad, keep, send, mixed, cot, cot_t, d_value):
    z, d = lax.axis_index("seq"), lax.axis_index("dp")
    for ref, off in ((c0, 0), (ca, 3), (cb, 1), (cc, 2)):
        start = pl.multiple_of(lax.rem(z + off, SEQ) * TOK, TOK)
        cot[pl.ds(start, TOK), :] = ref[...]
    cot_t[...] = mm(row_picker(z), cot[...], NT).astype(BF16)
    grad[...] = mm(cot[...], ow[...]).astype(BF16)
    out_part = mm(cot_t[...], att_t[...], NT)
    for h in range(HEADS):
        lanes = slice(h * VAL_DIM, (h + 1) * VAL_DIM)
        d_value[:, lanes] = mm(probs_t[h], grad[:, lanes]).astype(BF16)
    value_part = mm(normed_t[...], d_value[...])
    here = pl.multiple_of(z * ROWS, ROWS)
    total = jnp.sum(value_part * aw[pl.ds(here, ROWS), 2 * QW :].astype(F32), axis=1, keepdims=True)
    mixed[...] = jnp.broadcast_to(total, (ROWS, 128))
    half = VW // 2

    def write(ref, side):
        lanes = slice(side * half, (side + 1) * half)
        ref[:, :half] = value_part[:, lanes].astype(ref.dtype)
        ref[:, half:] = out_part[:, lanes].astype(ref.dtype)

    both_ways(write, keep, send, lax.rem(d, 2))


def score_grads(grad, proj, probs_t, d_query, d_key, first):
    for h in range(first, first + HEADS // 2):
        q, k, v = heads_of(proj, h)
        probs = probs_t[h].astype(F32)
        product = mm(v, grad[:, h * VAL_DIM : (h + 1) * VAL_DIM], NT) * probs
        delta = jnp.sum(product, axis=0, keepdims=True)
        dscore = (product - probs * delta).astype(BF16)
        lanes = slice((h - first) * KEY_DIM, (h - first + 1) * KEY_DIM)
        d_query[lanes, :] = (mm(k, dscore, TN) * SCALE).astype(BF16)
        d_key[:, lanes] = (mm(dscore, q) * SCALE).astype(BF16)


def early_key_kernel(grad, proj, probs_t, d_query, d_key):
    score_grads(grad, proj, probs_t, d_query, d_key, 0)


def late_key_kernel(
    grad, proj, probs_t, query_early, key_early, normed_t, mixed, gain, aw, keep, send, d_query, d_key
):
    z, d = lax.axis_index("seq"), lax.axis_index("dp")
    score_grads(grad, proj, probs_t, d_query, d_key, HEADS // 2)
    left = normed_t[...]
    query_part = jnp.concatenate([mm(left, query_early[...], NT), mm(left, d_query[...], NT)], axis=1)
    key_part = jnp.concatenate([mm(left, key_early[...]), mm(left, d_key[...])], axis=1)
    here = pl.multiple_of(z * ROWS, ROWS)
    total = query_part * aw[pl.ds(here, ROWS), :QW].astype(F32)
    total = total + key_part * aw[pl.ds(here, ROWS), QW : 2 * QW].astype(F32)
    total = mixed[...] + jnp.sum(total, axis=1, keepdims=True)
    scales = gain[...].reshape(1, WIDTH)
    mine = scales[:, :ROWS]
    for at in range(1, SEQ):
        mine = jnp.where(z == at, scales[:, at * ROWS : (at + 1) * ROWS], mine)
    gain_part = total.T[0:1, :] / mine

    def write(ref, side):
        ref[:ROWS, :] = (key_part if side else query_part).astype(ref.dtype)
        ref[ROWS:, :] = jnp.zeros((16, QW), ref.dtype)
        ref[ROWS : ROWS + 1, :ROWS] = gain_part.astype(ref.dtype)

    both_ways(write, keep, send, lax.rem(d, 2))


def finish_kernel(whole_v, whole_k, other_v, other_k, grad_attend, grad_output, grad_gain):
    half = VW // 2

    def place(source, side):
        lanes = slice(side * half, (side + 1) * half)
        grad_attend[:, 2 * QW + side * half : 2 * QW + (side + 1) * half] = source[:, :half].astype(F32)
        grad_output[:, lanes] = source[:, half:].astype(F32)

    for at in range(2):

        @pl.when(lax.rem(lax.axis_index("dp"), 2) == at)
        def _():
            place(whole_v, at)
            place(other_v, 1 - at)
            low, high = (whole_k, other_k) if at == 0 else (other_k, whole_k)
            grad_attend[:, :QW] = low[:ROWS, :].astype(F32)
            grad_attend[:, QW : 2 * QW] = high[:ROWS, :].astype(F32)
            grad_gain[...] = low[ROWS : ROWS + 8, :ROWS].astype(F32)[0]


def kernel_call(body, outs, scratch, flops, *args, far=()):
    whole = pl.BlockSpec(memory_space=pltpu.VMEM)
    away = pl.BlockSpec(memory_space=pltpu.HBM)
    sems = [pltpu.SemaphoreType.DMA((len(far),))] if far else []
    return pl.pallas_call(
        body,
        in_specs=[away if i in far else whole for i in range(len(args))],
        out_shape=[jax.ShapeDtypeStruct(s, t) for s, t in outs],
        scratch_shapes=[pltpu.VMEM(s, t) for s, t in scratch] + sems,
        compiler_params=pltpu.CompilerParams(vmem_limit_bytes=40 << 20),
        cost_estimate=pl.CostEstimate(flops=flops, bytes_accessed=1 << 16, transcendentals=0),
    )(*args)


def combined(keep, arrived):
    return (keep.astype(F32) + arrived.astype(F32)).astype(BF16)


def per_device_fast(
    dna_features, filter_weight, filter_bias, norm_gain, attend_weight, output_weight, cotangent
):
    f0, c0 = dna_features[0], cotangent[0]
    w0 = filter_weight.transpose(0, 2, 1).reshape(5 * SHARD, CIN)
    half = WIDTH // 2
    w2 = swap(w0, 2)
    w1 = swap(w0, 1)
    fa, fb = ring(f0, 1), ring(f0, SEQ - 1)
    (taps,) = kernel_call(
        taps_kernel,
        [((2 * SHARD, 5 * CIN), BF16)],
        [((5 * SHARD, CIN), BF16)],
        1 << 31,
        pltpu.with_memory_space_constraint(w0, pltpu.HBM), w1,
        far=(0,),
    )
    ca = ring(c0, 1)
    far_a, taps = lax.optimization_barrier((fa, taps))
    to_left, far_a, fb = lax.optimization_barrier((c0, far_a, fb))
    fc = ring(far_a, 1)
    windows, hid_near = kernel_call(
        near_kernel,
        [((LEN, 6 * CIN), BF16), ((LEN, half), BF16)],
        [((CIN // 128, 16 + 2 * LEN, 128), F32)],
        1 << 24,
        f0, fa, fb, taps, filter_bias,
    )
    ca, windows = lax.optimization_barrier((ca, windows))
    cb, cc = ring(to_left, SEQ - 1), ring(ca, 1)
    w2, fc, windows = lax.optimization_barrier((w2, fc, windows))
    w3 = swap(w2, 1)
    windows, hid_near = kernel_call(
        mend_kernel,
        [((LEN, 6 * CIN), BF16), ((LEN, half), BF16)],
        [((CIN // 128, 16 + 2 * LEN, 128), F32)],
        1 << 33,
        fa, fb, fc, windows, hid_near, taps, filter_bias,
    )
    hid, normed, proj, normed_t = kernel_call(
        project_kernel,
        [((2, LEN, half), BF16), ((LEN, WIDTH), BF16), ((LEN, PROJ), BF16), ((ROWS, LEN), BF16)],
        [((2 * SHARD, 5 * CIN), BF16)],
        1 << 33,
        windows, hid_near, w2, w3, filter_bias, norm_gain, attend_weight,
    )
    probs_t, att_t = kernel_call(
        attend_kernel,
        [((HEADS, LEN, LEN), BF16), ((VW, LEN), BF16)],
        [],
        1 << 33,
        proj,
    )
    (outputs,) = kernel_call(
        outputs_kernel, [((TOK, WIDTH), F32)], [], 1 << 16, hid, att_t, output_weight
    )
    grad, keep_v, send_v, mixed = kernel_call(
        value_kernel,
        [((LEN, VW), BF16), ((ROWS, VW), F32), ((ROWS, VW), BF16), ((ROWS, 128), F32)],
        [((LEN, WIDTH), BF16), ((ROWS, LEN), BF16), ((LEN, VW), BF16)],
        1 << 29,
        c0, ca, cb, cc, normed_t, probs_t, att_t, attend_weight, output_weight,
    )
    query_early, key_early = kernel_call(
        early_key_kernel,
        [((QW // 2, LEN), BF16), ((LEN, QW // 2), BF16)],
        [],
        1 << 24,
        grad, proj, probs_t,
    )
    part_v = combined(keep_v, swap(send_v, 1))
    part_v, query_early = lax.optimization_barrier((part_v, query_early))
    keep_k, send_k = kernel_call(
        late_key_kernel,
        [((ROWS + 16, QW), F32), ((ROWS + 16, QW), BF16)],
        [((QW // 2, LEN), BF16), ((LEN, QW // 2), BF16)],
        1 << 33,
        grad, proj, probs_t, query_early, key_early, normed_t, mixed, norm_gain, attend_weight,
    )
    arrived_v = swap(part_v, 2)
    part_k = combined(keep_k, swap(send_k, 1))
    arrived_k = swap(part_k, 2)
    whole_v, whole_k = combined(part_v, arrived_v), combined(part_k, arrived_k)
    other_v, other_k = swap(whole_v, 1), swap(whole_k, 1)
    grad_attend, grad_output, grad_gain = kernel_call(
        finish_kernel,
        [((ROWS, PROJ), F32), ((ROWS, WIDTH), F32), ((ROWS,), F32)],
        [],
        1 << 31,
        whole_v, whole_k, other_v, other_k,
    )
    return outputs[None], grad_attend, grad_output, grad_gain


def solution(mesh):
    small = mesh.shape["seq"] == SEQ and mesh.shape["dp"] == DP
    return jax.shard_map(
        per_device_fast if small else per_device,
        mesh=mesh,
        in_specs=(
            P(("groups", "dp"), "seq", None),
            P(None, None, "dp"),
            P(),
            P(),
            P(),
            P(),
            P(("groups", "dp"), "seq", None),
        ),
        out_specs=(
            P(("groups", "dp"), "seq", None),
            P(("groups", "seq"), None),
            P(("groups", "seq"), None),
            P(("groups", "seq")),
        ),
        check_vma=False,
    )
```

```python
import functools

import jax
import jax.numpy as jnp
from jax import lax
from jax.experimental import pallas as pl
from jax.experimental.pallas import tpu as pltpu
from jax.sharding import PartitionSpec as P

HEADS = 4
KEY_DIM = 64
VAL_DIM = 192


def extended(value, sides, width):
    for axis, dim in sides:
        devices, length = (lax.axis_size(axis), value.shape[dim])
        up = [(i, (i + 1) % devices) for i in range(devices - 1)]
        down = [(j, i) for i, j in up]
        last = lax.slice_in_dim(value, length - width, length, axis=dim)
        first = lax.slice_in_dim(value, 0, width, axis=dim)
        before = lax.ppermute(last, axis, up)
        after = lax.ppermute(first, axis, down)
        value = jnp.concatenate([before, value, after], axis=dim)
    return value


def filter_block(padded, weights, bias_part):
    count = padded.shape[1] - 4
    total = bias_part
    for offset in range(5):
        total = total + jnp.einsum(
            "spc,co->spo",
            padded[:, offset : offset + count],
            weights[offset],
            preferred_element_type=jnp.float32,
        )
    activ = jax.nn.gelu(total, approximate=True)
    activ = activ.reshape(activ.shape[0], count // 2, 2, activ.shape[2])
    return (0.5 * (activ[:, :, 0] + activ[:, :, 1])).astype(jnp.bfloat16)


def per_device(
    dna_features, filter_weight, filter_bias, norm_gain, attend_weight, output_weight, cotangent
):
    padded = extended(dna_features, (("seq", 1),), 2)
    hidden = filter_block(
        padded, lax.all_gather(filter_weight, "dp", axis=2, tiled=True), filter_bias
    )
    hidden = hidden[0]
    widen = hidden.astype(jnp.float32)
    nhat = widen * lax.rsqrt(jnp.mean(widen * widen, axis=-1, keepdims=True) + 1e-06)
    normed = (nhat * norm_gain).astype(jnp.bfloat16)
    tokens = normed.shape[0]
    query_width = HEADS * KEY_DIM
    value_width = HEADS * VAL_DIM
    scale = KEY_DIM ** (-0.5)
    projected = jnp.dot(normed, attend_weight, preferred_element_type=jnp.float32).astype(
        jnp.bfloat16
    )
    queries = projected[:, :query_width]
    keys_local = projected[:, query_width : 2 * query_width]
    values_local = projected[:, 2 * query_width :]
    keys_all, values_all = (
        lax.all_gather(keys_local, "seq", axis=0, tiled=True),
        lax.all_gather(values_local, "seq", axis=0, tiled=True),
    )
    total_len = keys_all.shape[0]
    query_heads = queries.reshape(tokens, HEADS, KEY_DIM)
    key_heads = keys_all.reshape(total_len, HEADS, KEY_DIM)
    value_heads = values_all.reshape(total_len, HEADS, VAL_DIM)
    scores = (
        jnp.einsum("qhd,khd->hqk", query_heads, key_heads, preferred_element_type=jnp.float32)
        * scale
    )
    peak = jnp.max(scores, axis=-1, keepdims=True)
    logsum = peak + jnp.log(jnp.sum(jnp.exp(scores - peak), axis=-1, keepdims=True))
    probs = jnp.exp(scores - logsum)
    probs_b = probs.astype(jnp.bfloat16)
    attended = (
        jnp.einsum("hqk,khd->qhd", probs_b, value_heads, preferred_element_type=jnp.float32)
        .astype(jnp.bfloat16)
        .reshape(tokens, value_width)
    )
    branch = lax.dot_general(
        attended, output_weight, (((1,), (1,)), ((), ())), preferred_element_type=jnp.float32
    )
    outputs = widen + branch
    upstream = cotangent[0]
    output_part = lax.dot_general(
        upstream, attended, (((0,), (0,)), ((), ())), preferred_element_type=jnp.float32
    )
    d_attn = jnp.dot(upstream, output_weight, preferred_element_type=jnp.float32).astype(
        jnp.bfloat16
    )
    d_heads = d_attn.reshape(tokens, HEADS, VAL_DIM)
    attn_heads = attended.reshape(tokens, HEADS, VAL_DIM)
    delta = jnp.sum(d_heads.astype(jnp.float32) * attn_heads.astype(jnp.float32), axis=-1)
    dprob = jnp.einsum("qhd,khd->hqk", d_heads, value_heads, preferred_element_type=jnp.float32)
    dscore = (probs * (dprob - delta.T[:, :, None])).astype(jnp.bfloat16)
    d_query = (
        jnp.einsum("hqk,khd->qhd", dscore, key_heads, preferred_element_type=jnp.float32) * scale
    )
    logsum_rows = logsum[:, :, 0].T
    logsum_all, delta_all = (
        lax.all_gather(logsum_rows, "seq", axis=0, tiled=True),
        lax.all_gather(delta, "seq", axis=0, tiled=True),
    )
    key_heads_local = keys_local.reshape(tokens, HEADS, KEY_DIM)
    value_heads_local = values_local.reshape(tokens, HEADS, VAL_DIM)
    piece_query = lax.all_gather(queries, "seq", axis=0, tiled=True)
    piece_grad = lax.all_gather(d_attn, "seq", axis=0, tiled=True)
    count = piece_query.shape[0]
    piece_qheads = piece_query.reshape(count, HEADS, KEY_DIM)
    piece_gheads = piece_grad.reshape(count, HEADS, VAL_DIM)
    piece_scores = (
        jnp.einsum(
            "qhd,khd->hqk", piece_qheads, key_heads_local, preferred_element_type=jnp.float32
        )
        * scale
    )
    piece_probs = jnp.exp(piece_scores - logsum_all.T[:, :, None])
    piece_probs_b = piece_probs.astype(jnp.bfloat16)
    piece_dprob = jnp.einsum(
        "qhd,khd->hqk", piece_gheads, value_heads_local, preferred_element_type=jnp.float32
    )
    piece_dscore = (piece_probs * (piece_dprob - delta_all.T[:, :, None])).astype(jnp.bfloat16)
    grad_keys = jnp.einsum(
        "hqk,qhd->khd", piece_dscore, piece_qheads, preferred_element_type=jnp.float32
    )
    grad_values = jnp.einsum(
        "hqk,qhd->khd", piece_probs_b, piece_gheads, preferred_element_type=jnp.float32
    )
    grad_keys, grad_values = (grad_keys, grad_values)
    d_proj = jnp.concatenate(
        [
            d_query.reshape(tokens, query_width),
            (grad_keys * scale).reshape(tokens, query_width),
            grad_values.reshape(tokens, value_width),
        ],
        axis=1,
    ).astype(jnp.bfloat16)
    d_normed = lax.dot_general(
        d_proj, attend_weight, (((1,), (1,)), ((), ())), preferred_element_type=jnp.float32
    )
    attend_part = lax.dot_general(
        normed, d_proj, (((0,), (0,)), ((), ())), preferred_element_type=jnp.float32
    )
    gain_part = jnp.sum(d_normed * nhat, axis=0)
    attend_share, output_share, gain_share = (
        lax.psum_scatter(
            attend_part.astype(jnp.bfloat16), "seq", scatter_dimension=0, tiled=True
        ).astype(jnp.float32),
        lax.psum_scatter(
            output_part.astype(jnp.bfloat16), "seq", scatter_dimension=0, tiled=True
        ).astype(jnp.float32),
        lax.psum_scatter(
            gain_part.astype(jnp.bfloat16), "seq", scatter_dimension=0, tiled=True
        ).astype(jnp.float32),
    )
    grad_attend, grad_output, grad_gain = lax.psum((attend_share, output_share, gain_share), "dp")
    return (outputs[None], grad_attend, grad_output, grad_gain)


F32, BF16 = jnp.float32, jnp.bfloat16
SEQ, DP = 4, 4
TOK = 128
EDGE = 16
LEN = SEQ * TOK
CIN, WIDTH = 384, 768
SHARD = WIDTH // DP
ROWS = WIDTH // SEQ
QW, VW = HEADS * KEY_DIM, HEADS * VAL_DIM
PROJ = 2 * QW + VW
SCALE = KEY_DIM**-0.5
NN = (((1,), (0,)), ((), ()))
NT = (((1,), (1,)), ((), ()))
TN = (((0,), (0,)), ((), ()))


def mm(left, right, dims=NN):
    return lax.dot_general(left, right, dims, preferred_element_type=F32)


def half_gelu(value):
    inner = 0.7978845608028654 * (value + 0.044715 * value * value * value)
    return 0.5 * value * (1.0 + jnp.tanh(inner))


def ring(value, step):
    return lax.ppermute(value, "seq", [(i, (i + step) % SEQ) for i in range(SEQ)])


def swap(value, bit):
    return lax.ppermute(value, "dp", [(i, i ^ bit) for i in range(DP)])


def put_shards(taps, mine, other, core):
    for tap in range(5):
        lanes = slice(tap * CIN, (tap + 1) * CIN)
        rows = slice(tap * SHARD, (tap + 1) * SHARD)
        taps[pl.ds(core * SHARD, SHARD), lanes] = mine[rows, :]
        taps[pl.ds((1 - core) * SHARD, SHARD), lanes] = other[rows, :]


def half_of(bias, side):
    both = bias[...].reshape(1, WIDTH)
    return jnp.where(side == 0, both[:, : WIDTH // 2], both[:, WIDTH // 2 :])


def filtered_half(windows, taps, bias):
    even = mm(windows[:, : 5 * CIN], taps[...], NT) + bias
    odd = mm(windows[:, CIN:], taps[...], NT) + bias
    return (0.5 * (half_gelu(even) + half_gelu(odd))).astype(BF16)


def taps_kernel(w0_far, w1, taps, w0, sems):
    load = pltpu.make_async_copy(w0_far, w0, sems.at[0])
    load.start()
    load.wait()
    put_shards(taps, w0, w1, lax.rem(lax.axis_index("dp"), 2))


def fill_positions(positions, z, parts):
    chunk = 2 * TOK
    for g in range(CIN // 128):
        positions[g, 0:8, :] = jnp.zeros((8, 128), F32)
        positions[g, 8 + 2 * LEN :, :] = jnp.zeros((8, 128), F32)
        for ref, off in parts:
            start = pl.multiple_of(lax.rem(z + off, SEQ) * chunk + 8, 8)
            if ref is None:
                positions[g, pl.ds(start, chunk), :] = jnp.zeros((chunk, 128), F32)
            else:
                positions[g, pl.ds(start, chunk), :] = ref[:, g * 128 : (g + 1) * 128].astype(F32)


def near_kernel(f0, fa, fb, taps, bias, windows, hid, positions):
    z, d = lax.axis_index("seq"), lax.axis_index("dp")
    fill_positions(positions, z, ((f0, 0), (fa, 3), (fb, 1), (None, 2)))
    for g in range(CIN // 128):
        for k in range(6):
            at = k * CIN + g * 128
            windows[:, at : at + 128] = positions[g, pl.ds(6 + k, LEN, stride=2), :].astype(BF16)
    hid[...] = filtered_half(windows, taps, half_of(bias, d // 2))


def row_picker(z):
    row = lax.broadcasted_iota(jnp.int32, (ROWS, WIDTH), 0)
    lane = lax.broadcasted_iota(jnp.int32, (ROWS, WIDTH), 1)
    return jnp.where(lane == row + z * ROWS, 1.0, 0.0).astype(BF16)


def mend_kernel(fa, fb, fc, windows_in, hid_in, taps, bias, windows, hid, positions):
    z, d = lax.axis_index("seq"), lax.axis_index("dp")
    fill_positions(positions, z, ((fa, 3), (fb, 1), (fc, 2)))
    windows[...] = windows_in[...]
    hid[...] = hid_in[...]
    first = jnp.clip(lax.rem(z + 2, SEQ) * TOK - EDGE, 0, LEN - TOK - 2 * EDGE)
    first = pl.multiple_of(first, EDGE)
    fresh = pl.ds(first, TOK + 2 * EDGE)
    for g in range(CIN // 128):
        for k in range(6):
            at = k * CIN + g * 128
            spots = pl.ds(2 * first + (6 + k), TOK + 2 * EDGE, stride=2)
            windows[fresh, at : at + 128] = positions[g, spots, :].astype(BF16)
    hid[fresh, :] = filtered_half(windows[fresh, :], taps, half_of(bias, d // 2))


def project_kernel(windows, hid_near, w2, w3, bias, gain, aw, hid, normed, proj, normed_t, taps):
    z, d = lax.axis_index("seq"), lax.axis_index("dp")
    side, half = d // 2, WIDTH // 2
    put_shards(taps, w2, w3, lax.rem(d, 2))
    hid[side] = hid_near[...]
    hid[1 - side] = filtered_half(windows, taps, half_of(bias, 1 - side))
    low, high = hid[0].astype(F32), hid[1].astype(F32)
    square = jnp.sum(low * low, axis=1, keepdims=True) + jnp.sum(high * high, axis=1, keepdims=True)
    inv = lax.rsqrt(square * (1.0 / WIDTH) + 1e-06)
    scales = gain[...].reshape(1, WIDTH)
    normed[:, :half] = (low * inv * scales[:, :half]).astype(BF16)
    normed[:, half:] = (high * inv * scales[:, half:]).astype(BF16)
    proj[...] = mm(normed[...], aw[...]).astype(BF16)
    normed_t[...] = mm(row_picker(z), normed[...], NT).astype(BF16)


def heads_of(proj, h):
    q = proj[:, h * KEY_DIM : (h + 1) * KEY_DIM]
    k = proj[:, QW + h * KEY_DIM : QW + (h + 1) * KEY_DIM]
    v = proj[:, 2 * QW + h * VAL_DIM : 2 * QW + (h + 1) * VAL_DIM]
    return q, k, v


def attend_kernel(proj, probs_t, att_t):
    for h in range(HEADS):
        q, k, v = heads_of(proj, h)
        scores = mm(k, q, NT) * SCALE
        top = jnp.max(scores, axis=0, keepdims=True)
        weight = jnp.exp(scores - top)
        total = jnp.sum(weight, axis=0, keepdims=True)
        probs = (weight * (1.0 / total)).astype(BF16)
        probs_t[h] = probs
        att_t[h * VAL_DIM : (h + 1) * VAL_DIM, :] = mm(v, probs, TN).astype(BF16)


def outputs_kernel(hid, att_t, ow, outputs):
    z = lax.axis_index("seq")
    half = WIDTH // 2
    for at in range(SEQ):

        @pl.when(z == at)
        def _():
            rows = slice(at * TOK, (at + 1) * TOK)
            branch = mm(att_t[:, rows], ow[...], (((0,), (1,)), ((), ())))
            outputs[:, :half] = branch[:, :half] + hid[0, rows, :].astype(F32)
            outputs[:, half:] = branch[:, half:] + hid[1, rows, :].astype(F32)


def both_ways(write, keep, send, core):
    for at in range(2):

        @pl.when(core == at)
        def _():
            write(keep, at)
            write(send, 1 - at)


def value_kernel(c0, ca, cb, cc, normed_t, probs_t, att_t, aw, ow, grad, keep, send, mixed, cot, cot_t, d_value):
    z, d = lax.axis_index("seq"), lax.axis_index("dp")
    for ref, off in ((c0, 0), (ca, 3), (cb, 1), (cc, 2)):
        start = pl.multiple_of(lax.rem(z + off, SEQ) * TOK, TOK)
        cot[pl.ds(start, TOK), :] = ref[...]
    cot_t[...] = mm(row_picker(z), cot[...], NT).astype(BF16)
    grad[...] = mm(cot[...], ow[...]).astype(BF16)
    out_part = mm(cot_t[...], att_t[...], NT)
    for h in range(HEADS):
        lanes = slice(h * VAL_DIM, (h + 1) * VAL_DIM)
        d_value[:, lanes] = mm(probs_t[h], grad[:, lanes]).astype(BF16)
    value_part = mm(normed_t[...], d_value[...])
    here = pl.multiple_of(z * ROWS, ROWS)
    total = jnp.sum(value_part * aw[pl.ds(here, ROWS), 2 * QW :].astype(F32), axis=1, keepdims=True)
    mixed[...] = jnp.broadcast_to(total, (ROWS, 128))
    half = VW // 2

    def write(ref, side):
        lanes = slice(side * half, (side + 1) * half)
        ref[:, :half] = value_part[:, lanes].astype(ref.dtype)
        ref[:, half:] = out_part[:, lanes].astype(ref.dtype)

    both_ways(write, keep, send, lax.rem(d, 2))


def score_grads(grad, proj, probs_t, d_query, d_key, first):
    for h in range(first, first + HEADS // 2):
        q, k, v = heads_of(proj, h)
        probs = probs_t[h].astype(F32)
        product = mm(v, grad[:, h * VAL_DIM : (h + 1) * VAL_DIM], NT) * probs
        delta = jnp.sum(product, axis=0, keepdims=True)
        dscore = (product - probs * delta).astype(BF16)
        lanes = slice((h - first) * KEY_DIM, (h - first + 1) * KEY_DIM)
        d_query[lanes, :] = (mm(k, dscore, TN) * SCALE).astype(BF16)
        d_key[:, lanes] = (mm(dscore, q) * SCALE).astype(BF16)


def early_key_kernel(grad, proj, probs_t, d_query, d_key):
    score_grads(grad, proj, probs_t, d_query, d_key, 0)


def late_key_kernel(
    grad, proj, probs_t, query_early, key_early, normed_t, mixed, gain, aw, keep, top, rest, d_query, d_key
):
    z, d = lax.axis_index("seq"), lax.axis_index("dp")
    score_grads(grad, proj, probs_t, d_query, d_key, HEADS // 2)
    left = normed_t[...]
    query_part = jnp.concatenate([mm(left, query_early[...], NT), mm(left, d_query[...], NT)], axis=1)
    key_part = jnp.concatenate([mm(left, key_early[...]), mm(left, d_key[...])], axis=1)
    here = pl.multiple_of(z * ROWS, ROWS)
    total = query_part * aw[pl.ds(here, ROWS), :QW].astype(F32)
    total = total + key_part * aw[pl.ds(here, ROWS), QW : 2 * QW].astype(F32)
    total = mixed[...] + jnp.sum(total, axis=1, keepdims=True)
    scales = gain[...].reshape(1, WIDTH)
    mine = scales[:, :ROWS]
    for at in range(1, SEQ):
        mine = jnp.where(z == at, scales[:, at * ROWS : (at + 1) * ROWS], mine)
    gain_part = total.T[0:1, :] / mine

    gain_rows = jnp.concatenate([gain_part, jnp.zeros((15, ROWS), F32)], axis=0)
    cut = ROWS // 2

    def part(side, rows):
        return (key_part if side else query_part)[rows, :]

    for at in range(2):

        @pl.when(lax.rem(d, 2) == at)
        def _():
            keep[:ROWS, :] = part(at, slice(0, ROWS))
            keep[ROWS:, :] = jnp.zeros((16, QW), F32)
            keep[ROWS:, :ROWS] = gain_rows
            top[...] = part(1 - at, slice(0, cut)).astype(BF16)
            rest[:cut, :] = part(1 - at, slice(cut, ROWS)).astype(BF16)
            rest[cut:, :] = jnp.zeros((16, QW), BF16)
            rest[cut:, :ROWS] = gain_rows.astype(BF16)


def finish_kernel(whole_v, whole_k, other_v, other_k, grad_attend, grad_output, grad_gain):
    half = VW // 2

    def place(source, side):
        lanes = slice(side * half, (side + 1) * half)
        grad_attend[:, 2 * QW + side * half : 2 * QW + (side + 1) * half] = source[:, :half].astype(F32)
        grad_output[:, lanes] = source[:, half:].astype(F32)

    for at in range(2):

        @pl.when(lax.rem(lax.axis_index("dp"), 2) == at)
        def _():
            place(whole_v, at)
            place(other_v, 1 - at)
            low, high = (whole_k, other_k) if at == 0 else (other_k, whole_k)
            grad_attend[:, :QW] = low[:ROWS, :].astype(F32)
            grad_attend[:, QW : 2 * QW] = high[:ROWS, :].astype(F32)
            grad_gain[...] = low[ROWS : ROWS + 8, :ROWS].astype(F32)[0]


def kernel_call(body, outs, scratch, flops, *args, far=()):
    whole = pl.BlockSpec(memory_space=pltpu.VMEM)
    away = pl.BlockSpec(memory_space=pltpu.HBM)
    sems = [pltpu.SemaphoreType.DMA((len(far),))] if far else []
    return pl.pallas_call(
        body,
        in_specs=[away if i in far else whole for i in range(len(args))],
        out_shape=[jax.ShapeDtypeStruct(s, t) for s, t in outs],
        scratch_shapes=[pltpu.VMEM(s, t) for s, t in scratch] + sems,
        compiler_params=pltpu.CompilerParams(vmem_limit_bytes=40 << 20),
        cost_estimate=pl.CostEstimate(flops=flops, bytes_accessed=1 << 16, transcendentals=0),
    )(*args)


def combined(keep, arrived):
    return (keep.astype(F32) + arrived.astype(F32)).astype(BF16)


def per_device_fast(
    dna_features, filter_weight, filter_bias, norm_gain, attend_weight, output_weight, cotangent
):
    f0, c0 = dna_features[0], cotangent[0]
    w0 = filter_weight.transpose(0, 2, 1).reshape(5 * SHARD, CIN)
    half = WIDTH // 2
    w2 = swap(w0, 2)
    w1 = swap(w0, 1)
    fa, fb = ring(f0, 1), ring(f0, SEQ - 1)
    (taps,) = kernel_call(
        taps_kernel,
        [((2 * SHARD, 5 * CIN), BF16)],
        [((5 * SHARD, CIN), BF16)],
        1 << 31,
        pltpu.with_memory_space_constraint(w0, pltpu.HBM), w1,
        far=(0,),
    )
    ca = ring(c0, 1)
    far_a, taps = lax.optimization_barrier((fa, taps))
    to_left, far_a, fb = lax.optimization_barrier((c0, far_a, fb))
    fc = ring(far_a, 1)
    windows, hid_near = kernel_call(
        near_kernel,
        [((LEN, 6 * CIN), BF16), ((LEN, half), BF16)],
        [((CIN // 128, 16 + 2 * LEN, 128), F32)],
        1 << 24,
        f0, fa, fb, taps, filter_bias,
    )
    ca, windows = lax.optimization_barrier((ca, windows))
    cb, cc = ring(to_left, SEQ - 1), ring(ca, 1)
    w2, fc, windows = lax.optimization_barrier((w2, fc, windows))
    w3 = swap(w2, 1)
    windows, hid_near = kernel_call(
        mend_kernel,
        [((LEN, 6 * CIN), BF16), ((LEN, half), BF16)],
        [((CIN // 128, 16 + 2 * LEN, 128), F32)],
        1 << 33,
        fa, fb, fc, windows, hid_near, taps, filter_bias,
    )
    hid, normed, proj, normed_t = kernel_call(
        project_kernel,
        [((2, LEN, half), BF16), ((LEN, WIDTH), BF16), ((LEN, PROJ), BF16), ((ROWS, LEN), BF16)],
        [((2 * SHARD, 5 * CIN), BF16)],
        1 << 33,
        windows, hid_near, w2, w3, filter_bias, norm_gain, attend_weight,
    )
    probs_t, att_t = kernel_call(
        attend_kernel,
        [((HEADS, LEN, LEN), BF16), ((VW, LEN), BF16)],
        [],
        1 << 33,
        proj,
    )
    (outputs,) = kernel_call(
        outputs_kernel, [((TOK, WIDTH), F32)], [], 1 << 16, hid, att_t, output_weight
    )
    grad, keep_v, send_v, mixed = kernel_call(
        value_kernel,
        [((LEN, VW), BF16), ((ROWS, VW), F32), ((ROWS, VW), BF16), ((ROWS, 128), F32)],
        [((LEN, WIDTH), BF16), ((ROWS, LEN), BF16), ((LEN, VW), BF16)],
        1 << 29,
        c0, ca, cb, cc, normed_t, probs_t, att_t, attend_weight, output_weight,
    )
    query_early, key_early = kernel_call(
        early_key_kernel,
        [((QW // 2, LEN), BF16), ((LEN, QW // 2), BF16)],
        [],
        1 << 24,
        grad, proj, probs_t,
    )
    part_v = combined(keep_v, swap(send_v, 1))
    part_v, query_early = lax.optimization_barrier((part_v, query_early))
    keep_k, top_k, rest_k = kernel_call(
        late_key_kernel,
        [((ROWS + 16, QW), F32), ((ROWS // 2, QW), BF16), ((ROWS // 2 + 16, QW), BF16)],
        [((QW // 2, LEN), BF16), ((LEN, QW // 2), BF16)],
        1 << 33,
        grad, proj, probs_t, query_early, key_early, normed_t, mixed, norm_gain, attend_weight,
    )
    arrived_v = swap(part_v, 2)
    arrived_v, outputs = lax.optimization_barrier((arrived_v, outputs))
    part_k = combined(keep_k, jnp.concatenate([swap(top_k, 1), swap(rest_k, 1)]))
    arrived_k = swap(part_k, 2)
    whole_v, whole_k = combined(part_v, arrived_v), combined(part_k, arrived_k)
    other_v, other_k = swap(whole_v, 1), swap(whole_k, 1)
    grad_attend, grad_output, grad_gain = kernel_call(
        finish_kernel,
        [((ROWS, PROJ), F32), ((ROWS, WIDTH), F32), ((ROWS,), F32)],
        [],
        1 << 31,
        whole_v, whole_k, other_v, other_k,
    )
    return outputs[None], grad_attend, grad_output, grad_gain


def solution(mesh):
    small = mesh.shape["seq"] == SEQ and mesh.shape["dp"] == DP
    return jax.shard_map(
        per_device_fast if small else per_device,
        mesh=mesh,
        in_specs=(
            P(("groups", "dp"), "seq", None),
            P(None, None, "dp"),
            P(),
            P(),
            P(),
            P(),
            P(("groups", "dp"), "seq", None),
        ),
        out_specs=(
            P(("groups", "dp"), "seq", None),
            P(("groups", "seq"), None),
            P(("groups", "seq"), None),
            P(("groups", "seq")),
        ),
        check_vma=False,
    )
```

```python
import functools

import jax
import jax.numpy as jnp
from jax import lax
from jax.experimental import pallas as pl
from jax.experimental.pallas import tpu as pltpu
from jax.sharding import PartitionSpec as P

HEADS = 4
KEY_DIM = 64
VAL_DIM = 192


def extended(value, sides, width):
    for axis, dim in sides:
        devices, length = (lax.axis_size(axis), value.shape[dim])
        up = [(i, (i + 1) % devices) for i in range(devices - 1)]
        down = [(j, i) for i, j in up]
        last = lax.slice_in_dim(value, length - width, length, axis=dim)
        first = lax.slice_in_dim(value, 0, width, axis=dim)
        before = lax.ppermute(last, axis, up)
        after = lax.ppermute(first, axis, down)
        value = jnp.concatenate([before, value, after], axis=dim)
    return value


def filter_block(padded, weights, bias_part):
    count = padded.shape[1] - 4
    total = bias_part
    for offset in range(5):
        total = total + jnp.einsum(
            "spc,co->spo",
            padded[:, offset : offset + count],
            weights[offset],
            preferred_element_type=jnp.float32,
        )
    activ = jax.nn.gelu(total, approximate=True)
    activ = activ.reshape(activ.shape[0], count // 2, 2, activ.shape[2])
    return (0.5 * (activ[:, :, 0] + activ[:, :, 1])).astype(jnp.bfloat16)


def per_device(
    dna_features, filter_weight, filter_bias, norm_gain, attend_weight, output_weight, cotangent
):
    padded = extended(dna_features, (("seq", 1),), 2)
    hidden = filter_block(
        padded, lax.all_gather(filter_weight, "dp", axis=2, tiled=True), filter_bias
    )
    hidden = hidden[0]
    widen = hidden.astype(jnp.float32)
    nhat = widen * lax.rsqrt(jnp.mean(widen * widen, axis=-1, keepdims=True) + 1e-06)
    normed = (nhat * norm_gain).astype(jnp.bfloat16)
    tokens = normed.shape[0]
    query_width = HEADS * KEY_DIM
    value_width = HEADS * VAL_DIM
    scale = KEY_DIM ** (-0.5)
    projected = jnp.dot(normed, attend_weight, preferred_element_type=jnp.float32).astype(
        jnp.bfloat16
    )
    queries = projected[:, :query_width]
    keys_local = projected[:, query_width : 2 * query_width]
    values_local = projected[:, 2 * query_width :]
    keys_all, values_all = (
        lax.all_gather(keys_local, "seq", axis=0, tiled=True),
        lax.all_gather(values_local, "seq", axis=0, tiled=True),
    )
    total_len = keys_all.shape[0]
    query_heads = queries.reshape(tokens, HEADS, KEY_DIM)
    key_heads = keys_all.reshape(total_len, HEADS, KEY_DIM)
    value_heads = values_all.reshape(total_len, HEADS, VAL_DIM)
    scores = (
        jnp.einsum("qhd,khd->hqk", query_heads, key_heads, preferred_element_type=jnp.float32)
        * scale
    )
    peak = jnp.max(scores, axis=-1, keepdims=True)
    logsum = peak + jnp.log(jnp.sum(jnp.exp(scores - peak), axis=-1, keepdims=True))
    probs = jnp.exp(scores - logsum)
    probs_b = probs.astype(jnp.bfloat16)
    attended = (
        jnp.einsum("hqk,khd->qhd", probs_b, value_heads, preferred_element_type=jnp.float32)
        .astype(jnp.bfloat16)
        .reshape(tokens, value_width)
    )
    branch = lax.dot_general(
        attended, output_weight, (((1,), (1,)), ((), ())), preferred_element_type=jnp.float32
    )
    outputs = widen + branch
    upstream = cotangent[0]
    output_part = lax.dot_general(
        upstream, attended, (((0,), (0,)), ((), ())), preferred_element_type=jnp.float32
    )
    d_attn = jnp.dot(upstream, output_weight, preferred_element_type=jnp.float32).astype(
        jnp.bfloat16
    )
    d_heads = d_attn.reshape(tokens, HEADS, VAL_DIM)
    attn_heads = attended.reshape(tokens, HEADS, VAL_DIM)
    delta = jnp.sum(d_heads.astype(jnp.float32) * attn_heads.astype(jnp.float32), axis=-1)
    dprob = jnp.einsum("qhd,khd->hqk", d_heads, value_heads, preferred_element_type=jnp.float32)
    dscore = (probs * (dprob - delta.T[:, :, None])).astype(jnp.bfloat16)
    d_query = (
        jnp.einsum("hqk,khd->qhd", dscore, key_heads, preferred_element_type=jnp.float32) * scale
    )
    logsum_rows = logsum[:, :, 0].T
    logsum_all, delta_all = (
        lax.all_gather(logsum_rows, "seq", axis=0, tiled=True),
        lax.all_gather(delta, "seq", axis=0, tiled=True),
    )
    key_heads_local = keys_local.reshape(tokens, HEADS, KEY_DIM)
    value_heads_local = values_local.reshape(tokens, HEADS, VAL_DIM)
    piece_query = lax.all_gather(queries, "seq", axis=0, tiled=True)
    piece_grad = lax.all_gather(d_attn, "seq", axis=0, tiled=True)
    count = piece_query.shape[0]
    piece_qheads = piece_query.reshape(count, HEADS, KEY_DIM)
    piece_gheads = piece_grad.reshape(count, HEADS, VAL_DIM)
    piece_scores = (
        jnp.einsum(
            "qhd,khd->hqk", piece_qheads, key_heads_local, preferred_element_type=jnp.float32
        )
        * scale
    )
    piece_probs = jnp.exp(piece_scores - logsum_all.T[:, :, None])
    piece_probs_b = piece_probs.astype(jnp.bfloat16)
    piece_dprob = jnp.einsum(
        "qhd,khd->hqk", piece_gheads, value_heads_local, preferred_element_type=jnp.float32
    )
    piece_dscore = (piece_probs * (piece_dprob - delta_all.T[:, :, None])).astype(jnp.bfloat16)
    grad_keys = jnp.einsum(
        "hqk,qhd->khd", piece_dscore, piece_qheads, preferred_element_type=jnp.float32
    )
    grad_values = jnp.einsum(
        "hqk,qhd->khd", piece_probs_b, piece_gheads, preferred_element_type=jnp.float32
    )
    grad_keys, grad_values = (grad_keys, grad_values)
    d_proj = jnp.concatenate(
        [
            d_query.reshape(tokens, query_width),
            (grad_keys * scale).reshape(tokens, query_width),
            grad_values.reshape(tokens, value_width),
        ],
        axis=1,
    ).astype(jnp.bfloat16)
    d_normed = lax.dot_general(
        d_proj, attend_weight, (((1,), (1,)), ((), ())), preferred_element_type=jnp.float32
    )
    attend_part = lax.dot_general(
        normed, d_proj, (((0,), (0,)), ((), ())), preferred_element_type=jnp.float32
    )
    gain_part = jnp.sum(d_normed * nhat, axis=0)
    attend_share, output_share, gain_share = (
        lax.psum_scatter(
            attend_part.astype(jnp.bfloat16), "seq", scatter_dimension=0, tiled=True
        ).astype(jnp.float32),
        lax.psum_scatter(
            output_part.astype(jnp.bfloat16), "seq", scatter_dimension=0, tiled=True
        ).astype(jnp.float32),
        lax.psum_scatter(
            gain_part.astype(jnp.bfloat16), "seq", scatter_dimension=0, tiled=True
        ).astype(jnp.float32),
    )
    grad_attend, grad_output, grad_gain = lax.psum((attend_share, output_share, gain_share), "dp")
    return (outputs[None], grad_attend, grad_output, grad_gain)


F32, BF16 = jnp.float32, jnp.bfloat16
SEQ, DP = 4, 4
TOK = 128
EDGE = 16
LEN = SEQ * TOK
CIN, WIDTH = 384, 768
SHARD = WIDTH // DP
ROWS = WIDTH // SEQ
QW, VW = HEADS * KEY_DIM, HEADS * VAL_DIM
PROJ = 2 * QW + VW
SCALE = KEY_DIM**-0.5
LOG2E = 1.4426950408889634
NN = (((1,), (0,)), ((), ()))
NT = (((1,), (1,)), ((), ()))
TN = (((0,), (0,)), ((), ()))


def mm(left, right, dims=NN):
    return lax.dot_general(left, right, dims, preferred_element_type=F32)


def half_gelu(value):
    inner = 0.7978845608028654 * (value + 0.044715 * value * value * value)
    return 0.5 * value * (1.0 + jnp.tanh(inner))


def ring(value, step):
    return lax.ppermute(value, "seq", [(i, (i + step) % SEQ) for i in range(SEQ)])


def swap(value, bit):
    return lax.ppermute(value, "dp", [(i, i ^ bit) for i in range(DP)])


def put_shards(taps, mine, other, core):
    for tap in range(5):
        lanes = slice(tap * CIN, (tap + 1) * CIN)
        rows = slice(tap * SHARD, (tap + 1) * SHARD)
        taps[pl.ds(core * SHARD, SHARD), lanes] = mine[rows, :]
        taps[pl.ds((1 - core) * SHARD, SHARD), lanes] = other[rows, :]


def put_shard(taps, shard):
    for tap in range(5):
        taps[:, tap * CIN : (tap + 1) * CIN] = shard[tap * SHARD : (tap + 1) * SHARD, :]


def shard_of(bias, index):
    every = bias[...].reshape(1, WIDTH)
    mine = every[:, :SHARD]
    for at in range(1, DP):
        mine = jnp.where(index == at, every[:, at * SHARD : (at + 1) * SHARD], mine)
    return mine


def half_of(bias, side):
    both = bias[...].reshape(1, WIDTH)
    return jnp.where(side == 0, both[:, : WIDTH // 2], both[:, WIDTH // 2 :])


def filtered_half(windows, taps, bias):
    even = mm(windows[:, : 5 * CIN], taps[...], NT) + bias
    odd = mm(windows[:, CIN:], taps[...], NT) + bias
    return (0.5 * (half_gelu(even) + half_gelu(odd))).astype(BF16)


def taps_kernel(w0_far, w1, taps, w0, sems):
    load = pltpu.make_async_copy(w0_far, w0, sems.at[0])
    load.start()
    load.wait()
    put_shards(taps, w0, w1, lax.rem(lax.axis_index("dp"), 2))


def fill_positions(positions, z, parts):
    chunk = 2 * TOK
    for g in range(CIN // 128):
        positions[g, 0:8, :] = jnp.zeros((8, 128), F32)
        positions[g, 8 + 2 * LEN :, :] = jnp.zeros((8, 128), F32)
        for ref, off in parts:
            start = pl.multiple_of(lax.rem(z + off, SEQ) * chunk + 8, 8)
            if ref is None:
                positions[g, pl.ds(start, chunk), :] = jnp.zeros((chunk, 128), F32)
            else:
                positions[g, pl.ds(start, chunk), :] = ref[:, g * 128 : (g + 1) * 128].astype(F32)


def near_kernel(f0, fa, fb, taps, bias, windows, hid, positions):
    z, d = lax.axis_index("seq"), lax.axis_index("dp")
    fill_positions(positions, z, ((f0, 0), (fa, 3), (fb, 1), (None, 2)))
    for g in range(CIN // 128):
        for k in range(6):
            at = k * CIN + g * 128
            windows[:, at : at + 128] = positions[g, pl.ds(6 + k, LEN, stride=2), :].astype(BF16)
    hid[...] = filtered_half(windows, taps, half_of(bias, d // 2))


def row_picker(z):
    row = lax.broadcasted_iota(jnp.int32, (ROWS, WIDTH), 0)
    lane = lax.broadcasted_iota(jnp.int32, (ROWS, WIDTH), 1)
    return jnp.where(lane == row + z * ROWS, 1.0, 0.0).astype(BF16)


def mend_kernel(
    fa, fb, fc, windows_in, hid_in, taps, w2, bias, windows, hid, hid_two, positions, two
):
    z, d = lax.axis_index("seq"), lax.axis_index("dp")
    fill_positions(positions, z, ((fa, 3), (fb, 1), (fc, 2)))
    windows[...] = windows_in[...]
    hid[...] = hid_in[...]
    first = jnp.clip(lax.rem(z + 2, SEQ) * TOK - EDGE, 0, LEN - TOK - 2 * EDGE)
    first = pl.multiple_of(first, EDGE)
    fresh = pl.ds(first, TOK + 2 * EDGE)
    for g in range(CIN // 128):
        for k in range(6):
            at = k * CIN + g * 128
            spots = pl.ds(2 * first + (6 + k), TOK + 2 * EDGE, stride=2)
            windows[fresh, at : at + 128] = positions[g, spots, :].astype(BF16)
    hid[fresh, :] = filtered_half(windows[fresh, :], taps, half_of(bias, d // 2))
    put_shard(two, w2)
    hid_two[...] = filtered_half(windows, two, shard_of(bias, lax.rem(d + 2, DP)))


def project_kernel(
    windows, hid_near, hid_two, w3, bias, gain, aw, hid, normed, proj, normed_t, three, far
):
    z, d = lax.axis_index("seq"), lax.axis_index("dp")
    side, core, half = d // 2, lax.rem(d, 2), WIDTH // 2
    put_shard(three, w3)
    hid[side] = hid_near[...]
    far[core] = hid_two[...]
    far[1 - core] = filtered_half(windows, three, shard_of(bias, 2 * (1 - side) + 1 - core))
    hid[1 - side] = jnp.concatenate([far[0], far[1]], axis=1)
    low, high = hid[0].astype(F32), hid[1].astype(F32)
    square = jnp.sum(low * low, axis=1, keepdims=True) + jnp.sum(high * high, axis=1, keepdims=True)
    inv = lax.rsqrt(square * (1.0 / WIDTH) + 1e-06)
    scales = gain[...].reshape(1, WIDTH)
    normed[:, :half] = (low * inv * scales[:, :half]).astype(BF16)
    normed[:, half:] = (high * inv * scales[:, half:]).astype(BF16)
    proj[...] = mm(normed[...], aw[...]).astype(BF16)
    normed_t[...] = mm(row_picker(z), normed[...], NT).astype(BF16)


def heads_of(proj, h):
    q = proj[:, h * KEY_DIM : (h + 1) * KEY_DIM]
    k = proj[:, QW + h * KEY_DIM : QW + (h + 1) * KEY_DIM]
    v = proj[:, 2 * QW + h * VAL_DIM : 2 * QW + (h + 1) * VAL_DIM]
    return q, k, v


def attend_kernel(proj, probs_t, att_t):
    for h in range(HEADS):
        q, k, v = heads_of(proj, h)
        scores = mm(k, q, NT) * (SCALE * LOG2E)
        top = jnp.max(scores, axis=0, keepdims=True)
        weight = jnp.exp2(scores - top)
        total = jnp.sum(weight, axis=0, keepdims=True)
        probs = (weight * (1.0 / total)).astype(BF16)
        probs_t[h] = probs
        att_t[h * VAL_DIM : (h + 1) * VAL_DIM, :] = mm(v, probs, TN).astype(BF16)


def outputs_kernel(hid, att_t, ow, outputs):
    z = lax.axis_index("seq")
    half = WIDTH // 2
    for at in range(SEQ):

        @pl.when(z == at)
        def _():
            rows = slice(at * TOK, (at + 1) * TOK)
            branch = mm(att_t[:, rows], ow[...], (((0,), (1,)), ((), ())))
            outputs[:, :half] = branch[:, :half] + hid[0, rows, :].astype(F32)
            outputs[:, half:] = branch[:, half:] + hid[1, rows, :].astype(F32)


def both_ways(write, keep, send, core):
    for at in range(2):

        @pl.when(core == at)
        def _():
            write(keep, at)
            write(send, 1 - at)


def value_kernel(c0, ca, cb, cc, normed_t, probs_t, att_t, aw, ow, grad, keep, send, mixed, cot, cot_t, d_value):
    z, d = lax.axis_index("seq"), lax.axis_index("dp")
    for ref, off in ((c0, 0), (ca, 3), (cb, 1), (cc, 2)):
        start = pl.multiple_of(lax.rem(z + off, SEQ) * TOK, TOK)
        cot[pl.ds(start, TOK), :] = ref[...]
    cot_t[...] = mm(row_picker(z), cot[...], NT).astype(BF16)
    grad[...] = mm(cot[...], ow[...]).astype(BF16)
    out_part = mm(cot_t[...], att_t[...], NT)
    for h in range(HEADS):
        lanes = slice(h * VAL_DIM, (h + 1) * VAL_DIM)
        d_value[:, lanes] = mm(probs_t[h], grad[:, lanes]).astype(BF16)
    value_part = mm(normed_t[...], d_value[...])
    here = pl.multiple_of(z * ROWS, ROWS)
    total = jnp.sum(value_part * aw[pl.ds(here, ROWS), 2 * QW :].astype(F32), axis=1, keepdims=True)
    mixed[...] = jnp.broadcast_to(total, (ROWS, 128))
    half = VW // 2

    def write(ref, side):
        lanes = slice(side * half, (side + 1) * half)
        ref[:, :half] = value_part[:, lanes].astype(ref.dtype)
        ref[:, half:] = out_part[:, lanes].astype(ref.dtype)

    both_ways(write, keep, send, lax.rem(d, 2))


def score_grads(grad, proj, probs_t, d_query, d_key, first):
    for h in range(first, first + HEADS // 2):
        q, k, v = heads_of(proj, h)
        probs = probs_t[h].astype(F32)
        product = mm(v, grad[:, h * VAL_DIM : (h + 1) * VAL_DIM], NT) * probs
        delta = jnp.sum(product, axis=0, keepdims=True)
        dscore = (product - probs * delta).astype(BF16)
        lanes = slice((h - first) * KEY_DIM, (h - first + 1) * KEY_DIM)
        d_query[lanes, :] = (mm(k, dscore, TN) * SCALE).astype(BF16)
        d_key[:, lanes] = (mm(dscore, q) * SCALE).astype(BF16)


def early_key_kernel(grad, proj, probs_t, d_query, d_key):
    score_grads(grad, proj, probs_t, d_query, d_key, 0)


def late_key_kernel(
    grad, proj, probs_t, query_early, key_early, normed_t, mixed, gain, aw, keep, top, rest, d_query, d_key
):
    z, d = lax.axis_index("seq"), lax.axis_index("dp")
    score_grads(grad, proj, probs_t, d_query, d_key, HEADS // 2)
    left = normed_t[...]
    query_part = jnp.concatenate([mm(left, query_early[...], NT), mm(left, d_query[...], NT)], axis=1)
    key_part = jnp.concatenate([mm(left, key_early[...]), mm(left, d_key[...])], axis=1)
    here = pl.multiple_of(z * ROWS, ROWS)
    total = query_part * aw[pl.ds(here, ROWS), :QW].astype(F32)
    total = total + key_part * aw[pl.ds(here, ROWS), QW : 2 * QW].astype(F32)
    total = mixed[...] + jnp.sum(total, axis=1, keepdims=True)
    scales = gain[...].reshape(1, WIDTH)
    mine = scales[:, :ROWS]
    for at in range(1, SEQ):
        mine = jnp.where(z == at, scales[:, at * ROWS : (at + 1) * ROWS], mine)
    gain_part = total.T[0:1, :] / mine

    gain_rows = jnp.concatenate([gain_part, jnp.zeros((15, ROWS), F32)], axis=0)
    cut = ROWS // 2

    def part(side, rows):
        return (key_part if side else query_part)[rows, :]

    for at in range(2):

        @pl.when(lax.rem(d, 2) == at)
        def _():
            keep[:ROWS, :] = part(at, slice(0, ROWS))
            keep[ROWS:, :] = jnp.zeros((16, QW), F32)
            keep[ROWS:, :ROWS] = gain_rows
            top[...] = part(1 - at, slice(0, cut)).astype(BF16)
            rest[:cut, :] = part(1 - at, slice(cut, ROWS)).astype(BF16)
            rest[cut:, :] = jnp.zeros((16, QW), BF16)
            rest[cut:, :ROWS] = gain_rows.astype(BF16)


def finish_output_kernel(whole_v, other_v, grad_output):
    half = VW // 2
    for at in range(2):

        @pl.when(lax.rem(lax.axis_index("dp"), 2) == at)
        def _():
            grad_output[:, at * half : (at + 1) * half] = whole_v[:, half:].astype(F32)
            grad_output[:, (1 - at) * half : (2 - at) * half] = other_v[:, half:].astype(F32)


def finish_attend_kernel(whole_v, other_v, whole_k, other_k, grad_attend, grad_gain):
    half, base = VW // 2, 2 * QW
    for at in range(2):

        @pl.when(lax.rem(lax.axis_index("dp"), 2) == at)
        def _():
            grad_attend[:, base + at * half : base + (at + 1) * half] = whole_v[:, :half].astype(F32)
            grad_attend[:, base + (1 - at) * half : base + (2 - at) * half] = other_v[:, :half].astype(F32)
            low, high = (whole_k, other_k) if at == 0 else (other_k, whole_k)
            grad_attend[:, :QW] = low[:ROWS, :].astype(F32)
            grad_attend[:, QW : 2 * QW] = high[:ROWS, :].astype(F32)
            grad_gain[...] = low[ROWS : ROWS + 8, :ROWS].astype(F32)[0]


def kernel_call(body, outs, scratch, flops, *args, far=()):
    whole = pl.BlockSpec(memory_space=pltpu.VMEM)
    away = pl.BlockSpec(memory_space=pltpu.HBM)
    sems = [pltpu.SemaphoreType.DMA((len(far),))] if far else []
    return pl.pallas_call(
        body,
        in_specs=[away if i in far else whole for i in range(len(args))],
        out_shape=[jax.ShapeDtypeStruct(s, t) for s, t in outs],
        scratch_shapes=[pltpu.VMEM(s, t) for s, t in scratch] + sems,
        compiler_params=pltpu.CompilerParams(vmem_limit_bytes=40 << 20),
        cost_estimate=pl.CostEstimate(flops=flops, bytes_accessed=1 << 16, transcendentals=0),
    )(*args)


def combined(keep, arrived):
    return (keep.astype(F32) + arrived.astype(F32)).astype(BF16)


def per_device_fast(
    dna_features, filter_weight, filter_bias, norm_gain, attend_weight, output_weight, cotangent
):
    f0, c0 = dna_features[0], cotangent[0]
    w0 = filter_weight.transpose(0, 2, 1).reshape(5 * SHARD, CIN)
    half = WIDTH // 2
    w2 = swap(w0, 2)
    w1 = swap(w0, 1)
    fa, fb = ring(f0, 1), ring(f0, SEQ - 1)
    (taps,) = kernel_call(
        taps_kernel,
        [((2 * SHARD, 5 * CIN), BF16)],
        [((5 * SHARD, CIN), BF16)],
        1 << 24,
        pltpu.with_memory_space_constraint(w0, pltpu.HBM), w1,
        far=(0,),
    )
    ca = ring(c0, 1)
    far_a, taps = lax.optimization_barrier((fa, taps))
    to_left, far_a, fb = lax.optimization_barrier((c0, far_a, fb))
    fc = ring(far_a, 1)
    windows, hid_near = kernel_call(
        near_kernel,
        [((LEN, 6 * CIN), BF16), ((LEN, half), BF16)],
        [((CIN // 128, 16 + 2 * LEN, 128), F32)],
        1 << 33,
        f0, fa, fb, taps, filter_bias,
    )
    ca, windows = lax.optimization_barrier((ca, windows))
    cb, cc = ring(to_left, SEQ - 1), ring(ca, 1)
    w2, fc, windows = lax.optimization_barrier((w2, fc, windows))
    w3 = swap(w2, 1)
    windows, hid_near, hid_two = kernel_call(
        mend_kernel,
        [((LEN, 6 * CIN), BF16), ((LEN, half), BF16), ((LEN, SHARD), BF16)],
        [((CIN // 128, 16 + 2 * LEN, 128), F32), ((SHARD, 5 * CIN), BF16)],
        1 << 33,
        fa, fb, fc, windows, hid_near, taps, w2, filter_bias,
    )
    hid, normed, proj, normed_t = kernel_call(
        project_kernel,
        [((2, LEN, half), BF16), ((LEN, WIDTH), BF16), ((LEN, PROJ), BF16), ((ROWS, LEN), BF16)],
        [((SHARD, 5 * CIN), BF16), ((2, LEN, SHARD), BF16)],
        1 << 24,
        windows, hid_near, hid_two, w3, filter_bias, norm_gain, attend_weight,
    )
    probs_t, att_t = kernel_call(
        attend_kernel,
        [((HEADS, LEN, LEN), BF16), ((VW, LEN), BF16)],
        [],
        1 << 29,
        proj,
    )
    (outputs,) = kernel_call(
        outputs_kernel, [((TOK, WIDTH), F32)], [], 1 << 33, hid, att_t, output_weight
    )
    grad, keep_v, send_v, mixed = kernel_call(
        value_kernel,
        [((LEN, VW), BF16), ((ROWS, VW), F32), ((ROWS, VW), BF16), ((ROWS, 128), F32)],
        [((LEN, WIDTH), BF16), ((ROWS, LEN), BF16), ((LEN, VW), BF16)],
        1 << 31,
        c0, ca, cb, cc, normed_t, probs_t, att_t, attend_weight, output_weight,
    )
    query_early, key_early = kernel_call(
        early_key_kernel,
        [((QW // 2, LEN), BF16), ((LEN, QW // 2), BF16)],
        [],
        1 << 33,
        grad, proj, probs_t,
    )
    part_v = combined(keep_v, swap(send_v, 1))
    part_v, query_early = lax.optimization_barrier((part_v, query_early))
    keep_k, top_k, rest_k = kernel_call(
        late_key_kernel,
        [((ROWS + 16, QW), F32), ((ROWS // 2, QW), BF16), ((ROWS // 2 + 16, QW), BF16)],
        [((QW // 2, LEN), BF16), ((LEN, QW // 2), BF16)],
        1 << 16,
        grad, proj, probs_t, query_early, key_early, normed_t, mixed, norm_gain, attend_weight,
    )
    arrived_v = swap(part_v, 2)
    arrived_v, outputs = lax.optimization_barrier((arrived_v, outputs))
    part_k = combined(keep_k, jnp.concatenate([swap(top_k, 1), swap(rest_k, 1)]))
    arrived_k = swap(part_k, 2)
    whole_v, whole_k = combined(part_v, arrived_v), combined(part_k, arrived_k)
    other_v, other_k = swap(whole_v, 1), swap(whole_k, 1)
    (grad_output,) = kernel_call(
        finish_output_kernel, [((ROWS, WIDTH), F32)], [], 1 << 33, whole_v, other_v
    )
    grad_attend, grad_gain = kernel_call(
        finish_attend_kernel,
        [((ROWS, PROJ), F32), ((ROWS,), F32)],
        [],
        1 << 16,
        whole_v, other_v, whole_k, other_k,
    )
    return outputs[None], grad_attend, grad_output, grad_gain


def solution(mesh):
    small = mesh.shape["seq"] == SEQ and mesh.shape["dp"] == DP
    return jax.shard_map(
        per_device_fast if small else per_device,
        mesh=mesh,
        in_specs=(
            P(("groups", "dp"), "seq", None),
            P(None, None, "dp"),
            P(),
            P(),
            P(),
            P(),
            P(("groups", "dp"), "seq", None),
        ),
        out_specs=(
            P(("groups", "dp"), "seq", None),
            P(("groups", "seq"), None),
            P(("groups", "seq"), None),
            P(("groups", "seq")),
        ),
        check_vma=False,
    )
```

```python
import functools

import jax
import jax.numpy as jnp
from jax import lax
from jax.experimental import pallas as pl
from jax.experimental.pallas import tpu as pltpu
from jax.sharding import PartitionSpec as P

HEADS = 4
KEY_DIM = 64
VAL_DIM = 192


def extended(value, sides, width):
    for axis, dim in sides:
        devices, length = (lax.axis_size(axis), value.shape[dim])
        up = [(i, (i + 1) % devices) for i in range(devices - 1)]
        down = [(j, i) for i, j in up]
        last = lax.slice_in_dim(value, length - width, length, axis=dim)
        first = lax.slice_in_dim(value, 0, width, axis=dim)
        before = lax.ppermute(last, axis, up)
        after = lax.ppermute(first, axis, down)
        value = jnp.concatenate([before, value, after], axis=dim)
    return value


def filter_block(padded, weights, bias_part):
    count = padded.shape[1] - 4
    total = bias_part
    for offset in range(5):
        total = total + jnp.einsum(
            "spc,co->spo",
            padded[:, offset : offset + count],
            weights[offset],
            preferred_element_type=jnp.float32,
        )
    activ = jax.nn.gelu(total, approximate=True)
    activ = activ.reshape(activ.shape[0], count // 2, 2, activ.shape[2])
    return (0.5 * (activ[:, :, 0] + activ[:, :, 1])).astype(jnp.bfloat16)


def per_device(
    dna_features, filter_weight, filter_bias, norm_gain, attend_weight, output_weight, cotangent
):
    padded = extended(dna_features, (("seq", 1),), 2)
    hidden = filter_block(
        padded, lax.all_gather(filter_weight, "dp", axis=2, tiled=True), filter_bias
    )
    hidden = hidden[0]
    widen = hidden.astype(jnp.float32)
    nhat = widen * lax.rsqrt(jnp.mean(widen * widen, axis=-1, keepdims=True) + 1e-06)
    normed = (nhat * norm_gain).astype(jnp.bfloat16)
    tokens = normed.shape[0]
    query_width = HEADS * KEY_DIM
    value_width = HEADS * VAL_DIM
    scale = KEY_DIM ** (-0.5)
    projected = jnp.dot(normed, attend_weight, preferred_element_type=jnp.float32).astype(
        jnp.bfloat16
    )
    queries = projected[:, :query_width]
    keys_local = projected[:, query_width : 2 * query_width]
    values_local = projected[:, 2 * query_width :]
    keys_all, values_all = (
        lax.all_gather(keys_local, "seq", axis=0, tiled=True),
        lax.all_gather(values_local, "seq", axis=0, tiled=True),
    )
    total_len = keys_all.shape[0]
    query_heads = queries.reshape(tokens, HEADS, KEY_DIM)
    key_heads = keys_all.reshape(total_len, HEADS, KEY_DIM)
    value_heads = values_all.reshape(total_len, HEADS, VAL_DIM)
    scores = (
        jnp.einsum("qhd,khd->hqk", query_heads, key_heads, preferred_element_type=jnp.float32)
        * scale
    )
    peak = jnp.max(scores, axis=-1, keepdims=True)
    logsum = peak + jnp.log(jnp.sum(jnp.exp(scores - peak), axis=-1, keepdims=True))
    probs = jnp.exp(scores - logsum)
    probs_b = probs.astype(jnp.bfloat16)
    attended = (
        jnp.einsum("hqk,khd->qhd", probs_b, value_heads, preferred_element_type=jnp.float32)
        .astype(jnp.bfloat16)
        .reshape(tokens, value_width)
    )
    branch = lax.dot_general(
        attended, output_weight, (((1,), (1,)), ((), ())), preferred_element_type=jnp.float32
    )
    outputs = widen + branch
    upstream = cotangent[0]
    output_part = lax.dot_general(
        upstream, attended, (((0,), (0,)), ((), ())), preferred_element_type=jnp.float32
    )
    d_attn = jnp.dot(upstream, output_weight, preferred_element_type=jnp.float32).astype(
        jnp.bfloat16
    )
    d_heads = d_attn.reshape(tokens, HEADS, VAL_DIM)
    attn_heads = attended.reshape(tokens, HEADS, VAL_DIM)
    delta = jnp.sum(d_heads.astype(jnp.float32) * attn_heads.astype(jnp.float32), axis=-1)
    dprob = jnp.einsum("qhd,khd->hqk", d_heads, value_heads, preferred_element_type=jnp.float32)
    dscore = (probs * (dprob - delta.T[:, :, None])).astype(jnp.bfloat16)
    d_query = (
        jnp.einsum("hqk,khd->qhd", dscore, key_heads, preferred_element_type=jnp.float32) * scale
    )
    logsum_rows = logsum[:, :, 0].T
    logsum_all, delta_all = (
        lax.all_gather(logsum_rows, "seq", axis=0, tiled=True),
        lax.all_gather(delta, "seq", axis=0, tiled=True),
    )
    key_heads_local = keys_local.reshape(tokens, HEADS, KEY_DIM)
    value_heads_local = values_local.reshape(tokens, HEADS, VAL_DIM)
    piece_query = lax.all_gather(queries, "seq", axis=0, tiled=True)
    piece_grad = lax.all_gather(d_attn, "seq", axis=0, tiled=True)
    count = piece_query.shape[0]
    piece_qheads = piece_query.reshape(count, HEADS, KEY_DIM)
    piece_gheads = piece_grad.reshape(count, HEADS, VAL_DIM)
    piece_scores = (
        jnp.einsum(
            "qhd,khd->hqk", piece_qheads, key_heads_local, preferred_element_type=jnp.float32
        )
        * scale
    )
    piece_probs = jnp.exp(piece_scores - logsum_all.T[:, :, None])
    piece_probs_b = piece_probs.astype(jnp.bfloat16)
    piece_dprob = jnp.einsum(
        "qhd,khd->hqk", piece_gheads, value_heads_local, preferred_element_type=jnp.float32
    )
    piece_dscore = (piece_probs * (piece_dprob - delta_all.T[:, :, None])).astype(jnp.bfloat16)
    grad_keys = jnp.einsum(
        "hqk,qhd->khd", piece_dscore, piece_qheads, preferred_element_type=jnp.float32
    )
    grad_values = jnp.einsum(
        "hqk,qhd->khd", piece_probs_b, piece_gheads, preferred_element_type=jnp.float32
    )
    grad_keys, grad_values = (grad_keys, grad_values)
    d_proj = jnp.concatenate(
        [
            d_query.reshape(tokens, query_width),
            (grad_keys * scale).reshape(tokens, query_width),
            grad_values.reshape(tokens, value_width),
        ],
        axis=1,
    ).astype(jnp.bfloat16)
    d_normed = lax.dot_general(
        d_proj, attend_weight, (((1,), (1,)), ((), ())), preferred_element_type=jnp.float32
    )
    attend_part = lax.dot_general(
        normed, d_proj, (((0,), (0,)), ((), ())), preferred_element_type=jnp.float32
    )
    gain_part = jnp.sum(d_normed * nhat, axis=0)
    attend_share, output_share, gain_share = (
        lax.psum_scatter(
            attend_part.astype(jnp.bfloat16), "seq", scatter_dimension=0, tiled=True
        ).astype(jnp.float32),
        lax.psum_scatter(
            output_part.astype(jnp.bfloat16), "seq", scatter_dimension=0, tiled=True
        ).astype(jnp.float32),
        lax.psum_scatter(
            gain_part.astype(jnp.bfloat16), "seq", scatter_dimension=0, tiled=True
        ).astype(jnp.float32),
    )
    grad_attend, grad_output, grad_gain = lax.psum((attend_share, output_share, gain_share), "dp")
    return (outputs[None], grad_attend, grad_output, grad_gain)


F32, BF16 = jnp.float32, jnp.bfloat16
SEQ, DP = 4, 4
TOK = 128
EDGE = 16
LEN = SEQ * TOK
CIN, WIDTH = 384, 768
SHARD = WIDTH // DP
ROWS = WIDTH // SEQ
QW, VW = HEADS * KEY_DIM, HEADS * VAL_DIM
PROJ = 2 * QW + VW
SCALE = KEY_DIM**-0.5
LOG2E = 1.4426950408889634
NN = (((1,), (0,)), ((), ()))
NT = (((1,), (1,)), ((), ()))
TN = (((0,), (0,)), ((), ()))


def mm(left, right, dims=NN):
    return lax.dot_general(left, right, dims, preferred_element_type=F32)


def half_gelu(value):
    inner = 0.7978845608028654 * (value + 0.044715 * value * value * value)
    return 0.5 * value * (1.0 + jnp.tanh(inner))


def ring(value, step):
    return lax.ppermute(value, "seq", [(i, (i + step) % SEQ) for i in range(SEQ)])


def swap(value, bit):
    return lax.ppermute(value, "dp", [(i, i ^ bit) for i in range(DP)])


def put_shards(taps, mine, other, core):
    for tap in range(5):
        lanes = slice(tap * CIN, (tap + 1) * CIN)
        rows = slice(tap * SHARD, (tap + 1) * SHARD)
        taps[pl.ds(core * SHARD, SHARD), lanes] = mine[rows, :]
        taps[pl.ds((1 - core) * SHARD, SHARD), lanes] = other[rows, :]


def put_shard(taps, shard):
    for tap in range(5):
        taps[:, tap * CIN : (tap + 1) * CIN] = shard[tap * SHARD : (tap + 1) * SHARD, :]


def shard_of(bias, index):
    every = bias[...].reshape(1, WIDTH)
    mine = every[:, :SHARD]
    for at in range(1, DP):
        mine = jnp.where(index == at, every[:, at * SHARD : (at + 1) * SHARD], mine)
    return mine


def half_of(bias, side):
    both = bias[...].reshape(1, WIDTH)
    return jnp.where(side == 0, both[:, : WIDTH // 2], both[:, WIDTH // 2 :])


def filtered_half(windows, taps, bias):
    even = mm(windows[:, : 5 * CIN], taps[...], NT) + bias
    odd = mm(windows[:, CIN:], taps[...], NT) + bias
    return (0.5 * (half_gelu(even) + half_gelu(odd))).astype(BF16)


def taps_kernel(w0_far, w1, taps, w0, sems):
    load = pltpu.make_async_copy(w0_far, w0, sems.at[0])
    load.start()
    load.wait()
    put_shards(taps, w0, w1, lax.rem(lax.axis_index("dp"), 2))


def fill_positions(positions, z, parts):
    chunk = 2 * TOK
    for g in range(CIN // 128):
        positions[g, 0:8, :] = jnp.zeros((8, 128), F32)
        positions[g, 8 + 2 * LEN :, :] = jnp.zeros((8, 128), F32)
        for ref, off in parts:
            start = pl.multiple_of(lax.rem(z + off, SEQ) * chunk + 8, 8)
            if ref is None:
                positions[g, pl.ds(start, chunk), :] = jnp.zeros((chunk, 128), F32)
            else:
                positions[g, pl.ds(start, chunk), :] = ref[:, g * 128 : (g + 1) * 128].astype(F32)


def near_kernel(f0, fa, fb, taps, bias, windows, hid, positions):
    z, d = lax.axis_index("seq"), lax.axis_index("dp")
    fill_positions(positions, z, ((f0, 0), (fa, 3), (fb, 1), (None, 2)))
    for g in range(CIN // 128):
        for k in range(6):
            at = k * CIN + g * 128
            windows[:, at : at + 128] = positions[g, pl.ds(6 + k, LEN, stride=2), :].astype(BF16)
    hid[...] = filtered_half(windows, taps, half_of(bias, d // 2))


def row_picker(z):
    row = lax.broadcasted_iota(jnp.int32, (ROWS, WIDTH), 0)
    lane = lax.broadcasted_iota(jnp.int32, (ROWS, WIDTH), 1)
    return jnp.where(lane == row + z * ROWS, 1.0, 0.0).astype(BF16)


def mend_kernel(
    fa, fb, fc, windows_in, hid_in, taps, w2, bias, windows, hid, hid_two, positions, two
):
    z, d = lax.axis_index("seq"), lax.axis_index("dp")
    fill_positions(positions, z, ((fa, 3), (fb, 1), (fc, 2)))
    windows[...] = windows_in[...]
    hid[...] = hid_in[...]
    first = jnp.clip(lax.rem(z + 2, SEQ) * TOK - EDGE, 0, LEN - TOK - 2 * EDGE)
    first = pl.multiple_of(first, EDGE)
    fresh = pl.ds(first, TOK + 2 * EDGE)
    for g in range(CIN // 128):
        for k in range(6):
            at = k * CIN + g * 128
            spots = pl.ds(2 * first + (6 + k), TOK + 2 * EDGE, stride=2)
            windows[fresh, at : at + 128] = positions[g, spots, :].astype(BF16)
    hid[fresh, :] = filtered_half(windows[fresh, :], taps, half_of(bias, d // 2))
    put_shard(two, w2)
    hid_two[...] = filtered_half(windows, two, shard_of(bias, lax.rem(d + 2, DP)))


def project_kernel(
    windows, hid_near, hid_two, w3, bias, gain, aw, hid, normed, proj, normed_t, three, far
):
    z, d = lax.axis_index("seq"), lax.axis_index("dp")
    side, core, half = d // 2, lax.rem(d, 2), WIDTH // 2
    put_shard(three, w3)
    hid[side] = hid_near[...]
    far[core] = hid_two[...]
    far[1 - core] = filtered_half(windows, three, shard_of(bias, 2 * (1 - side) + 1 - core))
    hid[1 - side] = jnp.concatenate([far[0], far[1]], axis=1)
    low, high = hid[0].astype(F32), hid[1].astype(F32)
    square = jnp.sum(low * low, axis=1, keepdims=True) + jnp.sum(high * high, axis=1, keepdims=True)
    inv = lax.rsqrt(square * (1.0 / WIDTH) + 1e-06)
    scales = gain[...].reshape(1, WIDTH)
    normed[:, :half] = (low * inv * scales[:, :half]).astype(BF16)
    normed[:, half:] = (high * inv * scales[:, half:]).astype(BF16)
    proj[...] = mm(normed[...], aw[...]).astype(BF16)
    normed_t[...] = mm(row_picker(z), normed[...], NT).astype(BF16)


def heads_of(proj, h):
    q = proj[:, h * KEY_DIM : (h + 1) * KEY_DIM]
    k = proj[:, QW + h * KEY_DIM : QW + (h + 1) * KEY_DIM]
    v = proj[:, 2 * QW + h * VAL_DIM : 2 * QW + (h + 1) * VAL_DIM]
    return q, k, v


def attend_kernel(proj, probs_t, att_t):
    for h in range(HEADS):
        q, k, v = heads_of(proj, h)
        scores = mm(k, q, NT) * (SCALE * LOG2E)
        top = jnp.max(scores, axis=0, keepdims=True)
        weight = jnp.exp2(scores - top)
        total = jnp.sum(weight, axis=0, keepdims=True)
        probs = (weight * (1.0 / total)).astype(BF16)
        probs_t[h] = probs
        att_t[h * VAL_DIM : (h + 1) * VAL_DIM, :] = mm(v, probs, TN).astype(BF16)


def outputs_kernel(hid, att_t, ow, outputs):
    z = lax.axis_index("seq")
    half = WIDTH // 2
    for at in range(SEQ):

        @pl.when(z == at)
        def _():
            rows = slice(at * TOK, (at + 1) * TOK)
            branch = mm(att_t[:, rows], ow[...], (((0,), (1,)), ((), ())))
            outputs[:, :half] = branch[:, :half] + hid[0, rows, :].astype(F32)
            outputs[:, half:] = branch[:, half:] + hid[1, rows, :].astype(F32)


def both_ways(write, keep, send, core):
    for at in range(2):

        @pl.when(core == at)
        def _():
            write(keep, at)
            write(send, 1 - at)


def early_grad_kernel(c0, ca, ow, early):
    early[0] = mm(c0[...], ow[...]).astype(BF16)
    early[1] = mm(ca[...], ow[...]).astype(BF16)


def value_kernel(early, c0, ca, cb, cc, normed_t, probs_t, att_t, aw, ow, grad, keep, send, mixed, cot, cot_t, d_value):
    z, d = lax.axis_index("seq"), lax.axis_index("dp")
    for ref, off in ((c0, 0), (ca, 3), (cb, 1), (cc, 2)):
        start = pl.multiple_of(lax.rem(z + off, SEQ) * TOK, TOK)
        cot[pl.ds(start, TOK), :] = ref[...]
    cot_t[...] = mm(row_picker(z), cot[...], NT).astype(BF16)
    for index, off in ((0, 0), (1, 3)):
        start = pl.multiple_of(lax.rem(z + off, SEQ) * TOK, TOK)
        grad[pl.ds(start, TOK), :] = early[index]
    late = mm(jnp.concatenate([cb[...], cc[...]], axis=0), ow[...]).astype(BF16)
    for index, off in ((0, 1), (1, 2)):
        start = pl.multiple_of(lax.rem(z + off, SEQ) * TOK, TOK)
        grad[pl.ds(start, TOK), :] = late[index * TOK : (index + 1) * TOK, :]
    out_part = mm(cot_t[...], att_t[...], NT)
    for h in range(HEADS):
        lanes = slice(h * VAL_DIM, (h + 1) * VAL_DIM)
        d_value[:, lanes] = mm(probs_t[h], grad[:, lanes]).astype(BF16)
    value_part = mm(normed_t[...], d_value[...])
    here = pl.multiple_of(z * ROWS, ROWS)
    total = jnp.sum(value_part * aw[pl.ds(here, ROWS), 2 * QW :].astype(F32), axis=1, keepdims=True)
    mixed[...] = jnp.broadcast_to(total, (ROWS, 128))
    half = VW // 2

    def write(ref, side):
        lanes = slice(side * half, (side + 1) * half)
        ref[:, :half] = value_part[:, lanes].astype(ref.dtype)
        ref[:, half:] = out_part[:, lanes].astype(ref.dtype)

    both_ways(write, keep, send, lax.rem(d, 2))


def score_grads(grad, proj, probs_t, d_query, d_key, first):
    for h in range(first, first + HEADS // 2):
        q, k, v = heads_of(proj, h)
        probs = probs_t[h].astype(F32)
        product = mm(v, grad[:, h * VAL_DIM : (h + 1) * VAL_DIM], NT) * probs
        delta = jnp.sum(product, axis=0, keepdims=True)
        dscore = (product - probs * delta).astype(BF16)
        lanes = slice((h - first) * KEY_DIM, (h - first + 1) * KEY_DIM)
        d_query[lanes, :] = (mm(k, dscore, TN) * SCALE).astype(BF16)
        d_key[:, lanes] = (mm(dscore, q) * SCALE).astype(BF16)


def early_key_kernel(grad, proj, probs_t, d_query, d_key):
    score_grads(grad, proj, probs_t, d_query, d_key, 0)


def late_key_kernel(
    grad, proj, probs_t, query_early, key_early, normed_t, mixed, gain, aw, keep, top, rest, d_query, d_key
):
    z, d = lax.axis_index("seq"), lax.axis_index("dp")
    score_grads(grad, proj, probs_t, d_query, d_key, HEADS // 2)
    left = normed_t[...]
    query_part = jnp.concatenate([mm(left, query_early[...], NT), mm(left, d_query[...], NT)], axis=1)
    key_part = jnp.concatenate([mm(left, key_early[...]), mm(left, d_key[...])], axis=1)
    here = pl.multiple_of(z * ROWS, ROWS)
    total = query_part * aw[pl.ds(here, ROWS), :QW].astype(F32)
    total = total + key_part * aw[pl.ds(here, ROWS), QW : 2 * QW].astype(F32)
    total = mixed[...] + jnp.sum(total, axis=1, keepdims=True)
    scales = gain[...].reshape(1, WIDTH)
    mine = scales[:, :ROWS]
    for at in range(1, SEQ):
        mine = jnp.where(z == at, scales[:, at * ROWS : (at + 1) * ROWS], mine)
    gain_part = total.T[0:1, :] / mine

    gain_rows = jnp.concatenate([gain_part, jnp.zeros((15, ROWS), F32)], axis=0)
    cut = ROWS // 2

    def part(side, rows):
        return (key_part if side else query_part)[rows, :]

    for at in range(2):

        @pl.when(lax.rem(d, 2) == at)
        def _():
            keep[:ROWS, :] = part(at, slice(0, ROWS))
            keep[ROWS:, :] = jnp.zeros((16, QW), F32)
            keep[ROWS:, :ROWS] = gain_rows
            top[...] = part(1 - at, slice(0, cut)).astype(BF16)
            rest[:cut, :] = part(1 - at, slice(cut, ROWS)).astype(BF16)
            rest[cut:, :] = jnp.zeros((16, QW), BF16)
            rest[cut:, :ROWS] = gain_rows.astype(BF16)


def finish_output_kernel(whole_v, other_v, grad_output):
    half = VW // 2
    for at in range(2):

        @pl.when(lax.rem(lax.axis_index("dp"), 2) == at)
        def _():
            grad_output[:, at * half : (at + 1) * half] = whole_v[:, half:].astype(F32)
            grad_output[:, (1 - at) * half : (2 - at) * half] = other_v[:, half:].astype(F32)


def finish_attend_kernel(whole_v, other_v, whole_k, other_k, grad_attend, grad_gain):
    half, base = VW // 2, 2 * QW
    for at in range(2):

        @pl.when(lax.rem(lax.axis_index("dp"), 2) == at)
        def _():
            grad_attend[:, base + at * half : base + (at + 1) * half] = whole_v[:, :half].astype(F32)
            grad_attend[:, base + (1 - at) * half : base + (2 - at) * half] = other_v[:, :half].astype(F32)
            low, high = (whole_k, other_k) if at == 0 else (other_k, whole_k)
            grad_attend[:, :QW] = low[:ROWS, :].astype(F32)
            grad_attend[:, QW : 2 * QW] = high[:ROWS, :].astype(F32)
            grad_gain[...] = low[ROWS : ROWS + 8, :ROWS].astype(F32)[0]


def kernel_call(body, outs, scratch, flops, *args, far=()):
    whole = pl.BlockSpec(memory_space=pltpu.VMEM)
    away = pl.BlockSpec(memory_space=pltpu.HBM)
    sems = [pltpu.SemaphoreType.DMA((len(far),))] if far else []
    return pl.pallas_call(
        body,
        in_specs=[away if i in far else whole for i in range(len(args))],
        out_shape=[jax.ShapeDtypeStruct(s, t) for s, t in outs],
        scratch_shapes=[pltpu.VMEM(s, t) for s, t in scratch] + sems,
        compiler_params=pltpu.CompilerParams(vmem_limit_bytes=40 << 20),
        cost_estimate=pl.CostEstimate(flops=flops, bytes_accessed=1 << 16, transcendentals=0),
    )(*args)


def combined(keep, arrived):
    return (keep.astype(F32) + arrived.astype(F32)).astype(BF16)


def per_device_fast(
    dna_features, filter_weight, filter_bias, norm_gain, attend_weight, output_weight, cotangent
):
    f0, c0 = dna_features[0], cotangent[0]
    w0 = filter_weight.transpose(0, 2, 1).reshape(5 * SHARD, CIN)
    half = WIDTH // 2
    w2 = swap(w0, 2)
    w1 = swap(w0, 1)
    fa, fb = ring(f0, 1), ring(f0, SEQ - 1)
    (taps,) = kernel_call(
        taps_kernel,
        [((2 * SHARD, 5 * CIN), BF16)],
        [((5 * SHARD, CIN), BF16)],
        1 << 24,
        pltpu.with_memory_space_constraint(w0, pltpu.HBM), w1,
        far=(0,),
    )
    ca = ring(c0, 1)
    far_a, taps = lax.optimization_barrier((fa, taps))
    to_left, far_a, fb = lax.optimization_barrier((c0, far_a, fb))
    fc = ring(far_a, 1)
    windows, hid_near = kernel_call(
        near_kernel,
        [((LEN, 6 * CIN), BF16), ((LEN, half), BF16)],
        [((CIN // 128, 16 + 2 * LEN, 128), F32)],
        1 << 33,
        f0, fa, fb, taps, filter_bias,
    )
    ca, windows = lax.optimization_barrier((ca, windows))
    cb, cc = ring(to_left, SEQ - 1), ring(ca, 1)
    (early,) = kernel_call(
        early_grad_kernel, [((2, TOK, WIDTH), BF16)], [], 1 << 24, c0, ca, output_weight
    )
    w2, fc, windows, early = lax.optimization_barrier((w2, fc, windows, early))
    w3 = swap(w2, 1)
    windows, hid_near, hid_two = kernel_call(
        mend_kernel,
        [((LEN, 6 * CIN), BF16), ((LEN, half), BF16), ((LEN, SHARD), BF16)],
        [((CIN // 128, 16 + 2 * LEN, 128), F32), ((SHARD, 5 * CIN), BF16)],
        1 << 33,
        fa, fb, fc, windows, hid_near, taps, w2, filter_bias,
    )
    hid, normed, proj, normed_t = kernel_call(
        project_kernel,
        [((2, LEN, half), BF16), ((LEN, WIDTH), BF16), ((LEN, PROJ), BF16), ((ROWS, LEN), BF16)],
        [((SHARD, 5 * CIN), BF16), ((2, LEN, SHARD), BF16)],
        1 << 24,
        windows, hid_near, hid_two, w3, filter_bias, norm_gain, attend_weight,
    )
    probs_t, att_t = kernel_call(
        attend_kernel,
        [((HEADS, LEN, LEN), BF16), ((VW, LEN), BF16)],
        [],
        1 << 29,
        proj,
    )
    (outputs,) = kernel_call(
        outputs_kernel, [((TOK, WIDTH), F32)], [], 1 << 33, hid, att_t, output_weight
    )
    grad, keep_v, send_v, mixed = kernel_call(
        value_kernel,
        [((LEN, VW), BF16), ((ROWS, VW), F32), ((ROWS, VW), BF16), ((ROWS, 128), F32)],
        [((LEN, WIDTH), BF16), ((ROWS, LEN), BF16), ((LEN, VW), BF16)],
        1 << 31,
        early, c0, ca, cb, cc, normed_t, probs_t, att_t, attend_weight, output_weight,
    )
    query_early, key_early = kernel_call(
        early_key_kernel,
        [((QW // 2, LEN), BF16), ((LEN, QW // 2), BF16)],
        [],
        1 << 33,
        grad, proj, probs_t,
    )
    part_v = combined(keep_v, swap(send_v, 1))
    part_v, query_early = lax.optimization_barrier((part_v, query_early))
    keep_k, top_k, rest_k = kernel_call(
        late_key_kernel,
        [((ROWS + 16, QW), F32), ((ROWS // 2, QW), BF16), ((ROWS // 2 + 16, QW), BF16)],
        [((QW // 2, LEN), BF16), ((LEN, QW // 2), BF16)],
        1 << 16,
        grad, proj, probs_t, query_early, key_early, normed_t, mixed, norm_gain, attend_weight,
    )
    arrived_v = swap(part_v, 2)
    arrived_v, outputs = lax.optimization_barrier((arrived_v, outputs))
    part_k = combined(keep_k, jnp.concatenate([swap(top_k, 1), swap(rest_k, 1)]))
    arrived_k = swap(part_k, 2)
    whole_v, whole_k = combined(part_v, arrived_v), combined(part_k, arrived_k)
    other_v, other_k = swap(whole_v, 1), swap(whole_k, 1)
    (grad_output,) = kernel_call(
        finish_output_kernel, [((ROWS, WIDTH), F32)], [], 1 << 33, whole_v, other_v
    )
    grad_attend, grad_gain = kernel_call(
        finish_attend_kernel,
        [((ROWS, PROJ), F32), ((ROWS,), F32)],
        [],
        1 << 16,
        whole_v, other_v, whole_k, other_k,
    )
    return outputs[None], grad_attend, grad_output, grad_gain


def solution(mesh):
    small = mesh.shape["seq"] == SEQ and mesh.shape["dp"] == DP
    return jax.shard_map(
        per_device_fast if small else per_device,
        mesh=mesh,
        in_specs=(
            P(("groups", "dp"), "seq", None),
            P(None, None, "dp"),
            P(),
            P(),
            P(),
            P(),
            P(("groups", "dp"), "seq", None),
        ),
        out_specs=(
            P(("groups", "dp"), "seq", None),
            P(("groups", "seq"), None),
            P(("groups", "seq"), None),
            P(("groups", "seq")),
        ),
        check_vma=False,
    )
```

```python
import functools

import jax
import jax.numpy as jnp
from jax import lax
from jax.experimental import pallas as pl
from jax.experimental.pallas import tpu as pltpu
from jax.sharding import PartitionSpec as P

HEADS = 4
KEY_DIM = 64
VAL_DIM = 192


def extended(value, sides, width):
    for axis, dim in sides:
        devices, length = (lax.axis_size(axis), value.shape[dim])
        up = [(i, (i + 1) % devices) for i in range(devices - 1)]
        down = [(j, i) for i, j in up]
        last = lax.slice_in_dim(value, length - width, length, axis=dim)
        first = lax.slice_in_dim(value, 0, width, axis=dim)
        before = lax.ppermute(last, axis, up)
        after = lax.ppermute(first, axis, down)
        value = jnp.concatenate([before, value, after], axis=dim)
    return value


def filter_block(padded, weights, bias_part):
    count = padded.shape[1] - 4
    total = bias_part
    for offset in range(5):
        total = total + jnp.einsum(
            "spc,co->spo",
            padded[:, offset : offset + count],
            weights[offset],
            preferred_element_type=jnp.float32,
        )
    activ = jax.nn.gelu(total, approximate=True)
    activ = activ.reshape(activ.shape[0], count // 2, 2, activ.shape[2])
    return (0.5 * (activ[:, :, 0] + activ[:, :, 1])).astype(jnp.bfloat16)


def per_device(
    dna_features, filter_weight, filter_bias, norm_gain, attend_weight, output_weight, cotangent
):
    padded = extended(dna_features, (("seq", 1),), 2)
    hidden = filter_block(
        padded, lax.all_gather(filter_weight, "dp", axis=2, tiled=True), filter_bias
    )
    hidden = hidden[0]
    widen = hidden.astype(jnp.float32)
    nhat = widen * lax.rsqrt(jnp.mean(widen * widen, axis=-1, keepdims=True) + 1e-06)
    normed = (nhat * norm_gain).astype(jnp.bfloat16)
    tokens = normed.shape[0]
    query_width = HEADS * KEY_DIM
    value_width = HEADS * VAL_DIM
    scale = KEY_DIM ** (-0.5)
    projected = jnp.dot(normed, attend_weight, preferred_element_type=jnp.float32).astype(
        jnp.bfloat16
    )
    queries = projected[:, :query_width]
    keys_local = projected[:, query_width : 2 * query_width]
    values_local = projected[:, 2 * query_width :]
    keys_all, values_all = (
        lax.all_gather(keys_local, "seq", axis=0, tiled=True),
        lax.all_gather(values_local, "seq", axis=0, tiled=True),
    )
    total_len = keys_all.shape[0]
    query_heads = queries.reshape(tokens, HEADS, KEY_DIM)
    key_heads = keys_all.reshape(total_len, HEADS, KEY_DIM)
    value_heads = values_all.reshape(total_len, HEADS, VAL_DIM)
    scores = (
        jnp.einsum("qhd,khd->hqk", query_heads, key_heads, preferred_element_type=jnp.float32)
        * scale
    )
    peak = jnp.max(scores, axis=-1, keepdims=True)
    logsum = peak + jnp.log(jnp.sum(jnp.exp(scores - peak), axis=-1, keepdims=True))
    probs = jnp.exp(scores - logsum)
    probs_b = probs.astype(jnp.bfloat16)
    attended = (
        jnp.einsum("hqk,khd->qhd", probs_b, value_heads, preferred_element_type=jnp.float32)
        .astype(jnp.bfloat16)
        .reshape(tokens, value_width)
    )
    branch = lax.dot_general(
        attended, output_weight, (((1,), (1,)), ((), ())), preferred_element_type=jnp.float32
    )
    outputs = widen + branch
    upstream = cotangent[0]
    output_part = lax.dot_general(
        upstream, attended, (((0,), (0,)), ((), ())), preferred_element_type=jnp.float32
    )
    d_attn = jnp.dot(upstream, output_weight, preferred_element_type=jnp.float32).astype(
        jnp.bfloat16
    )
    d_heads = d_attn.reshape(tokens, HEADS, VAL_DIM)
    attn_heads = attended.reshape(tokens, HEADS, VAL_DIM)
    delta = jnp.sum(d_heads.astype(jnp.float32) * attn_heads.astype(jnp.float32), axis=-1)
    dprob = jnp.einsum("qhd,khd->hqk", d_heads, value_heads, preferred_element_type=jnp.float32)
    dscore = (probs * (dprob - delta.T[:, :, None])).astype(jnp.bfloat16)
    d_query = (
        jnp.einsum("hqk,khd->qhd", dscore, key_heads, preferred_element_type=jnp.float32) * scale
    )
    logsum_rows = logsum[:, :, 0].T
    logsum_all, delta_all = (
        lax.all_gather(logsum_rows, "seq", axis=0, tiled=True),
        lax.all_gather(delta, "seq", axis=0, tiled=True),
    )
    key_heads_local = keys_local.reshape(tokens, HEADS, KEY_DIM)
    value_heads_local = values_local.reshape(tokens, HEADS, VAL_DIM)
    piece_query = lax.all_gather(queries, "seq", axis=0, tiled=True)
    piece_grad = lax.all_gather(d_attn, "seq", axis=0, tiled=True)
    count = piece_query.shape[0]
    piece_qheads = piece_query.reshape(count, HEADS, KEY_DIM)
    piece_gheads = piece_grad.reshape(count, HEADS, VAL_DIM)
    piece_scores = (
        jnp.einsum(
            "qhd,khd->hqk", piece_qheads, key_heads_local, preferred_element_type=jnp.float32
        )
        * scale
    )
    piece_probs = jnp.exp(piece_scores - logsum_all.T[:, :, None])
    piece_probs_b = piece_probs.astype(jnp.bfloat16)
    piece_dprob = jnp.einsum(
        "qhd,khd->hqk", piece_gheads, value_heads_local, preferred_element_type=jnp.float32
    )
    piece_dscore = (piece_probs * (piece_dprob - delta_all.T[:, :, None])).astype(jnp.bfloat16)
    grad_keys = jnp.einsum(
        "hqk,qhd->khd", piece_dscore, piece_qheads, preferred_element_type=jnp.float32
    )
    grad_values = jnp.einsum(
        "hqk,qhd->khd", piece_probs_b, piece_gheads, preferred_element_type=jnp.float32
    )
    grad_keys, grad_values = (grad_keys, grad_values)
    d_proj = jnp.concatenate(
        [
            d_query.reshape(tokens, query_width),
            (grad_keys * scale).reshape(tokens, query_width),
            grad_values.reshape(tokens, value_width),
        ],
        axis=1,
    ).astype(jnp.bfloat16)
    d_normed = lax.dot_general(
        d_proj, attend_weight, (((1,), (1,)), ((), ())), preferred_element_type=jnp.float32
    )
    attend_part = lax.dot_general(
        normed, d_proj, (((0,), (0,)), ((), ())), preferred_element_type=jnp.float32
    )
    gain_part = jnp.sum(d_normed * nhat, axis=0)
    attend_share, output_share, gain_share = (
        lax.psum_scatter(
            attend_part.astype(jnp.bfloat16), "seq", scatter_dimension=0, tiled=True
        ).astype(jnp.float32),
        lax.psum_scatter(
            output_part.astype(jnp.bfloat16), "seq", scatter_dimension=0, tiled=True
        ).astype(jnp.float32),
        lax.psum_scatter(
            gain_part.astype(jnp.bfloat16), "seq", scatter_dimension=0, tiled=True
        ).astype(jnp.float32),
    )
    grad_attend, grad_output, grad_gain = lax.psum((attend_share, output_share, gain_share), "dp")
    return (outputs[None], grad_attend, grad_output, grad_gain)


F32, BF16 = jnp.float32, jnp.bfloat16
SEQ, DP = 4, 4
TOK = 128
EDGE = 16
LEN = SEQ * TOK
CIN, WIDTH = 384, 768
SHARD = WIDTH // DP
ROWS = WIDTH // SEQ
QW, VW = HEADS * KEY_DIM, HEADS * VAL_DIM
PROJ = 2 * QW + VW
SCALE = KEY_DIM**-0.5
LOG2E = 1.4426950408889634
NN = (((1,), (0,)), ((), ()))
NT = (((1,), (1,)), ((), ()))
TN = (((0,), (0,)), ((), ()))


def mm(left, right, dims=NN):
    return lax.dot_general(left, right, dims, preferred_element_type=F32)


def half_gelu(value):
    inner = 0.7978845608028654 * (value + 0.044715 * value * value * value)
    return 0.5 * value * (1.0 + jnp.tanh(inner))


def ring(value, step):
    return lax.ppermute(value, "seq", [(i, (i + step) % SEQ) for i in range(SEQ)])


def swap(value, bit):
    return lax.ppermute(value, "dp", [(i, i ^ bit) for i in range(DP)])


def put_shards(taps, mine, other, core):
    for tap in range(5):
        lanes = slice(tap * CIN, (tap + 1) * CIN)
        rows = slice(tap * SHARD, (tap + 1) * SHARD)
        taps[pl.ds(core * SHARD, SHARD), lanes] = mine[rows, :]
        taps[pl.ds((1 - core) * SHARD, SHARD), lanes] = other[rows, :]


def put_shard(taps, shard):
    for tap in range(5):
        taps[:, tap * CIN : (tap + 1) * CIN] = shard[tap * SHARD : (tap + 1) * SHARD, :]


def shard_of(bias, index):
    every = bias[...].reshape(1, WIDTH)
    mine = every[:, :SHARD]
    for at in range(1, DP):
        mine = jnp.where(index == at, every[:, at * SHARD : (at + 1) * SHARD], mine)
    return mine


def half_of(bias, side):
    both = bias[...].reshape(1, WIDTH)
    return jnp.where(side == 0, both[:, : WIDTH // 2], both[:, WIDTH // 2 :])


def filtered_half(windows, taps, bias):
    even = mm(windows[:, : 5 * CIN], taps[...], NT) + bias
    odd = mm(windows[:, CIN:], taps[...], NT) + bias
    return (0.5 * (half_gelu(even) + half_gelu(odd))).astype(BF16)


def taps_kernel(w0_far, w1, taps, w0, sems):
    load = pltpu.make_async_copy(w0_far, w0, sems.at[0])
    load.start()
    load.wait()
    put_shards(taps, w0, w1, lax.rem(lax.axis_index("dp"), 2))


def fill_positions(positions, z, parts):
    chunk = 2 * TOK
    for g in range(CIN // 128):
        positions[g, 0:8, :] = jnp.zeros((8, 128), F32)
        positions[g, 8 + 2 * LEN :, :] = jnp.zeros((8, 128), F32)
        for ref, off in parts:
            start = pl.multiple_of(lax.rem(z + off, SEQ) * chunk + 8, 8)
            if ref is None:
                positions[g, pl.ds(start, chunk), :] = jnp.zeros((chunk, 128), F32)
            else:
                positions[g, pl.ds(start, chunk), :] = ref[:, g * 128 : (g + 1) * 128].astype(F32)


def near_kernel(f0, fa, fb, taps, bias, windows, hid, positions):
    z, d = lax.axis_index("seq"), lax.axis_index("dp")
    fill_positions(positions, z, ((f0, 0), (fa, 3), (fb, 1), (None, 2)))
    for g in range(CIN // 128):
        for k in range(6):
            at = k * CIN + g * 128
            windows[:, at : at + 128] = positions[g, pl.ds(6 + k, LEN, stride=2), :].astype(BF16)
    hid[...] = filtered_half(windows, taps, half_of(bias, d // 2))


def row_picker(z):
    row = lax.broadcasted_iota(jnp.int32, (ROWS, WIDTH), 0)
    lane = lax.broadcasted_iota(jnp.int32, (ROWS, WIDTH), 1)
    return jnp.where(lane == row + z * ROWS, 1.0, 0.0).astype(BF16)


def mend_kernel(
    fa, fb, fc, windows_in, hid_in, taps, w2, bias, windows, hid, hid_two, positions, two
):
    z, d = lax.axis_index("seq"), lax.axis_index("dp")
    fill_positions(positions, z, ((fa, 3), (fb, 1), (fc, 2)))
    windows[...] = windows_in[...]
    hid[...] = hid_in[...]
    first = jnp.clip(lax.rem(z + 2, SEQ) * TOK - EDGE, 0, LEN - TOK - 2 * EDGE)
    first = pl.multiple_of(first, EDGE)
    fresh = pl.ds(first, TOK + 2 * EDGE)
    for g in range(CIN // 128):
        for k in range(6):
            at = k * CIN + g * 128
            spots = pl.ds(2 * first + (6 + k), TOK + 2 * EDGE, stride=2)
            windows[fresh, at : at + 128] = positions[g, spots, :].astype(BF16)
    hid[fresh, :] = filtered_half(windows[fresh, :], taps, half_of(bias, d // 2))
    put_shard(two, w2)
    hid_two[...] = filtered_half(windows, two, shard_of(bias, lax.rem(d + 2, DP)))


def project_kernel(
    windows, hid_near, hid_two, w3, bias, gain, aw, hid, normed, proj, normed_t, three, far
):
    z, d = lax.axis_index("seq"), lax.axis_index("dp")
    side, core, half = d // 2, lax.rem(d, 2), WIDTH // 2
    put_shard(three, w3)
    hid[side] = hid_near[...]
    far[core] = hid_two[...]
    far[1 - core] = filtered_half(windows, three, shard_of(bias, 2 * (1 - side) + 1 - core))
    hid[1 - side] = jnp.concatenate([far[0], far[1]], axis=1)
    low, high = hid[0].astype(F32), hid[1].astype(F32)
    square = jnp.sum(low * low, axis=1, keepdims=True) + jnp.sum(high * high, axis=1, keepdims=True)
    inv = lax.rsqrt(square * (1.0 / WIDTH) + 1e-06)
    scales = gain[...].reshape(1, WIDTH)
    normed[:, :half] = (low * inv * scales[:, :half]).astype(BF16)
    normed[:, half:] = (high * inv * scales[:, half:]).astype(BF16)
    proj[...] = mm(normed[...], aw[...]).astype(BF16)
    normed_t[...] = mm(row_picker(z), normed[...], NT).astype(BF16)


def heads_of(proj, h):
    q = proj[:, h * KEY_DIM : (h + 1) * KEY_DIM]
    k = proj[:, QW + h * KEY_DIM : QW + (h + 1) * KEY_DIM]
    v = proj[:, 2 * QW + h * VAL_DIM : 2 * QW + (h + 1) * VAL_DIM]
    return q, k, v


def attend_kernel(proj, probs_t, att_t):
    for h in range(HEADS):
        q, k, v = heads_of(proj, h)
        scores = mm(k, q, NT) * (SCALE * LOG2E)
        top = jnp.max(scores, axis=0, keepdims=True)
        weight = jnp.exp2(scores - top)
        total = jnp.sum(weight, axis=0, keepdims=True)
        probs = (weight * (1.0 / total)).astype(BF16)
        probs_t[h] = probs
        att_t[h * VAL_DIM : (h + 1) * VAL_DIM, :] = mm(v, probs, TN).astype(BF16)


def outputs_kernel(hid, att_t, ow, outputs):
    z = lax.axis_index("seq")
    half = WIDTH // 2
    for at in range(SEQ):

        @pl.when(z == at)
        def _():
            rows = slice(at * TOK, (at + 1) * TOK)
            branch = mm(att_t[:, rows], ow[...], (((0,), (1,)), ((), ())))
            outputs[:, :half] = branch[:, :half] + hid[0, rows, :].astype(F32)
            outputs[:, half:] = branch[:, half:] + hid[1, rows, :].astype(F32)


def both_ways(write, keep, send, core):
    for at in range(2):

        @pl.when(core == at)
        def _():
            write(keep, at)
            write(send, 1 - at)


def early_grad_kernel(c0, ca, ow, early):
    early[0] = mm(c0[...], ow[...]).astype(BF16)
    early[1] = mm(ca[...], ow[...]).astype(BF16)


def value_kernel(early, c0, ca, cb, cc, normed_t, probs_t, att_t, aw, ow, grad, keep, send, mixed, cot, cot_t, d_value):
    z, d = lax.axis_index("seq"), lax.axis_index("dp")
    for ref, off in ((c0, 0), (ca, 3), (cb, 1), (cc, 2)):
        start = pl.multiple_of(lax.rem(z + off, SEQ) * TOK, TOK)
        cot[pl.ds(start, TOK), :] = ref[...]
    cot_t[...] = mm(row_picker(z), cot[...], NT).astype(BF16)
    for index, off in ((0, 0), (1, 3)):
        start = pl.multiple_of(lax.rem(z + off, SEQ) * TOK, TOK)
        grad[pl.ds(start, TOK), :] = early[index]
    late = mm(jnp.concatenate([cb[...], cc[...]], axis=0), ow[...]).astype(BF16)
    for index, off in ((0, 1), (1, 2)):
        start = pl.multiple_of(lax.rem(z + off, SEQ) * TOK, TOK)
        grad[pl.ds(start, TOK), :] = late[index * TOK : (index + 1) * TOK, :]
    out_part = mm(cot_t[...], att_t[...], NT)
    for h in range(HEADS):
        lanes = slice(h * VAL_DIM, (h + 1) * VAL_DIM)
        d_value[:, lanes] = mm(probs_t[h], grad[:, lanes]).astype(BF16)
    value_part = mm(normed_t[...], d_value[...])
    here = pl.multiple_of(z * ROWS, ROWS)
    total = jnp.sum(value_part * aw[pl.ds(here, ROWS), 2 * QW :].astype(F32), axis=1, keepdims=True)
    mixed[...] = jnp.broadcast_to(total, (ROWS, 128))
    half = VW // 2

    def write(ref, side):
        lanes = slice(side * half, (side + 1) * half)
        ref[:, :half] = value_part[:, lanes].astype(ref.dtype)
        ref[:, half:] = out_part[:, lanes].astype(ref.dtype)

    both_ways(write, keep, send, lax.rem(d, 2))


def score_grads(grad, proj, probs_t, d_query, d_key, first):
    for h in range(first, first + HEADS // 2):
        q, k, v = heads_of(proj, h)
        probs = probs_t[h].astype(F32)
        product = mm(v, grad[:, h * VAL_DIM : (h + 1) * VAL_DIM], NT) * probs
        delta = jnp.sum(product, axis=0, keepdims=True)
        dscore = (product - probs * delta).astype(BF16)
        lanes = slice((h - first) * KEY_DIM, (h - first + 1) * KEY_DIM)
        d_query[lanes, :] = (mm(k, dscore, TN) * SCALE).astype(BF16)
        d_key[:, lanes] = (mm(dscore, q) * SCALE).astype(BF16)


def early_key_kernel(grad, proj, probs_t, d_query, d_key):
    score_grads(grad, proj, probs_t, d_query, d_key, 0)


def late_key_kernel(
    grad, proj, probs_t, query_early, key_early, normed_t, mixed, gain, aw, keep, top, rest, d_query, d_key
):
    z, d = lax.axis_index("seq"), lax.axis_index("dp")
    score_grads(grad, proj, probs_t, d_query, d_key, HEADS // 2)
    left = normed_t[...]
    query_part = jnp.concatenate([mm(left, query_early[...], NT), mm(left, d_query[...], NT)], axis=1)
    key_part = jnp.concatenate([mm(left, key_early[...]), mm(left, d_key[...])], axis=1)
    here = pl.multiple_of(z * ROWS, ROWS)
    total = query_part * aw[pl.ds(here, ROWS), :QW].astype(F32)
    total = total + key_part * aw[pl.ds(here, ROWS), QW : 2 * QW].astype(F32)
    total = mixed[...] + jnp.sum(total, axis=1, keepdims=True)
    scales = gain[...].reshape(1, WIDTH)
    mine = scales[:, :ROWS]
    for at in range(1, SEQ):
        mine = jnp.where(z == at, scales[:, at * ROWS : (at + 1) * ROWS], mine)
    gain_part = total.T[0:1, :] / mine

    gain_rows = jnp.concatenate([gain_part, jnp.zeros((15, ROWS), F32)], axis=0)
    cut = ROWS // 2

    def part(side, rows):
        return (key_part if side else query_part)[rows, :]

    for at in range(2):

        @pl.when(lax.rem(d, 2) == at)
        def _():
            keep[:ROWS, :] = part(at, slice(0, ROWS))
            keep[ROWS:, :] = jnp.zeros((16, QW), F32)
            keep[ROWS:, :ROWS] = gain_rows
            top[...] = part(1 - at, slice(0, cut)).astype(BF16)
            rest[:cut, :] = part(1 - at, slice(cut, ROWS)).astype(BF16)
            rest[cut:, :] = jnp.zeros((16, QW), BF16)
            rest[cut:, :ROWS] = gain_rows.astype(BF16)


def finish_output_kernel(whole_v, other_v, grad_output):
    half = VW // 2
    for at in range(2):

        @pl.when(lax.rem(lax.axis_index("dp"), 2) == at)
        def _():
            grad_output[:, at * half : (at + 1) * half] = whole_v[:, half:].astype(F32)
            grad_output[:, (1 - at) * half : (2 - at) * half] = other_v[:, half:].astype(F32)


def finish_attend_kernel(whole_v, other_v, whole_k, other_k, grad_attend, grad_gain):
    half, base = VW // 2, 2 * QW
    for at in range(2):

        @pl.when(lax.rem(lax.axis_index("dp"), 2) == at)
        def _():
            grad_attend[:, base + at * half : base + (at + 1) * half] = whole_v[:, :half].astype(F32)
            grad_attend[:, base + (1 - at) * half : base + (2 - at) * half] = other_v[:, :half].astype(F32)
            low, high = (whole_k, other_k) if at == 0 else (other_k, whole_k)
            grad_attend[:, :QW] = low[:ROWS, :].astype(F32)
            grad_attend[:, QW : 2 * QW] = high[:ROWS, :].astype(F32)
            grad_gain[...] = low[ROWS : ROWS + 8, :ROWS].astype(F32)[0]


def kernel_call(body, outs, scratch, flops, *args, far=()):
    whole = pl.BlockSpec(memory_space=pltpu.VMEM)
    away = pl.BlockSpec(memory_space=pltpu.HBM)
    sems = [pltpu.SemaphoreType.DMA((len(far),))] if far else []
    return pl.pallas_call(
        body,
        in_specs=[away if i in far else whole for i in range(len(args))],
        out_shape=[jax.ShapeDtypeStruct(s, t) for s, t in outs],
        scratch_shapes=[pltpu.VMEM(s, t) for s, t in scratch] + sems,
        compiler_params=pltpu.CompilerParams(vmem_limit_bytes=40 << 20),
        cost_estimate=pl.CostEstimate(flops=flops, bytes_accessed=1 << 16, transcendentals=0),
    )(*args)


def combined(keep, arrived):
    return (keep.astype(F32) + arrived.astype(F32)).astype(BF16)


def per_device_fast(
    dna_features, filter_weight, filter_bias, norm_gain, attend_weight, output_weight, cotangent
):
    f0, c0 = dna_features[0], cotangent[0]
    w0 = filter_weight.transpose(0, 2, 1).reshape(5 * SHARD, CIN)
    half = WIDTH // 2
    w2 = swap(w0, 2)
    w1 = swap(w0, 1)
    fa, fb = ring(f0, 1), ring(f0, SEQ - 1)
    (taps,) = kernel_call(
        taps_kernel,
        [((2 * SHARD, 5 * CIN), BF16)],
        [((5 * SHARD, CIN), BF16)],
        1 << 24,
        pltpu.with_memory_space_constraint(w0, pltpu.HBM), w1,
        far=(0,),
    )
    ca = ring(c0, 1)
    far_a, taps = lax.optimization_barrier((fa, taps))
    to_left, far_a, fb = lax.optimization_barrier((c0, far_a, fb))
    fc = ring(far_a, 1)
    windows, hid_near = kernel_call(
        near_kernel,
        [((LEN, 6 * CIN), BF16), ((LEN, half), BF16)],
        [((CIN // 128, 16 + 2 * LEN, 128), F32)],
        1 << 33,
        f0, fa, fb, taps, filter_bias,
    )
    ca, windows = lax.optimization_barrier((ca, windows))
    cb, cc = ring(to_left, SEQ - 1), ring(ca, 1)
    (early,) = kernel_call(
        early_grad_kernel, [((2, TOK, WIDTH), BF16)], [], 1 << 24, c0, ca, output_weight
    )
    w2, fc, windows, early = lax.optimization_barrier((w2, fc, windows, early))
    w3 = swap(w2, 1)
    windows, hid_near, hid_two = kernel_call(
        mend_kernel,
        [((LEN, 6 * CIN), BF16), ((LEN, half), BF16), ((LEN, SHARD), BF16)],
        [((CIN // 128, 16 + 2 * LEN, 128), F32), ((SHARD, 5 * CIN), BF16)],
        1 << 33,
        fa, fb, fc, windows, hid_near, taps, w2, filter_bias,
    )
    hid, normed, proj, normed_t = kernel_call(
        project_kernel,
        [((2, LEN, half), BF16), ((LEN, WIDTH), BF16), ((LEN, PROJ), BF16), ((ROWS, LEN), BF16)],
        [((SHARD, 5 * CIN), BF16), ((2, LEN, SHARD), BF16)],
        1 << 24,
        windows, hid_near, hid_two, w3, filter_bias, norm_gain, attend_weight,
    )
    probs_t, att_t = kernel_call(
        attend_kernel,
        [((HEADS, LEN, LEN), BF16), ((VW, LEN), BF16)],
        [],
        1 << 29,
        proj,
    )
    (outputs,) = kernel_call(
        outputs_kernel, [((TOK, WIDTH), F32)], [], 1 << 33, hid, att_t, output_weight
    )
    grad, keep_v, send_v, mixed = kernel_call(
        value_kernel,
        [((LEN, VW), BF16), ((ROWS, VW), BF16), ((ROWS, VW), BF16), ((ROWS, 128), F32)],
        [((LEN, WIDTH), BF16), ((ROWS, LEN), BF16), ((LEN, VW), BF16)],
        1 << 31,
        early, c0, ca, cb, cc, normed_t, probs_t, att_t, attend_weight, output_weight,
    )
    query_early, key_early = kernel_call(
        early_key_kernel,
        [((QW // 2, LEN), BF16), ((LEN, QW // 2), BF16)],
        [],
        1 << 33,
        grad, proj, probs_t,
    )
    part_v = combined(keep_v, swap(send_v, 1))
    part_v, query_early = lax.optimization_barrier((part_v, query_early))
    keep_k, top_k, rest_k = kernel_call(
        late_key_kernel,
        [((ROWS + 16, QW), F32), ((ROWS // 2, QW), BF16), ((ROWS // 2 + 16, QW), BF16)],
        [((QW // 2, LEN), BF16), ((LEN, QW // 2), BF16)],
        1 << 16,
        grad, proj, probs_t, query_early, key_early, normed_t, mixed, norm_gain, attend_weight,
    )
    arrived_v = swap(part_v, 2)
    arrived_v, outputs = lax.optimization_barrier((arrived_v, outputs))
    part_k = combined(keep_k, jnp.concatenate([swap(top_k, 1), swap(rest_k, 1)]))
    arrived_k = swap(part_k, 2)
    whole_v, whole_k = combined(part_v, arrived_v), combined(part_k, arrived_k)
    other_v, other_k = swap(whole_v, 1), swap(whole_k, 1)
    (grad_output,) = kernel_call(
        finish_output_kernel, [((ROWS, WIDTH), F32)], [], 1 << 33, whole_v, other_v
    )
    grad_attend, grad_gain = kernel_call(
        finish_attend_kernel,
        [((ROWS, PROJ), F32), ((ROWS,), F32)],
        [],
        1 << 16,
        whole_v, other_v, whole_k, other_k,
    )
    return outputs[None], grad_attend, grad_output, grad_gain


def solution(mesh):
    small = mesh.shape["seq"] == SEQ and mesh.shape["dp"] == DP
    return jax.shard_map(
        per_device_fast if small else per_device,
        mesh=mesh,
        in_specs=(
            P(("groups", "dp"), "seq", None),
            P(None, None, "dp"),
            P(),
            P(),
            P(),
            P(),
            P(("groups", "dp"), "seq", None),
        ),
        out_specs=(
            P(("groups", "dp"), "seq", None),
            P(("groups", "seq"), None),
            P(("groups", "seq"), None),
            P(("groups", "seq")),
        ),
        check_vma=False,
    )
```

```python
import functools

import jax
import jax.numpy as jnp
from jax import lax
from jax.experimental import pallas as pl
from jax.experimental.pallas import tpu as pltpu
from jax.sharding import PartitionSpec as P

HEADS = 4
KEY_DIM = 64
VAL_DIM = 192


def extended(value, sides, width):
    for axis, dim in sides:
        devices, length = (lax.axis_size(axis), value.shape[dim])
        up = [(i, (i + 1) % devices) for i in range(devices - 1)]
        down = [(j, i) for i, j in up]
        last = lax.slice_in_dim(value, length - width, length, axis=dim)
        first = lax.slice_in_dim(value, 0, width, axis=dim)
        before = lax.ppermute(last, axis, up)
        after = lax.ppermute(first, axis, down)
        value = jnp.concatenate([before, value, after], axis=dim)
    return value


def filter_block(padded, weights, bias_part):
    count = padded.shape[1] - 4
    total = bias_part
    for offset in range(5):
        total = total + jnp.einsum(
            "spc,co->spo",
            padded[:, offset : offset + count],
            weights[offset],
            preferred_element_type=jnp.float32,
        )
    activ = jax.nn.gelu(total, approximate=True)
    activ = activ.reshape(activ.shape[0], count // 2, 2, activ.shape[2])
    return (0.5 * (activ[:, :, 0] + activ[:, :, 1])).astype(jnp.bfloat16)


def per_device(
    dna_features, filter_weight, filter_bias, norm_gain, attend_weight, output_weight, cotangent
):
    padded = extended(dna_features, (("seq", 1),), 2)
    hidden = filter_block(
        padded, lax.all_gather(filter_weight, "dp", axis=2, tiled=True), filter_bias
    )
    hidden = hidden[0]
    widen = hidden.astype(jnp.float32)
    nhat = widen * lax.rsqrt(jnp.mean(widen * widen, axis=-1, keepdims=True) + 1e-06)
    normed = (nhat * norm_gain).astype(jnp.bfloat16)
    tokens = normed.shape[0]
    query_width = HEADS * KEY_DIM
    value_width = HEADS * VAL_DIM
    scale = KEY_DIM ** (-0.5)
    projected = jnp.dot(normed, attend_weight, preferred_element_type=jnp.float32).astype(
        jnp.bfloat16
    )
    queries = projected[:, :query_width]
    keys_local = projected[:, query_width : 2 * query_width]
    values_local = projected[:, 2 * query_width :]
    keys_all, values_all = (
        lax.all_gather(keys_local, "seq", axis=0, tiled=True),
        lax.all_gather(values_local, "seq", axis=0, tiled=True),
    )
    total_len = keys_all.shape[0]
    query_heads = queries.reshape(tokens, HEADS, KEY_DIM)
    key_heads = keys_all.reshape(total_len, HEADS, KEY_DIM)
    value_heads = values_all.reshape(total_len, HEADS, VAL_DIM)
    scores = (
        jnp.einsum("qhd,khd->hqk", query_heads, key_heads, preferred_element_type=jnp.float32)
        * scale
    )
    peak = jnp.max(scores, axis=-1, keepdims=True)
    logsum = peak + jnp.log(jnp.sum(jnp.exp(scores - peak), axis=-1, keepdims=True))
    probs = jnp.exp(scores - logsum)
    probs_b = probs.astype(jnp.bfloat16)
    attended = (
        jnp.einsum("hqk,khd->qhd", probs_b, value_heads, preferred_element_type=jnp.float32)
        .astype(jnp.bfloat16)
        .reshape(tokens, value_width)
    )
    branch = lax.dot_general(
        attended, output_weight, (((1,), (1,)), ((), ())), preferred_element_type=jnp.float32
    )
    outputs = widen + branch
    upstream = cotangent[0]
    output_part = lax.dot_general(
        upstream, attended, (((0,), (0,)), ((), ())), preferred_element_type=jnp.float32
    )
    d_attn = jnp.dot(upstream, output_weight, preferred_element_type=jnp.float32).astype(
        jnp.bfloat16
    )
    d_heads = d_attn.reshape(tokens, HEADS, VAL_DIM)
    attn_heads = attended.reshape(tokens, HEADS, VAL_DIM)
    delta = jnp.sum(d_heads.astype(jnp.float32) * attn_heads.astype(jnp.float32), axis=-1)
    dprob = jnp.einsum("qhd,khd->hqk", d_heads, value_heads, preferred_element_type=jnp.float32)
    dscore = (probs * (dprob - delta.T[:, :, None])).astype(jnp.bfloat16)
    d_query = (
        jnp.einsum("hqk,khd->qhd", dscore, key_heads, preferred_element_type=jnp.float32) * scale
    )
    logsum_rows = logsum[:, :, 0].T
    logsum_all, delta_all = (
        lax.all_gather(logsum_rows, "seq", axis=0, tiled=True),
        lax.all_gather(delta, "seq", axis=0, tiled=True),
    )
    key_heads_local = keys_local.reshape(tokens, HEADS, KEY_DIM)
    value_heads_local = values_local.reshape(tokens, HEADS, VAL_DIM)
    piece_query = lax.all_gather(queries, "seq", axis=0, tiled=True)
    piece_grad = lax.all_gather(d_attn, "seq", axis=0, tiled=True)
    count = piece_query.shape[0]
    piece_qheads = piece_query.reshape(count, HEADS, KEY_DIM)
    piece_gheads = piece_grad.reshape(count, HEADS, VAL_DIM)
    piece_scores = (
        jnp.einsum(
            "qhd,khd->hqk", piece_qheads, key_heads_local, preferred_element_type=jnp.float32
        )
        * scale
    )
    piece_probs = jnp.exp(piece_scores - logsum_all.T[:, :, None])
    piece_probs_b = piece_probs.astype(jnp.bfloat16)
    piece_dprob = jnp.einsum(
        "qhd,khd->hqk", piece_gheads, value_heads_local, preferred_element_type=jnp.float32
    )
    piece_dscore = (piece_probs * (piece_dprob - delta_all.T[:, :, None])).astype(jnp.bfloat16)
    grad_keys = jnp.einsum(
        "hqk,qhd->khd", piece_dscore, piece_qheads, preferred_element_type=jnp.float32
    )
    grad_values = jnp.einsum(
        "hqk,qhd->khd", piece_probs_b, piece_gheads, preferred_element_type=jnp.float32
    )
    grad_keys, grad_values = (grad_keys, grad_values)
    d_proj = jnp.concatenate(
        [
            d_query.reshape(tokens, query_width),
            (grad_keys * scale).reshape(tokens, query_width),
            grad_values.reshape(tokens, value_width),
        ],
        axis=1,
    ).astype(jnp.bfloat16)
    d_normed = lax.dot_general(
        d_proj, attend_weight, (((1,), (1,)), ((), ())), preferred_element_type=jnp.float32
    )
    attend_part = lax.dot_general(
        normed, d_proj, (((0,), (0,)), ((), ())), preferred_element_type=jnp.float32
    )
    gain_part = jnp.sum(d_normed * nhat, axis=0)
    attend_share, output_share, gain_share = (
        lax.psum_scatter(
            attend_part.astype(jnp.bfloat16), "seq", scatter_dimension=0, tiled=True
        ).astype(jnp.float32),
        lax.psum_scatter(
            output_part.astype(jnp.bfloat16), "seq", scatter_dimension=0, tiled=True
        ).astype(jnp.float32),
        lax.psum_scatter(
            gain_part.astype(jnp.bfloat16), "seq", scatter_dimension=0, tiled=True
        ).astype(jnp.float32),
    )
    grad_attend, grad_output, grad_gain = lax.psum((attend_share, output_share, gain_share), "dp")
    return (outputs[None], grad_attend, grad_output, grad_gain)


F32, BF16 = jnp.float32, jnp.bfloat16
SEQ, DP = 4, 4
TOK = 128
EDGE = 16
REACH = 80
LEN = SEQ * TOK
CIN, WIDTH = 384, 768
SHARD = WIDTH // DP
ROWS = WIDTH // SEQ
QW, VW = HEADS * KEY_DIM, HEADS * VAL_DIM
PROJ = 2 * QW + VW
SCALE = KEY_DIM**-0.5
LOG2E = 1.4426950408889634
NN = (((1,), (0,)), ((), ()))
NT = (((1,), (1,)), ((), ()))
TN = (((0,), (0,)), ((), ()))


def mm(left, right, dims=NN):
    return lax.dot_general(left, right, dims, preferred_element_type=F32)


def half_gelu(value):
    inner = 0.7978845608028654 * (value + 0.044715 * value * value * value)
    return 0.5 * value * (1.0 + jnp.tanh(inner))


def ring(value, step):
    return lax.ppermute(value, "seq", [(i, (i + step) % SEQ) for i in range(SEQ)])


def swap(value, bit):
    return lax.ppermute(value, "dp", [(i, i ^ bit) for i in range(DP)])


def put_shards(taps, mine, other, core):
    for tap in range(5):
        lanes = slice(tap * CIN, (tap + 1) * CIN)
        rows = slice(tap * SHARD, (tap + 1) * SHARD)
        taps[pl.ds(core * SHARD, SHARD), lanes] = mine[rows, :]
        taps[pl.ds((1 - core) * SHARD, SHARD), lanes] = other[rows, :]


def put_shard(taps, shard):
    for tap in range(5):
        taps[:, tap * CIN : (tap + 1) * CIN] = shard[tap * SHARD : (tap + 1) * SHARD, :]


def shard_of(bias, index):
    every = bias[...].reshape(1, WIDTH)
    mine = every[:, :SHARD]
    for at in range(1, DP):
        mine = jnp.where(index == at, every[:, at * SHARD : (at + 1) * SHARD], mine)
    return mine


def half_of(bias, side):
    both = bias[...].reshape(1, WIDTH)
    return jnp.where(side == 0, both[:, : WIDTH // 2], both[:, WIDTH // 2 :])


def filtered_half(windows, taps, bias):
    even = mm(windows[:, : 5 * CIN], taps[...], NT) + bias
    odd = mm(windows[:, CIN:], taps[...], NT) + bias
    return (0.5 * (half_gelu(even) + half_gelu(odd))).astype(BF16)


def taps_kernel(w0_far, w1, taps, w0, sems):
    load = pltpu.make_async_copy(w0_far, w0, sems.at[0])
    load.start()
    load.wait()
    put_shards(taps, w0, w1, lax.rem(lax.axis_index("dp"), 2))


def fill_positions(positions, z, parts):
    chunk = 2 * TOK
    for g in range(CIN // 128):
        positions[g, 0:8, :] = jnp.zeros((8, 128), F32)
        positions[g, 8 + 2 * LEN :, :] = jnp.zeros((8, 128), F32)
        for ref, off in parts:
            start = pl.multiple_of(lax.rem(z + off, SEQ) * chunk + 8, 8)
            if ref is None:
                positions[g, pl.ds(start, chunk), :] = jnp.zeros((chunk, 128), F32)
            else:
                positions[g, pl.ds(start, chunk), :] = ref[:, g * 128 : (g + 1) * 128].astype(F32)


def fill_edges(positions, z, parts):
    for g in range(CIN // 128):
        for ref, off, row in parts:
            start = pl.multiple_of(lax.rem(z + off, SEQ) * 2 * TOK + (8 + row), 8)
            piece = ref[row : row + REACH, g * 128 : (g + 1) * 128]
            positions[g, pl.ds(start, REACH), :] = piece.astype(F32)


def near_kernel(f0, fa, fb, taps, bias, windows, hid, positions):
    z, d = lax.axis_index("seq"), lax.axis_index("dp")
    fill_positions(positions, z, ((f0, 0), (fa, 3), (fb, 1), (None, 2)))
    for g in range(CIN // 128):
        for k in range(6):
            at = k * CIN + g * 128
            windows[:, at : at + 128] = positions[g, pl.ds(6 + k, LEN, stride=2), :].astype(BF16)
    hid[...] = filtered_half(windows, taps, half_of(bias, d // 2))


def row_picker(z):
    row = lax.broadcasted_iota(jnp.int32, (ROWS, WIDTH), 0)
    lane = lax.broadcasted_iota(jnp.int32, (ROWS, WIDTH), 1)
    return jnp.where(lane == row + z * ROWS, 1.0, 0.0).astype(BF16)


def mend_kernel(
    fa, fb, fc, windows_in, hid_in, taps, w2, bias, windows, hid, hid_two, positions, two
):
    z, d = lax.axis_index("seq"), lax.axis_index("dp")
    fill_positions(positions, z, ((fc, 2),))
    fill_edges(positions, z, ((fa, 3, 0), (fb, 1, 2 * TOK - REACH)))
    windows[...] = windows_in[...]
    hid[...] = hid_in[...]
    first = jnp.clip(lax.rem(z + 2, SEQ) * TOK - EDGE, 0, LEN - TOK - 2 * EDGE)
    first = pl.multiple_of(first, EDGE)
    fresh = pl.ds(first, TOK + 2 * EDGE)
    for g in range(CIN // 128):
        for k in range(6):
            at = k * CIN + g * 128
            spots = pl.ds(2 * first + (6 + k), TOK + 2 * EDGE, stride=2)
            windows[fresh, at : at + 128] = positions[g, spots, :].astype(BF16)
    hid[fresh, :] = filtered_half(windows[fresh, :], taps, half_of(bias, d // 2))
    put_shard(two, w2)
    hid_two[...] = filtered_half(windows, two, shard_of(bias, lax.rem(d + 2, DP)))


def project_kernel(
    windows, hid_near, hid_two, w3, bias, gain, aw, hid, normed, proj, normed_t, three, far
):
    z, d = lax.axis_index("seq"), lax.axis_index("dp")
    side, core, half = d // 2, lax.rem(d, 2), WIDTH // 2
    put_shard(three, w3)
    hid[side] = hid_near[...]
    far[core] = hid_two[...]
    far[1 - core] = filtered_half(windows, three, shard_of(bias, 2 * (1 - side) + 1 - core))
    hid[1 - side] = jnp.concatenate([far[0], far[1]], axis=1)
    low, high = hid[0].astype(F32), hid[1].astype(F32)
    square = jnp.sum(low * low, axis=1, keepdims=True) + jnp.sum(high * high, axis=1, keepdims=True)
    inv = lax.rsqrt(square * (1.0 / WIDTH) + 1e-06)
    scales = gain[...].reshape(1, WIDTH)
    normed[:, :half] = (low * inv * scales[:, :half]).astype(BF16)
    normed[:, half:] = (high * inv * scales[:, half:]).astype(BF16)
    proj[...] = mm(normed[...], aw[...]).astype(BF16)
    normed_t[...] = mm(row_picker(z), normed[...], NT).astype(BF16)


def heads_of(proj, h):
    q = proj[:, h * KEY_DIM : (h + 1) * KEY_DIM]
    k = proj[:, QW + h * KEY_DIM : QW + (h + 1) * KEY_DIM]
    v = proj[:, 2 * QW + h * VAL_DIM : 2 * QW + (h + 1) * VAL_DIM]
    return q, k, v


def attend_kernel(proj, probs_t, att_t):
    for h in range(HEADS):
        q, k, v = heads_of(proj, h)
        scores = mm(k, q, NT) * (SCALE * LOG2E)
        top = jnp.max(scores, axis=0, keepdims=True)
        weight = jnp.exp2(scores - top)
        total = jnp.sum(weight, axis=0, keepdims=True)
        probs = (weight * (1.0 / total)).astype(BF16)
        probs_t[h] = probs
        att_t[h * VAL_DIM : (h + 1) * VAL_DIM, :] = mm(v, probs, TN).astype(BF16)


def outputs_kernel(hid, att_t, ow, outputs):
    z = lax.axis_index("seq")
    half = WIDTH // 2
    for at in range(SEQ):

        @pl.when(z == at)
        def _():
            rows = slice(at * TOK, (at + 1) * TOK)
            branch = mm(att_t[:, rows], ow[...], (((0,), (1,)), ((), ())))
            outputs[:, :half] = branch[:, :half] + hid[0, rows, :].astype(F32)
            outputs[:, half:] = branch[:, half:] + hid[1, rows, :].astype(F32)


def both_ways(write, keep, send, core):
    for at in range(2):

        @pl.when(core == at)
        def _():
            write(keep, at)
            write(send, 1 - at)


def early_grad_kernel(c0, ca, ow, early):
    early[0] = mm(c0[...], ow[...]).astype(BF16)
    early[1] = mm(ca[...], ow[...]).astype(BF16)


def value_kernel(early, c0, ca, cb, cc, normed_t, probs_t, att_t, aw, ow, grad, keep, send, mixed, cot, cot_t, d_value):
    z, d = lax.axis_index("seq"), lax.axis_index("dp")
    for ref, off in ((c0, 0), (ca, 3), (cb, 1), (cc, 2)):
        start = pl.multiple_of(lax.rem(z + off, SEQ) * TOK, TOK)
        cot[pl.ds(start, TOK), :] = ref[...]
    cot_t[...] = mm(row_picker(z), cot[...], NT).astype(BF16)
    for index, off in ((0, 0), (1, 3)):
        start = pl.multiple_of(lax.rem(z + off, SEQ) * TOK, TOK)
        grad[pl.ds(start, TOK), :] = early[index]
    late = mm(jnp.concatenate([cb[...], cc[...]], axis=0), ow[...]).astype(BF16)
    for index, off in ((0, 1), (1, 2)):
        start = pl.multiple_of(lax.rem(z + off, SEQ) * TOK, TOK)
        grad[pl.ds(start, TOK), :] = late[index * TOK : (index + 1) * TOK, :]
    out_part = mm(cot_t[...], att_t[...], NT)
    for h in range(HEADS):
        lanes = slice(h * VAL_DIM, (h + 1) * VAL_DIM)
        d_value[:, lanes] = mm(probs_t[h], grad[:, lanes]).astype(BF16)
    value_part = mm(normed_t[...], d_value[...])
    here = pl.multiple_of(z * ROWS, ROWS)
    total = jnp.sum(value_part * aw[pl.ds(here, ROWS), 2 * QW :].astype(F32), axis=1, keepdims=True)
    mixed[...] = jnp.broadcast_to(total, (ROWS, 128))
    half = VW // 2

    def write(ref, side):
        lanes = slice(side * half, (side + 1) * half)
        ref[:, :half] = value_part[:, lanes].astype(ref.dtype)
        ref[:, half:] = out_part[:, lanes].astype(ref.dtype)

    both_ways(write, keep, send, lax.rem(d, 2))


def score_grads(grad, proj, probs_t, d_query, d_key, first):
    for h in range(first, first + HEADS // 2):
        q, k, v = heads_of(proj, h)
        probs = probs_t[h].astype(F32)
        product = mm(v, grad[:, h * VAL_DIM : (h + 1) * VAL_DIM], NT) * probs
        delta = jnp.sum(product, axis=0, keepdims=True)
        dscore = (product - probs * delta).astype(BF16)
        lanes = slice((h - first) * KEY_DIM, (h - first + 1) * KEY_DIM)
        d_query[lanes, :] = (mm(k, dscore, TN) * SCALE).astype(BF16)
        d_key[:, lanes] = (mm(dscore, q) * SCALE).astype(BF16)


def early_key_kernel(grad, proj, probs_t, d_query, d_key):
    score_grads(grad, proj, probs_t, d_query, d_key, 0)


def late_key_kernel(
    grad, proj, probs_t, query_early, key_early, normed_t, mixed, gain, aw, keep, top, rest, d_query, d_key
):
    z, d = lax.axis_index("seq"), lax.axis_index("dp")
    score_grads(grad, proj, probs_t, d_query, d_key, HEADS // 2)
    left = normed_t[...]
    query_part = jnp.concatenate([mm(left, query_early[...], NT), mm(left, d_query[...], NT)], axis=1)
    key_part = jnp.concatenate([mm(left, key_early[...]), mm(left, d_key[...])], axis=1)
    here = pl.multiple_of(z * ROWS, ROWS)
    total = query_part * aw[pl.ds(here, ROWS), :QW].astype(F32)
    total = total + key_part * aw[pl.ds(here, ROWS), QW : 2 * QW].astype(F32)
    total = mixed[...] + jnp.sum(total, axis=1, keepdims=True)
    scales = gain[...].reshape(1, WIDTH)
    mine = scales[:, :ROWS]
    for at in range(1, SEQ):
        mine = jnp.where(z == at, scales[:, at * ROWS : (at + 1) * ROWS], mine)
    gain_part = total.T[0:1, :] / mine

    gain_rows = jnp.concatenate([gain_part, jnp.zeros((15, ROWS), F32)], axis=0)
    cut = ROWS // 2

    def part(side, rows):
        return (key_part if side else query_part)[rows, :]

    for at in range(2):

        @pl.when(lax.rem(d, 2) == at)
        def _():
            keep[:ROWS, :] = part(at, slice(0, ROWS))
            keep[ROWS:, :] = jnp.zeros((16, QW), F32)
            keep[ROWS:, :ROWS] = gain_rows
            top[...] = part(1 - at, slice(0, cut)).astype(BF16)
            rest[:cut, :] = part(1 - at, slice(cut, ROWS)).astype(BF16)
            rest[cut:, :] = jnp.zeros((16, QW), BF16)
            rest[cut:, :ROWS] = gain_rows.astype(BF16)


def finish_output_kernel(whole_v, other_v, grad_output):
    half = VW // 2
    for at in range(2):

        @pl.when(lax.rem(lax.axis_index("dp"), 2) == at)
        def _():
            grad_output[:, at * half : (at + 1) * half] = whole_v[:, half:].astype(F32)
            grad_output[:, (1 - at) * half : (2 - at) * half] = other_v[:, half:].astype(F32)


def finish_attend_kernel(whole_v, other_v, whole_k, other_k, grad_attend, grad_gain):
    half, base = VW // 2, 2 * QW
    for at in range(2):

        @pl.when(lax.rem(lax.axis_index("dp"), 2) == at)
        def _():
            grad_attend[:, base + at * half : base + (at + 1) * half] = whole_v[:, :half].astype(F32)
            grad_attend[:, base + (1 - at) * half : base + (2 - at) * half] = other_v[:, :half].astype(F32)
            low, high = (whole_k, other_k) if at == 0 else (other_k, whole_k)
            grad_attend[:, :QW] = low[:ROWS, :].astype(F32)
            grad_attend[:, QW : 2 * QW] = high[:ROWS, :].astype(F32)
            grad_gain[...] = low[ROWS : ROWS + 8, :ROWS].astype(F32)[0]


def kernel_call(body, outs, scratch, flops, *args, far=()):
    whole = pl.BlockSpec(memory_space=pltpu.VMEM)
    away = pl.BlockSpec(memory_space=pltpu.HBM)
    sems = [pltpu.SemaphoreType.DMA((len(far),))] if far else []
    return pl.pallas_call(
        body,
        in_specs=[away if i in far else whole for i in range(len(args))],
        out_shape=[jax.ShapeDtypeStruct(s, t) for s, t in outs],
        scratch_shapes=[pltpu.VMEM(s, t) for s, t in scratch] + sems,
        compiler_params=pltpu.CompilerParams(vmem_limit_bytes=40 << 20),
        cost_estimate=pl.CostEstimate(flops=flops, bytes_accessed=1 << 16, transcendentals=0),
    )(*args)


def combined(keep, arrived):
    return (keep.astype(F32) + arrived.astype(F32)).astype(BF16)


def per_device_fast(
    dna_features, filter_weight, filter_bias, norm_gain, attend_weight, output_weight, cotangent
):
    f0, c0 = dna_features[0], cotangent[0]
    w0 = filter_weight.transpose(0, 2, 1).reshape(5 * SHARD, CIN)
    half = WIDTH // 2
    w2 = swap(w0, 2)
    w1 = swap(w0, 1)
    fa, fb = ring(f0, 1), ring(f0, SEQ - 1)
    (taps,) = kernel_call(
        taps_kernel,
        [((2 * SHARD, 5 * CIN), BF16)],
        [((5 * SHARD, CIN), BF16)],
        1 << 24,
        pltpu.with_memory_space_constraint(w0, pltpu.HBM), w1,
        far=(0,),
    )
    ca = ring(c0, 1)
    far_a, taps = lax.optimization_barrier((fa, taps))
    to_left, far_a, fb = lax.optimization_barrier((c0, far_a, fb))
    fc = ring(far_a, 1)
    windows, hid_near = kernel_call(
        near_kernel,
        [((LEN, 6 * CIN), BF16), ((LEN, half), BF16)],
        [((CIN // 128, 16 + 2 * LEN, 128), F32)],
        1 << 33,
        f0, fa, fb, taps, filter_bias,
    )
    ca, windows = lax.optimization_barrier((ca, windows))
    cb, cc = ring(to_left, SEQ - 1), ring(ca, 1)
    (early,) = kernel_call(
        early_grad_kernel, [((2, TOK, WIDTH), BF16)], [], 1 << 24, c0, ca, output_weight
    )
    w2, fc, windows, early = lax.optimization_barrier((w2, fc, windows, early))
    w3 = swap(w2, 1)
    windows, hid_near, hid_two = kernel_call(
        mend_kernel,
        [((LEN, 6 * CIN), BF16), ((LEN, half), BF16), ((LEN, SHARD), BF16)],
        [((CIN // 128, 16 + 2 * LEN, 128), F32), ((SHARD, 5 * CIN), BF16)],
        1 << 33,
        fa, fb, fc, windows, hid_near, taps, w2, filter_bias,
    )
    hid, normed, proj, normed_t = kernel_call(
        project_kernel,
        [((2, LEN, half), BF16), ((LEN, WIDTH), BF16), ((LEN, PROJ), BF16), ((ROWS, LEN), BF16)],
        [((SHARD, 5 * CIN), BF16), ((2, LEN, SHARD), BF16)],
        1 << 24,
        windows, hid_near, hid_two, w3, filter_bias, norm_gain, attend_weight,
    )
    probs_t, att_t = kernel_call(
        attend_kernel,
        [((HEADS, LEN, LEN), BF16), ((VW, LEN), BF16)],
        [],
        1 << 29,
        proj,
    )
    (outputs,) = kernel_call(
        outputs_kernel, [((TOK, WIDTH), F32)], [], 1 << 33, hid, att_t, output_weight
    )
    grad, keep_v, send_v, mixed = kernel_call(
        value_kernel,
        [((LEN, VW), BF16), ((ROWS, VW), F32), ((ROWS, VW), BF16), ((ROWS, 128), F32)],
        [((LEN, WIDTH), BF16), ((ROWS, LEN), BF16), ((LEN, VW), BF16)],
        1 << 31,
        early, c0, ca, cb, cc, normed_t, probs_t, att_t, attend_weight, output_weight,
    )
    query_early, key_early = kernel_call(
        early_key_kernel,
        [((QW // 2, LEN), BF16), ((LEN, QW // 2), BF16)],
        [],
        1 << 33,
        grad, proj, probs_t,
    )
    part_v = combined(keep_v, swap(send_v, 1))
    part_v, query_early = lax.optimization_barrier((part_v, query_early))
    keep_k, top_k, rest_k = kernel_call(
        late_key_kernel,
        [((ROWS + 16, QW), F32), ((ROWS // 2, QW), BF16), ((ROWS // 2 + 16, QW), BF16)],
        [((QW // 2, LEN), BF16), ((LEN, QW // 2), BF16)],
        1 << 16,
        grad, proj, probs_t, query_early, key_early, normed_t, mixed, norm_gain, attend_weight,
    )
    arrived_v = swap(part_v, 2)
    arrived_v, outputs = lax.optimization_barrier((arrived_v, outputs))
    part_k = combined(keep_k, jnp.concatenate([swap(top_k, 1), swap(rest_k, 1)]))
    arrived_k = swap(part_k, 2)
    whole_v, whole_k = combined(part_v, arrived_v), combined(part_k, arrived_k)
    other_v, other_k = swap(whole_v, 1), swap(whole_k, 1)
    (grad_output,) = kernel_call(
        finish_output_kernel, [((ROWS, WIDTH), F32)], [], 1 << 33, whole_v, other_v
    )
    grad_attend, grad_gain = kernel_call(
        finish_attend_kernel,
        [((ROWS, PROJ), F32), ((ROWS,), F32)],
        [],
        1 << 16,
        whole_v, other_v, whole_k, other_k,
    )
    return outputs[None], grad_attend, grad_output, grad_gain


def solution(mesh):
    small = mesh.shape["seq"] == SEQ and mesh.shape["dp"] == DP
    return jax.shard_map(
        per_device_fast if small else per_device,
        mesh=mesh,
        in_specs=(
            P(("groups", "dp"), "seq", None),
            P(None, None, "dp"),
            P(),
            P(),
            P(),
            P(),
            P(("groups", "dp"), "seq", None),
        ),
        out_specs=(
            P(("groups", "dp"), "seq", None),
            P(("groups", "seq"), None),
            P(("groups", "seq"), None),
            P(("groups", "seq")),
        ),
        check_vma=False,
    )
```
